32 devices in a mesh: seq: 16 (over z, y, core), batch: 2 (over x).
Axes of the slice: x: 2, y: 2, z: 4, core: 2. Of those that a mesh axis runs over, the one named last changes fastest.
Arguments:
- tokens: bfloat16 [2, 2, 4096, 1024], P(None, 'batch', 'seq'), may hold values from -6 to 6
- segments: int32 [2, 2, 4096], P(None, 'batch'), may hold values from 0 to 3, never falling along the last dimension, each value on 1 to 2048 neighbouring positions
- value_experts: int32 [2, 2, 4096, 4, 2], P(None, 'batch', 'seq'), may hold values from 0 to 4, all different within a row
- out_experts: int32 [2, 2, 4096, 4, 2], P(None, 'batch', 'seq'), may hold values from 0 to 4, all different within a row
- norm_gain: bfloat16 [1024], replicated, may hold values from 0.099609375 to 1.8984375
- w_query: bfloat16 [1024, 448], replicated, may hold values from -0.375 to 0.375
- w_key: bfloat16 [1024, 448], replicated, may hold values from -0.1875 to 0.1875
- w_value: bfloat16 [1024, 2240], replicated, may hold values from -0.1875 to 0.1875
- w_vgate: bfloat16 [1024, 20], replicated, may hold values from -0.125 to 0.125
- w_ogate: bfloat16 [1024, 20], replicated, may hold values from -0.125 to 0.125
- w_out: bfloat16 [2240, 1024], replicated, may hold values from -1.5 to 1.5
- ffn_gain: bfloat16 [1024], replicated, may hold values from 0.099609375 to 1.8984375
- w_up: bfloat16 [1024, 4096], replicated, may hold values from -0.1875 to 0.1875
- w_down: bfloat16 [4096, 1024], replicated, may hold values from -0.125 to 0.125
- cotangent: bfloat16 [2, 2, 4096, 1024], P(None, 'batch', 'seq'), may hold values from -6 to 6
Outputs:
- output: bfloat16 [2, 2, 4096, 1024], P(None, 'batch', 'seq')
- input_grad: bfloat16 [2, 2, 4096, 1024], P(None, 'batch', 'seq')
- norm_gain_grad: float32 [1024], P(('seq', 'batch'))
- w_query_grad: float32 [1024, 448], P(('seq', 'batch'))
- w_key_grad: float32 [1024, 448], P(('seq', 'batch'))
- w_value_grad: float32 [1024, 2240], P(('seq', 'batch'))
- w_vgate_grad: float32 [1024, 20], P(('seq', 'batch'))
- w_ogate_grad: float32 [1024, 20], P(('seq', 'batch'))
- w_out_grad: float32 [2240, 1024], P(None, ('seq', 'batch'))
- ffn_gain_grad: float32 [1024], P(('seq', 'batch'))
- w_up_grad: float32 [1024, 4096], P(('seq', 'batch'))
- w_down_grad: float32 [4096, 1024], P(('seq', 'batch'))
The draws below stay inside these ranges and needn't reach their ends.
Inputs may be any that keep to these rules, and one draw needn't show every extreme that they name: `segments`: in each stream the document numbers never fall; a document has 1 to 2048 positions and some document exactly 2048. `value_experts`: two different experts for each token and head; every expert is chosen somewhere. `out_experts`: two different experts for each token and head; every expert is chosen somewhere.
All inputs are finite; a program needn't handle non-finite values.
Results may differ from the reference program's by a relative error of at most 0.017.
Values may be sent and summed in bfloat16 or wider, within the bound.
No kernel may reach another device: no remote copies, remote signals or barrier semaphores. Data moves between devices by JAX's collectives and lax.ppermute only.
A program may use at most 192 MiB of HBM per device.

```python
import math
import jax
import jax.numpy as jnp
import numpy as np
from jax import lax

D = 1024
HEADS = 4
HEAD = 112
EXPERTS = 5
FF = 4096
BLK = 256
MICRO = 2
DOC_MAX = 2048
STREAM = 4096
ROWS = 2
DOC_COUNT = 4


def levels(own_key, extent, cuts, least, largest):
    factor_of = 1.0
    for axis_at, parts in cuts:
        steps = jax.random.uniform(jax.random.fold_in(jax.random.fold_in(own_key, 6), axis_at), (parts,), jnp.float32, least / len(cuts), largest / len(cuts))
        factor_of = factor_of * jnp.repeat(jnp.exp(steps), extent[axis_at] // parts).reshape((-1,) + (1,) * (len(extent) - 1 - axis_at))
    return factor_of


def choose_distinct(stream_key, rows, amount, top, lift):
    sequence = jax.random.permutation(jax.random.fold_in(stream_key, 1), amount)
    favour = sequence
    for power in range(3):
        favour = favour * favour // amount
    favour = favour * lift // amount
    tickets = jax.random.randint(jax.random.fold_in(stream_key, 2), (rows, amount), 0, 4096) + favour
    sure = jax.random.permutation(jax.random.fold_in(stream_key, 3), rows)[jnp.arange(amount) % rows]
    tickets = jnp.where(jnp.arange(rows)[:, None] == sure[None, :], 1 << 14, tickets)
    merit = tickets * amount + jnp.arange(amount)
    return lax.top_k(merit.astype(jnp.int32), top)[1].astype(jnp.int32)


def profile(amount, total, limit, skew):
    portions = [(1 << 20) // math.isqrt(standing ** skew) + 1 for standing in range(2, amount + 1)]
    spare, given = total - limit - (amount - 1), [1] * (amount - 1)
    while spare > 0:
        free = [i for i in range(amount - 1) if given[i] < limit]
        mass, budget = sum([portions[i] for i in free]), spare
        for i in free:
            addition = min(limit - given[i], max(1, budget * portions[i] // mass), spare)
            given[i] = given[i] + addition
            spare = spare - addition
    return np.array([limit] + given)


def ragged_sizes(stream_key, number_of, total, most, lean):
    if number_of == 2:
        one = jax.random.randint(stream_key, (), max(1, total - most), min(most, total - 1) + 1)
        return jnp.stack([one, total - one])
    tallies = jnp.asarray(profile(number_of, total, most, lean), jnp.int32)
    twos = (number_of - 1) // 2
    source_of, receiver = tallies[1:1 + 2 * twos:2], tallies[2:2 + 2 * twos:2]
    margin = jnp.minimum(source_of - 1, most - receiver)
    passed = jax.random.randint(jax.random.fold_in(stream_key, 1), (twos,), 0, 1 << 20) % (margin + 1)
    tallies = tallies.at[1:1 + 2 * twos:2].set(source_of - passed).at[2:2 + 2 * twos:2].set(receiver + passed)
    return tallies[jax.random.permutation(jax.random.fold_in(stream_key, 2), number_of)]


def bell_draw(stream_key, dims, scale, bound, shards=(), kind=jnp.bfloat16):
    array = scale * jax.random.normal(stream_key, dims, jnp.float32)
    if shards:
        array = array * levels(stream_key, dims, shards, -0.22, 0.18)
    return jnp.clip(array, -bound, bound).astype(kind)


def setup_inputs(seed: int = 0) -> dict:
    streams_of = jax.random.split(jax.random.key(seed), 16)
    return {
        "tokens": bell_draw(streams_of[0], (MICRO, ROWS, STREAM, D), 1.0, 6.0, ((1, 2), (2, 16))),
        "segments": jax.vmap(lambda own: jnp.searchsorted(jnp.cumsum(ragged_sizes(own, DOC_COUNT, STREAM, DOC_MAX, 2)), jnp.arange(STREAM), side="right"))(jax.random.split(streams_of[1], MICRO * ROWS)).reshape((MICRO, ROWS, STREAM)).astype(jnp.int32),
        "value_experts": choose_distinct(streams_of[2], MICRO * ROWS * STREAM * HEADS, EXPERTS, 2, 3276).reshape((MICRO, ROWS, STREAM, HEADS, 2)),
        "out_experts": choose_distinct(streams_of[3], MICRO * ROWS * STREAM * HEADS, EXPERTS, 2, 3276).reshape((MICRO, ROWS, STREAM, HEADS, 2)),
        "norm_gain": jnp.clip(1.0 + 0.18 * jax.random.normal(streams_of[4], (D,), jnp.float32), 0.099609375, 1.8984375).astype(jnp.bfloat16),
        "w_query": bell_draw(streams_of[5], (D, HEADS * HEAD), (D // 4) ** -0.5, 0.375),
        "w_key": bell_draw(streams_of[6], (D, HEADS * HEAD), D ** -0.5, 0.1875),
        "w_value": bell_draw(streams_of[7], (D, HEADS * EXPERTS * HEAD), D ** -0.5, 0.1875),
        "w_vgate": bell_draw(streams_of[8], (D, HEADS * EXPERTS), (2 * D) ** -0.5, 0.125),
        "w_ogate": bell_draw(streams_of[9], (D, HEADS * EXPERTS), (2 * D) ** -0.5, 0.125),
        "w_out": bell_draw(streams_of[10], (HEADS * EXPERTS * HEAD, D), 16 ** -0.5, 1.5),
        "ffn_gain": jnp.clip(1.0 + 0.18 * jax.random.normal(streams_of[11], (D,), jnp.float32), 0.099609375, 1.8984375).astype(jnp.bfloat16),
        "w_up": bell_draw(streams_of[12], (D, FF), D ** -0.5, 0.1875),
        "w_down": bell_draw(streams_of[13], (FF, D), (FF // 2) ** -0.5, 0.125),
        "cotangent": bell_draw(streams_of[14], (MICRO, ROWS, STREAM, D), 1.0, 6.0, ((1, 2), (2, 16))),
    }


@jax.custom_vjp
def low(v):
    return lax.optimization_barrier(v.astype(jnp.bfloat16)).astype(jnp.float32)

@jax.custom_vjp
def low_back(v):
    return v

def low_keep(v):
    return (low(v), None)

def low_pass(kept, grad):
    return (grad,)

def back_keep(v):
    return (v, None)

def back_low(kept, grad):
    return (low(grad),)
low.defvjp(low_keep, low_pass)
low_back.defvjp(back_keep, back_low)

def matmul(left, right):
    return jnp.dot(left, right, precision=lax.Precision.HIGHEST)

def rms_scale(field, gain):
    return field * lax.rsqrt(lax.optimization_barrier(jnp.mean(field * field, axis=-1, keepdims=True)) + 1e-06) * gain

def gates_of(logits, chosen):
    labels = jnp.arange(EXPERTS, dtype=jnp.int32)
    picks = lax.optimization_barrier(jnp.sum((chosen[:, :, :, None] == labels[None, None, None, :]).astype(jnp.float32), axis=2))
    return jax.nn.sigmoid(logits.reshape(-1, HEADS, EXPERTS)) * picks

def keys_values(field, weights, value_sel):
    gain_one, w_query, w_key, w_value, w_vgate, w_ogate, w_out, gain_two, w_up, w_down = weights
    length = field.shape[0]
    normed = low(rms_scale(field, gain_one))
    keys = low(low_back(matmul(normed, w_key))).reshape(length, HEADS, HEAD)
    value_gates = gates_of(low_back(matmul(normed, w_vgate)), value_sel)
    expert_values = low_back(matmul(normed, w_value)).reshape(length, HEADS, EXPERTS, HEAD)
    values = low(low_back(lax.optimization_barrier(jnp.sum(value_gates[..., None] * expert_values, axis=2))))
    return (normed, keys, values)

def block_attention(query_block, key_block, value_block, query_segs, key_segs):
    scores = low_back(jnp.einsum('qhd,khd->hqk', query_block, key_block, precision=lax.Precision.HIGHEST) * HEAD ** (-0.5))
    query_place = jnp.arange(BLK, dtype=jnp.int32) + BLK
    key_place = jnp.arange(2 * BLK, dtype=jnp.int32)
    allowed = ((query_segs[:, None] == key_segs[None, :]) & (key_place[None, :] <= query_place[:, None]))[None]
    safe = jnp.where(allowed, scores, jnp.zeros_like(scores))
    top = lax.optimization_barrier(jnp.max(jnp.where(allowed, safe, jnp.full_like(safe, -10000.0)), axis=-1, keepdims=True))
    expo = jnp.where(allowed, jnp.exp(safe - top), jnp.zeros_like(safe))
    probs = expo / lax.optimization_barrier(jnp.sum(expo, axis=-1, keepdims=True))
    return jnp.einsum('hqk,khd->qhd', low(probs), value_block, precision=lax.Precision.HIGHEST)

def block_forward(field, weights, seg, prior_seg, value_sel, out_sel, memory_keys, memory_values):
    gain_one, w_query, w_key, w_value, w_vgate, w_ogate, w_out, gain_two, w_up, w_down = weights
    length = field.shape[0]
    normed, keys, values = keys_values(field, weights, value_sel)
    query = low(low_back(matmul(normed, w_query))).reshape(length, HEADS, HEAD)
    key_block = jnp.concatenate([memory_keys, keys], 0)
    value_block = jnp.concatenate([memory_values, values], 0)
    key_segs = jnp.concatenate([prior_seg, seg], 0).astype(jnp.int32)
    attended = block_attention(query, key_block, value_block, seg, key_segs)
    attended = low(low_back(attended))
    out_gates = gates_of(low_back(matmul(normed, w_ogate)), out_sel)
    mixed = low(out_gates[..., None] * attended[:, :, None, :]).reshape(length, HEADS * EXPERTS * HEAD)
    hidden = field + low_back(matmul(mixed, w_out))
    normed_two = low(rms_scale(hidden, gain_two))
    upper = low(jax.nn.gelu(low_back(matmul(normed_two, w_up)), approximate=False))
    return hidden + low_back(matmul(upper, w_down))

def reference(tokens, segments, value_experts, out_experts, norm_gain, w_query, w_key, w_value, w_vgate, w_ogate, w_out, ffn_gain, w_up, w_down, cotangent):
    weights = tuple((w.astype(jnp.float32) for w in (norm_gain, w_query, w_key, w_value, w_vgate, w_ogate, w_out, ffn_gain, w_up, w_down)))
    streams = MICRO * ROWS
    count = STREAM // BLK
    fields = tokens.astype(jnp.float32).reshape(streams, count, BLK, D)
    cots = cotangent.astype(jnp.float32).reshape(streams, count, BLK, D)
    segs = segments.astype(jnp.int32).reshape(streams, count, BLK)
    value_sels = value_experts.astype(jnp.int32).reshape(streams, count, BLK, HEADS, 2)
    out_sels = out_experts.astype(jnp.int32).reshape(streams, count, BLK, HEADS, 2)

    def one(total, index):
        stream_at = (index // count).astype(jnp.int32)
        block_at = (index % count).astype(jnp.int32)
        prior_at = jnp.maximum(block_at - 1, 0).astype(jnp.int32)
        field = fields[stream_at, block_at]
        cot = cots[stream_at, block_at]
        seg = segs[stream_at, block_at]
        prior_seg = jnp.where(block_at > 0, segs[stream_at, prior_at], jnp.full((BLK,), -1, jnp.int32)).astype(jnp.int32)
        value_sel = value_sels[stream_at, block_at]
        out_sel = out_sels[stream_at, block_at]
        unused, memory_keys, memory_values = keys_values(fields[stream_at, prior_at], weights, value_sels[stream_at, prior_at])
        result, pull = jax.vjp(lambda inner, params: block_forward(inner, params, seg, prior_seg, value_sel, out_sel, memory_keys, memory_values), field, weights)
        field_grad, weight_grads = pull(cot)
        return (tuple((a + b for a, b in zip(total, weight_grads))), (result, field_grad))
    start = tuple((jnp.zeros(w.shape, jnp.float32) for w in weights))
    grads, (results, field_grads) = lax.scan(one, start, jnp.arange(streams * count, dtype=jnp.int32))
    output = results.reshape(MICRO, ROWS, STREAM, D).astype(jnp.bfloat16)
    input_grad = field_grads.reshape(MICRO, ROWS, STREAM, D).astype(jnp.bfloat16)
    return (output, input_grad, grads[0], grads[1], grads[2], grads[3], grads[4], grads[5], grads[6], grads[7], grads[8], grads[9])
```

```python
import math

import jax
import jax.numpy as jnp
from jax import lax
from jax.sharding import PartitionSpec as P

HEADS = 4
HEAD = 112
EXPERTS = 5

eps = 1e-06


def product(left, right):
    return jnp.dot(left, right, preferred_element_type=jnp.float32)


def product_tn(left, right):
    return lax.dot_general(
        left, right, (((0,), (0,)), ((), ())), preferred_element_type=jnp.float32
    )


def product_nt(left, right):
    return lax.dot_general(
        left, right, (((1,), (1,)), ((), ())), preferred_element_type=jnp.float32
    )


def passed_along(value, axis, steps):
    count = lax.axis_size(axis)
    initial, last = (max(0, -steps), min(count, count - steps))
    return lax.ppermute(value, axis, [(source, source + steps) for source in range(initial, last)])


class Grid:
    def __init__(self):
        self.sizes = {"seq": lax.axis_size("seq"), "batch": lax.axis_size("batch")}
        self.bits = []
        for axis in ("seq", "batch"):
            count = self.sizes[axis].bit_length() - 1
            self.bits += [(axis, at) for at in reversed(range(count))]
        self.index = {"seq": lax.axis_index("seq"), "batch": lax.axis_index("batch")}

    def mine(self, bit):
        axis, at = bit
        return (self.index[axis] >> at) & 1

    def swap(self, value, bit):
        axis, at = bit
        return lax.ppermute(
            value, axis, [(i, i ^ (1 << at)) for i in range(self.sizes[axis])]
        )


class Shards:
    def __init__(self, array, bits):
        self.array, self.bits = array, list(bits)

    def pick(self, bit, value):
        at = self.bits.index(bit)
        rest = self.bits[:at] + self.bits[at + 1 :]
        return Shards(lax.dynamic_index_in_dim(self.array, value, at, keepdims=False), rest)

    def map(self, f):
        return Shards(f(self.array), self.bits)


def flat_rows(array, tail):
    return array.reshape((-1,) + array.shape[array.ndim - tail :])


def reduce_pair(grid, parts, bit):
    mine = grid.mine(bit)
    sent = parts(1 - mine).map(lambda a: a.astype(jnp.bfloat16))
    came = Shards(grid.swap(sent.array, bit), sent.bits)
    return came, (lambda: parts(mine))


def norm_forward(field, gain):
    factor = lax.rsqrt(jnp.mean(field * field, axis=-1, keepdims=True) + eps)
    return ((field * factor * gain).astype(jnp.bfloat16), factor)


def norm_backward(field, factor, gain, grad):
    weighted = grad * gain
    gain_grad = jnp.sum(grad * field * factor, axis=0)
    field_grad = factor * weighted - field * factor**3 * jnp.mean(
        weighted * field, axis=-1, keepdims=True
    )
    return (field_grad, gain_grad)


def chosen_mask(picked):
    labels = jnp.arange(EXPERTS, dtype=jnp.int32)
    return jnp.sum(
        (picked[:, :, :, None] == labels[None, None, None, :]).astype(jnp.float32), axis=2
    )


def core_stage(grid, left, right, extra=None):
    bit = ("seq", 0)
    mine = grid.mine(bit)

    def partial(chosen, columns=None, extra_part=None):
        shape = chosen.array.shape
        out = product(chosen.array.reshape(-1, shape[-1]), right if columns is None else right[:, columns])
        out = out.reshape(shape[:-1] + (out.shape[-1],))
        if extra_part is not None:
            out = out + extra_part.array
        return out

    theirs = left.pick(bit, 1 - mine)
    extra_theirs = None if extra is None else extra.pick(bit, 1 - mine)
    sent = partial(theirs, None, extra_theirs).astype(jnp.bfloat16)
    came = Shards(grid.swap(sent, bit), theirs.bits)
    own = left.pick(bit, mine)
    extra_own = None if extra is None else extra.pick(bit, mine)
    return own, came, extra_own, partial


def plane_stage(grid, staged, first, second, columns):
    own, came, extra, partial = staged
    mine = grid.mine(first)

    def half(value):
        chosen, arrived = own.pick(first, value), came.pick(first, value)
        part = None if extra is None else extra.pick(first, value).map(lambda a: a[..., columns])
        total = partial(chosen, columns, part) + arrived.array[..., columns].astype(jnp.float32)
        return Shards(total.astype(jnp.bfloat16), chosen.bits)

    sent = half(1 - mine)
    arrived = Shards(grid.swap(sent.array, first), sent.bits)
    kept = half(mine)
    return halve(grid, kept, arrived, second)


def halve(grid, kept, arrived, bit):
    mine = grid.mine(bit)

    def half(value):
        a, b = kept.pick(bit, value), arrived.pick(bit, value)
        return Shards(
            (a.array.astype(jnp.float32) + b.array.astype(jnp.float32)).astype(jnp.bfloat16), a.bits
        )

    sent = half(1 - mine)
    return half(mine), Shards(grid.swap(sent.array, bit), sent.bits)


def rest_stages(grid, pair, bits):
    kept, arrived = pair
    for bit in bits:
        kept, arrived = halve(grid, kept, arrived, bit)
    return kept.array.astype(jnp.float32) + arrived.array.astype(jnp.float32)


def joined(pairs):
    kept = Shards(jnp.stack([p[0].array for p in pairs], len(pairs[0][0].bits)), pairs[0][0].bits)
    came = Shards(jnp.stack([p[1].array for p in pairs], len(pairs[0][1].bits)), pairs[0][1].bits)
    return kept, came


def body(
    tokens,
    segments,
    value_experts,
    out_experts,
    norm_gain,
    w_query,
    w_key,
    w_value,
    w_vgate,
    w_ogate,
    w_out,
    ffn_gain,
    w_up,
    w_down,
    cotangent,
):
    grid = Grid()
    bits = grid.bits
    cube = (2,) * len(bits)
    core, plane_a, plane_b = ("seq", 0), ("batch", 0), ("seq", 1)
    rest = [b for b in reversed(bits) if b not in (core, plane_a, plane_b)]
    micro, _, block, width = tokens.shape
    rows = micro * block
    hidden_units = w_up.shape[1]
    place = lax.axis_index("seq")
    own_segs = lax.dynamic_slice_in_dim(segments, place * block, block, 2)[:, 0]
    prior_start = jnp.maximum(place - 1, 0) * block
    prior_segs = jnp.where(
        place > 0, lax.dynamic_slice_in_dim(segments, prior_start, block, 2)[:, 0], -1
    )
    gain_one, gain_two = norm_gain.astype(jnp.float32), ffn_gain.astype(jnp.float32)
    att_scale = HEAD ** (-0.5)

    field = tokens.reshape(rows, width).astype(jnp.float32)
    normed, factor_one = norm_forward(field, gain_one)
    keys = product(normed, w_key).astype(jnp.bfloat16)
    value_sig = jax.nn.sigmoid(product(normed, w_vgate)).reshape(rows, HEADS, EXPERTS)
    value_pick = chosen_mask(value_experts.reshape(rows, HEADS, 2))
    value_gates = value_sig * value_pick
    expert_values = product(normed, w_value).reshape(rows, HEADS, EXPERTS, HEAD)
    values = (
        jnp.sum(value_gates[..., None] * expert_values, axis=2)
        .reshape(rows, HEADS * HEAD)
        .astype(jnp.bfloat16)
    )
    mem_keys, mem_values = passed_along((keys, values), "seq", 1)
    query = product(normed, w_query).astype(jnp.bfloat16)
    split = (micro, block, HEADS, HEAD)
    key_all = jnp.concatenate([mem_keys.reshape(split), keys.reshape(split)], 1)
    value_all = jnp.concatenate([mem_values.reshape(split), values.reshape(split)], 1)
    query_heads = query.reshape(split)
    key_segs = jnp.concatenate([prior_segs, own_segs], 1)
    query_place = jnp.arange(block, dtype=jnp.int32) + block
    key_place = jnp.arange(2 * block, dtype=jnp.int32)
    allowed = (own_segs[:, :, None] == key_segs[:, None, :]) & (
        key_place[None, None, :] <= query_place[None, :, None]
    )
    scores = (
        jnp.einsum("mqhd,mkhd->mhqk", query_heads, key_all, preferred_element_type=jnp.float32)
        * att_scale
    )
    scores = jnp.where(allowed[:, None], scores, -1e30)
    top = jnp.max(scores, axis=-1, keepdims=True)
    expo = jnp.exp(scores - top)
    probs = expo / jnp.sum(expo, axis=-1, keepdims=True)
    probs_low = probs.astype(jnp.bfloat16)
    attended = (
        jnp.einsum("mhqk,mkhd->mqhd", probs_low, value_all, preferred_element_type=jnp.float32)
        .astype(jnp.bfloat16)
        .reshape(rows, HEADS, HEAD)
    )
    out_sig = jax.nn.sigmoid(product(normed, w_ogate)).reshape(rows, HEADS, EXPERTS)
    out_pick = chosen_mask(out_experts.reshape(rows, HEADS, 2))
    out_gates = out_sig * out_pick
    attended_f = attended.astype(jnp.float32)
    mixed = (
        (out_gates[..., None] * attended_f[:, :, None, :])
        .reshape(rows, HEADS * EXPERTS * HEAD)
        .astype(jnp.bfloat16)
    )
    hidden = field + product(mixed, w_out)
    normed_two, factor_two = norm_forward(hidden, gain_two)
    pre = product(normed_two, w_up)
    cdf = 0.5 * (1.0 + lax.erf(pre * (1.0 / math.sqrt(2.0))))
    upper = (pre * cdf).astype(jnp.bfloat16)
    slope = cdf + pre * (jnp.exp(-0.5 * pre * pre) * (1.0 / math.sqrt(2.0 * math.pi)))
    d_down = cotangent.reshape(rows, width)
    grad_out = d_down.astype(jnp.float32)

    upper_t = Shards(upper.T.reshape(cube + (-1, rows)), bits)
    staged_down = core_stage(grid, upper_t, d_down)
    d_pre = (product_nt(d_down, w_down) * slope).astype(jnp.bfloat16)
    normed_two_t = Shards(normed_two.T.reshape(cube + (-1, rows)), bits)
    staged_up = core_stage(grid, normed_two_t, d_pre)
    half = width // 2
    down_a = plane_stage(grid, staged_down, plane_a, plane_b, slice(0, half))
    down_b = plane_stage(grid, staged_down, plane_b, plane_a, slice(half, width))
    half = hidden_units // 2
    up_a = plane_stage(grid, staged_up, plane_a, plane_b, slice(0, half))
    up_b = plane_stage(grid, staged_up, plane_b, plane_a, slice(half, hidden_units))
    d_normed_two = product_nt(d_pre, w_up)
    d_hidden_norm, grad_gain_two = norm_backward(hidden, factor_two, gain_two, d_normed_two)
    d_hidden = grad_out + d_hidden_norm
    d_branch = d_hidden.astype(jnp.bfloat16)
    branch_t = Shards(d_branch.T.reshape(cube + (-1, rows)), bits)
    staged_out = core_stage(grid, branch_t, mixed)
    d_mixed = product_nt(d_branch, w_out).reshape(rows, HEADS, EXPERTS, HEAD)
    out_pair = plane_stage(grid, staged_out, plane_a, plane_b, slice(0, mixed.shape[1]))
    result = (hidden + product(upper, w_down)).astype(jnp.bfloat16)
    d_attended = jnp.sum(out_gates[..., None] * d_mixed, axis=2).astype(jnp.bfloat16)
    d_ogate = jnp.sum(attended_f[:, :, None, :] * d_mixed, axis=3)
    d_ologit = (
        (d_ogate * out_pick * out_sig * (1.0 - out_sig))
        .reshape(rows, HEADS * EXPERTS)
        .astype(jnp.bfloat16)
    )
    d_attended = d_attended.reshape(split)
    d_probs = jnp.einsum(
        "mqhd,mkhd->mhqk", d_attended, value_all, preferred_element_type=jnp.float32
    )
    delta = jnp.sum(probs * d_probs, axis=-1, keepdims=True)
    d_scores = (probs * (d_probs - delta)).astype(jnp.bfloat16)
    d_query = (
        (
            jnp.einsum("mhqk,mkhd->mqhd", d_scores, key_all, preferred_element_type=jnp.float32)
            * att_scale
        )
        .reshape(rows, HEADS * HEAD)
        .astype(jnp.bfloat16)
    )
    d_keys = (
        (
            jnp.einsum(
                "mhqk,mqhd->mkhd",
                d_scores[..., block:],
                query_heads,
                preferred_element_type=jnp.float32,
            )
            * att_scale
        )
        .reshape(rows, HEADS * HEAD)
        .astype(jnp.bfloat16)
    )
    d_values = (
        jnp.einsum(
            "mhqk,mqhd->mkhd",
            probs_low[..., block:],
            d_attended,
            preferred_element_type=jnp.float32,
        )
        .astype(jnp.bfloat16)
        .reshape(rows, HEADS, HEAD)
    )
    d_values_f = d_values.astype(jnp.float32)
    d_expert = (
        (value_gates[..., None] * d_values_f[:, :, None, :])
        .reshape(rows, HEADS * EXPERTS * HEAD)
        .astype(jnp.bfloat16)
    )
    d_vgate = jnp.sum(expert_values * d_values_f[:, :, None, :], axis=3)
    d_vlogit = (
        (d_vgate * value_pick * value_sig * (1.0 - value_sig))
        .reshape(rows, HEADS * EXPERTS)
        .astype(jnp.bfloat16)
    )
    d_normed = (
        product_nt(d_ologit, w_ogate)
        + product_nt(d_query, w_query)
        + product_nt(d_keys, w_key)
        + product_nt(d_expert, w_value)
        + product_nt(d_vlogit, w_vgate)
    )
    d_field_norm, grad_gain_one = norm_backward(field, factor_one, gain_one, d_normed)
    field_grad = (d_hidden + d_field_norm).astype(jnp.bfloat16)

    wide = jnp.concatenate([d_query, d_keys, d_expert, d_vlogit, d_ologit], 1)
    used = wide.shape[1]
    full = -(-(used + 2) // 128) * 128
    wide = jnp.pad(wide, ((0, 0), (0, full - used)))
    gains = jnp.stack([grad_gain_one, grad_gain_two], 1)
    gains = jnp.pad(gains, ((0, 0), (used, full - used - 2)))
    gains = Shards(gains.reshape(cube + (-1, full)), bits)
    normed_t = Shards(normed.T.reshape(cube + (-1, rows)), bits)
    staged_in = core_stage(grid, normed_t, wide, gains)
    in_pair = plane_stage(grid, staged_in, plane_b, plane_a, slice(0, full))

    down = rest_stages(grid, joined([down_a, down_b]), rest)
    grad_down = jnp.concatenate([down[0], down[1]], -1)
    up = rest_stages(grid, joined([up_a, up_b]), rest)
    grad_up = jnp.concatenate([up[0], up[1]], -1)
    grad_out_w = rest_stages(grid, out_pair, rest).T
    grad_in = rest_stages(grid, in_pair, rest)
    pieces = []
    start = 0
    for size in (w_query.shape[1], w_key.shape[1], w_value.shape[1], w_vgate.shape[1], w_ogate.shape[1]):
        pieces.append(grad_in[:, start : start + size])
        start += size
    return (
        result.reshape(tokens.shape),
        field_grad.reshape(tokens.shape),
        grad_in[:, start],
        pieces[0],
        pieces[1],
        pieces[2],
        pieces[3],
        pieces[4],
        grad_out_w,
        grad_in[:, start + 1],
        grad_up,
        grad_down,
    )


def solution(mesh):
    both = ("seq", "batch")
    stream = P(None, "batch", "seq", None)
    picks = P(None, "batch", "seq", None, None)
    return jax.shard_map(
        body,
        mesh=mesh,
        in_specs=(stream, P(None, "batch", None), picks, picks) + (P(),) * 10 + (stream,),
        out_specs=(
            stream,
            stream,
            P(both),
            P(both, None),
            P(both, None),
            P(both, None),
            P(both, None),
            P(both, None),
            P(None, both),
            P(both),
            P(both, None),
            P(both, None),
        ),
        check_vma=False,
    )
```

```python
import functools
import math

import jax
import jax.numpy as jnp
from jax import lax
from jax.experimental import pallas as pl
from jax.experimental.pallas import tpu as pltpu
from jax.sharding import PartitionSpec as P

HEADS = 4
HEAD = 112
EXPERTS = 5

eps = 1e-06
VMEM = 56 << 20


def product(left, right):
    return jnp.dot(left, right, preferred_element_type=jnp.float32)


def product_tn(left, right):
    return lax.dot_general(
        left, right, (((0,), (0,)), ((), ())), preferred_element_type=jnp.float32
    )


def product_nt(left, right):
    return lax.dot_general(
        left, right, (((1,), (1,)), ((), ())), preferred_element_type=jnp.float32
    )


def passed_along(value, axis, steps):
    count = lax.axis_size(axis)
    initial, last = (max(0, -steps), min(count, count - steps))
    return lax.ppermute(value, axis, [(source, source + steps) for source in range(initial, last)])


class Grid:
    def __init__(self):
        self.seq, self.batch = lax.axis_size("seq"), lax.axis_size("batch")
        self.count = self.seq * self.batch
        low = self.batch.bit_length() - 1
        self.core, self.plane_a, self.plane_b = 1 << low, 1, 2 << low
        taken = self.core | self.plane_a | self.plane_b
        masks = [m for m in range(self.count) if not m & taken]
        self.rest = masks
        self.me = lax.axis_index("seq") * self.batch + lax.axis_index("batch")

    def swap(self, value, mask):
        both = ("seq", "batch")
        return lax.ppermute(value, both, [(i, i ^ mask) for i in range(self.count)])

    def order(self, first, second, theirs):
        base = self.core if theirs else 0
        masks = [
            base | f | s | m for f in (first, 0) for s in (second, 0) for m in self.rest
        ]
        return self.me ^ jnp.array(masks, jnp.int32)


def after(value, *others):
    return lax.optimization_barrier((value,) + others)[0]


def rows_kernel(adding, src_ref, left_ref, right_ref, *refs):
    turned = refs[-1]
    order, at = pl.program_id(0), pl.program_id(1)

    @pl.when(at == 0)
    def _():
        places = lax.broadcasted_iota(jnp.int32, (turned.shape[0], left_ref.shape[1]), 1)
        picks = (src_ref[0] == places).astype(jnp.float32).astype(jnp.bfloat16)
        turned[...] = product_nt(picks, left_ref[...]).astype(jnp.bfloat16)

    total = product(turned[...], right_ref[...])
    if not adding:
        refs[0][0] = total.astype(jnp.bfloat16)
        return
    total = (total + refs[0][0].astype(jnp.float32)).astype(jnp.bfloat16)
    half = total.shape[0] // 2
    for number in range(2):

        @pl.when(order == number)
        def _():
            refs[1 + 2 * number][...] = total[:half]
            refs[2 + 2 * number][...] = total[half:]


def gradient_rows(src, left, right, steps, came=None):
    tokens, features = left.shape
    columns = right.shape[1] // 2
    size = columns // steps
    rows = src.shape[1]
    in_specs = [
        pl.BlockSpec((1, rows, 1), lambda o, j: (o, 0, 0)),
        pl.BlockSpec((tokens, features), lambda o, j: (0, 0)),
        pl.BlockSpec((tokens, size), lambda o, j: (0, o * steps + j)),
    ]
    operands = [src, left, right]
    paired = pl.BlockSpec((1, rows, size), lambda o, j: (o, 0, j))
    if came is None:
        out_shape = jax.ShapeDtypeStruct((2, rows, columns), jnp.bfloat16)
        out_specs = paired
    else:
        in_specs.append(paired)
        operands.append(came)
        out_shape = [jax.ShapeDtypeStruct((rows // 2, columns), jnp.bfloat16)] * 4
        early = pl.BlockSpec((rows // 2, size), lambda o, j: (0, jnp.where(o == 0, j, steps - 1)))
        late = pl.BlockSpec((rows // 2, size), lambda o, j: (0, jnp.where(o == 0, 0, j)))
        out_specs = [early, early, late, late]
    return pl.pallas_call(
        functools.partial(rows_kernel, came is not None),
        grid=(2, steps),
        in_specs=in_specs,
        out_specs=out_specs,
        out_shape=out_shape,
        scratch_shapes=[pltpu.VMEM((rows, tokens), jnp.bfloat16)],
        compiler_params=pltpu.CompilerParams(vmem_limit_bytes=VMEM),
        cost_estimate=pl.CostEstimate(
            flops=4 * rows * tokens * columns,
            bytes_accessed=2 * (tokens * features + 2 * columns * (tokens + rows)),
            transcendentals=0,
        ),
    )(*operands)


def units_kernel(adding, order_ref, left_ref, right_ref, *refs):
    order, at = pl.program_id(0), pl.program_id(1)
    blocks = order_ref.shape[1] // 2
    chosen = jnp.concatenate(
        [
            left_ref[:, pl.ds(pl.multiple_of(order_ref[order, at * blocks + i] * 128, 128), 128)]
            for i in range(blocks)
        ],
        1,
    )
    total = product_tn(chosen, right_ref[...])
    if not adding:
        refs[0][0] = total.astype(jnp.bfloat16)
        return
    total = (total + refs[0][0].astype(jnp.float32)).astype(jnp.bfloat16)
    for number in range(4):

        @pl.when(order * 2 + at == number)
        def _():
            refs[1 + number][...] = total


def gradient_units(order, left, right, came=None):
    tokens = left.shape[0]
    rows, columns = order.shape[1] * 128, right.shape[1] // 2
    paired = pl.BlockSpec((1, rows // 2, columns), lambda o, j, *_: (o, j, 0))
    in_specs = [
        pl.BlockSpec(left.shape, lambda o, j, *_: (0, 0)),
        pl.BlockSpec((tokens, columns), lambda o, j, *_: (0, o)),
    ]
    operands = [order, left, right]
    if came is None:
        out_shape = jax.ShapeDtypeStruct((2, rows, columns), jnp.bfloat16)
        out_specs = paired
    else:
        in_specs.append(paired)
        operands.append(came)
        out_shape = [jax.ShapeDtypeStruct((rows // 2, columns), jnp.bfloat16)] * 4
        out_specs = [pl.BlockSpec((rows // 2, columns), lambda o, j, *_: (0, 0))] * 4
    return pl.pallas_call(
        functools.partial(units_kernel, came is not None),
        grid_spec=pltpu.PrefetchScalarGridSpec(
            num_scalar_prefetch=1, grid=(2, 2), in_specs=in_specs, out_specs=out_specs
        ),
        out_shape=out_shape,
        compiler_params=pltpu.CompilerParams(vmem_limit_bytes=VMEM),
        cost_estimate=pl.CostEstimate(
            flops=4 * rows * tokens * columns,
            bytes_accessed=2 * (left.size + right.size + 4 * rows * columns),
            transcendentals=0,
        ),
    )(*operands)


def added(kept, came, pieces):
    size = kept.shape[0] // pieces
    return [
        kept[i * size : (i + 1) * size].astype(jnp.float32)
        + came[i * size : (i + 1) * size].astype(jnp.float32)
        for i in range(pieces)
    ]


def second_halving(grid, kept, came, mask):
    sent, own = (part.astype(jnp.bfloat16) for part in added(kept, came, 2))
    return own, grid.swap(sent, mask)


def last_sum(grid, kept, came):
    parts = added(kept, came, len(grid.rest))
    total = parts[0]
    for part, mask in zip(parts[1:], grid.rest[1:]):
        total = total + grid.swap(part.astype(jnp.bfloat16), mask).astype(jnp.float32)
    return total


def norm_forward(field, gain):
    factor = lax.rsqrt(jnp.mean(field * field, axis=-1, keepdims=True) + eps)
    return ((field * factor * gain).astype(jnp.bfloat16), factor)


def norm_backward(field, factor, gain, grad):
    weighted = grad * gain
    gain_grad = jnp.sum(grad * field * factor, axis=0)
    field_grad = factor * weighted - field * factor**3 * jnp.mean(
        weighted * field, axis=-1, keepdims=True
    )
    return (field_grad, gain_grad)


def chosen_mask(picked):
    labels = jnp.arange(EXPERTS, dtype=jnp.int32)
    return jnp.sum(
        (picked[:, :, :, None] == labels[None, None, None, :]).astype(jnp.float32), axis=2
    )


def core_stage(grid, left, right, extra=None):
    bit = ("seq", 0)
    mine = grid.mine(bit)

    def partial(chosen, columns=None, extra_part=None):
        shape = chosen.array.shape
        out = product(chosen.array.reshape(-1, shape[-1]), right if columns is None else right[:, columns])
        out = out.reshape(shape[:-1] + (out.shape[-1],))
        if extra_part is not None:
            out = out + extra_part.array
        return out

    theirs = left.pick(bit, 1 - mine)
    extra_theirs = None if extra is None else extra.pick(bit, 1 - mine)
    sent = partial(theirs, None, extra_theirs).astype(jnp.bfloat16)
    came = Shards(grid.swap(sent, bit), theirs.bits)
    own = left.pick(bit, mine)
    extra_own = None if extra is None else extra.pick(bit, mine)
    return own, came, extra_own, partial


def plane_stage(grid, staged, first, second, columns):
    own, came, extra, partial = staged
    mine = grid.mine(first)

    def half(value):
        chosen, arrived = own.pick(first, value), came.pick(first, value)
        part = None if extra is None else extra.pick(first, value).map(lambda a: a[..., columns])
        total = partial(chosen, columns, part) + arrived.array[..., columns].astype(jnp.float32)
        return Shards(total.astype(jnp.bfloat16), chosen.bits)

    sent = half(1 - mine)
    arrived = Shards(grid.swap(sent.array, first), sent.bits)
    kept = half(mine)
    return halve(grid, kept, arrived, second)


def halve(grid, kept, arrived, bit):
    mine = grid.mine(bit)

    def half(value):
        a, b = kept.pick(bit, value), arrived.pick(bit, value)
        return Shards(
            (a.array.astype(jnp.float32) + b.array.astype(jnp.float32)).astype(jnp.bfloat16), a.bits
        )

    sent = half(1 - mine)
    return half(mine), Shards(grid.swap(sent.array, bit), sent.bits)


def rest_stages(grid, pair, bits):
    kept, arrived = pair
    for bit in bits:
        kept, arrived = halve(grid, kept, arrived, bit)
    return kept.array.astype(jnp.float32) + arrived.array.astype(jnp.float32)


def joined(pairs):
    kept = Shards(jnp.stack([p[0].array for p in pairs], len(pairs[0][0].bits)), pairs[0][0].bits)
    came = Shards(jnp.stack([p[1].array for p in pairs], len(pairs[0][1].bits)), pairs[0][1].bits)
    return kept, came


def body(
    tokens,
    segments,
    value_experts,
    out_experts,
    norm_gain,
    w_query,
    w_key,
    w_value,
    w_vgate,
    w_ogate,
    w_out,
    ffn_gain,
    w_up,
    w_down,
    cotangent,
):
    grid = Grid()
    orders = [
        jnp.stack(
            [
                grid.order(grid.plane_a, grid.plane_b, theirs),
                grid.order(grid.plane_b, grid.plane_a, theirs),
            ]
        )
        for theirs in (True, False)
    ]
    micro, _, block, width = tokens.shape
    rows = micro * block
    hidden_units = w_up.shape[1]
    place = lax.axis_index("seq")
    own_segs = lax.dynamic_slice_in_dim(segments, place * block, block, 2)[:, 0]
    prior_start = jnp.maximum(place - 1, 0) * block
    prior_segs = jnp.where(
        place > 0, lax.dynamic_slice_in_dim(segments, prior_start, block, 2)[:, 0], -1
    )
    gain_one, gain_two = norm_gain.astype(jnp.float32), ffn_gain.astype(jnp.float32)
    att_scale = HEAD ** (-0.5)

    field = tokens.reshape(rows, width).astype(jnp.float32)
    normed, factor_one = norm_forward(field, gain_one)
    keys = product(normed, w_key).astype(jnp.bfloat16)
    value_sig = jax.nn.sigmoid(product(normed, w_vgate)).reshape(rows, HEADS, EXPERTS)
    value_pick = chosen_mask(value_experts.reshape(rows, HEADS, 2))
    value_gates = value_sig * value_pick
    expert_values = product(normed, w_value).reshape(rows, HEADS, EXPERTS, HEAD)
    values = (
        jnp.sum(value_gates[..., None] * expert_values, axis=2)
        .reshape(rows, HEADS * HEAD)
        .astype(jnp.bfloat16)
    )
    mem_keys, mem_values = passed_along((keys, values), "seq", 1)
    query = product(normed, w_query).astype(jnp.bfloat16)
    split = (micro, block, HEADS, HEAD)
    key_all = jnp.concatenate([mem_keys.reshape(split), keys.reshape(split)], 1)
    value_all = jnp.concatenate([mem_values.reshape(split), values.reshape(split)], 1)
    query_heads = query.reshape(split)
    key_segs = jnp.concatenate([prior_segs, own_segs], 1)
    query_place = jnp.arange(block, dtype=jnp.int32) + block
    key_place = jnp.arange(2 * block, dtype=jnp.int32)
    allowed = (own_segs[:, :, None] == key_segs[:, None, :]) & (
        key_place[None, None, :] <= query_place[None, :, None]
    )
    scores = (
        jnp.einsum("mqhd,mkhd->mhqk", query_heads, key_all, preferred_element_type=jnp.float32)
        * att_scale
    )
    scores = jnp.where(allowed[:, None], scores, -1e30)
    top = jnp.max(scores, axis=-1, keepdims=True)
    expo = jnp.exp(scores - top)
    probs = expo / jnp.sum(expo, axis=-1, keepdims=True)
    probs_low = probs.astype(jnp.bfloat16)
    attended = (
        jnp.einsum("mhqk,mkhd->mqhd", probs_low, value_all, preferred_element_type=jnp.float32)
        .astype(jnp.bfloat16)
        .reshape(rows, HEADS, HEAD)
    )
    out_sig = jax.nn.sigmoid(product(normed, w_ogate)).reshape(rows, HEADS, EXPERTS)
    out_pick = chosen_mask(out_experts.reshape(rows, HEADS, 2))
    out_gates = out_sig * out_pick
    attended_f = attended.astype(jnp.float32)
    mixed = (
        (out_gates[..., None] * attended_f[:, :, None, :])
        .reshape(rows, HEADS * EXPERTS * HEAD)
        .astype(jnp.bfloat16)
    )
    hidden = field + product(mixed, w_out)
    normed_two, factor_two = norm_forward(hidden, gain_two)
    pre = product(normed_two, w_up)
    cdf = 0.5 * (1.0 + lax.erf(pre * (1.0 / math.sqrt(2.0))))
    upper = (pre * cdf).astype(jnp.bfloat16)
    slope = cdf + pre * (jnp.exp(-0.5 * pre * pre) * (1.0 / math.sqrt(2.0 * math.pi)))
    d_down = cotangent.reshape(rows, width)
    grad_out = d_down.astype(jnp.float32)

    share = width // grid.count
    sources = [
        (order[:, :, None] * share + jnp.arange(share, dtype=jnp.int32)).reshape(2, -1, 1)
        for order in orders
    ]
    units = hidden_units // grid.count
    if units == 128:
        unit_left, unit_orders = [upper, upper], orders
    else:
        lists = [(o[:, :, None] * units + jnp.arange(units)).reshape(-1) for o in orders]
        unit_left = [upper[:, at] for at in lists]
        unit_orders = [jnp.arange(hidden_units // 128, dtype=jnp.int32).reshape(2, -1)] * 2
    down_sent = gradient_units(unit_orders[0], unit_left[0], d_down)
    down_came = grid.swap(down_sent, grid.core)
    d_up = after(d_down, down_sent)
    d_pre = (product_nt(d_up, w_down) * slope).astype(jnp.bfloat16)
    up_sent = gradient_rows(sources[0], normed_two, d_pre, 2)
    up_came = grid.swap(up_sent, grid.core)
    down_parts = gradient_units(unit_orders[1], unit_left[1], after(d_down, up_sent), down_came)
    down_one = [grid.swap(down_parts[0], grid.plane_a), grid.swap(down_parts[2], grid.plane_b)]
    up_parts = gradient_rows(sources[1], after(normed_two, *down_parts), d_pre, 2, up_came)
    up_one = [grid.swap(up_parts[0], grid.plane_a), grid.swap(up_parts[2], grid.plane_b)]
    d_pre = after(d_pre, *up_parts)
    d_normed_two = product_nt(d_pre, w_up)
    d_hidden_norm, grad_gain_two = norm_backward(hidden, factor_two, gain_two, d_normed_two)
    d_hidden = grad_out + d_hidden_norm
    d_branch = d_hidden.astype(jnp.bfloat16)
    mixed_wide = jnp.pad(mixed, ((0, 0), (0, -mixed.shape[1] % 256)))
    out_sent = gradient_rows(sources[0], d_branch, mixed_wide, 1)
    out_came = grid.swap(out_sent, grid.core)
    d_mixed = product_nt(after(d_branch, out_sent), w_out)
    out_parts = gradient_rows(sources[1], after(d_branch, d_mixed), mixed_wide, 1, out_came)
    out_one = [grid.swap(out_parts[0], grid.plane_a), grid.swap(out_parts[2], grid.plane_b)]
    d_mixed = after(d_mixed, *out_parts).reshape(rows, HEADS, EXPERTS, HEAD)
    result = (hidden + product(upper, w_down)).astype(jnp.bfloat16)
    d_attended = jnp.sum(out_gates[..., None] * d_mixed, axis=2).astype(jnp.bfloat16)
    d_ogate = jnp.sum(attended_f[:, :, None, :] * d_mixed, axis=3)
    d_ologit = (
        (d_ogate * out_pick * out_sig * (1.0 - out_sig))
        .reshape(rows, HEADS * EXPERTS)
        .astype(jnp.bfloat16)
    )
    d_attended = d_attended.reshape(split)
    d_probs = jnp.einsum(
        "mqhd,mkhd->mhqk", d_attended, value_all, preferred_element_type=jnp.float32
    )
    delta = jnp.sum(probs * d_probs, axis=-1, keepdims=True)
    d_scores = (probs * (d_probs - delta)).astype(jnp.bfloat16)
    d_query = (
        (
            jnp.einsum("mhqk,mkhd->mqhd", d_scores, key_all, preferred_element_type=jnp.float32)
            * att_scale
        )
        .reshape(rows, HEADS * HEAD)
        .astype(jnp.bfloat16)
    )
    d_keys = (
        (
            jnp.einsum(
                "mhqk,mqhd->mkhd",
                d_scores[..., block:],
                query_heads,
                preferred_element_type=jnp.float32,
            )
            * att_scale
        )
        .reshape(rows, HEADS * HEAD)
        .astype(jnp.bfloat16)
    )
    d_values = (
        jnp.einsum(
            "mhqk,mqhd->mkhd",
            probs_low[..., block:],
            d_attended,
            preferred_element_type=jnp.float32,
        )
        .astype(jnp.bfloat16)
        .reshape(rows, HEADS, HEAD)
    )
    d_values_f = d_values.astype(jnp.float32)
    d_expert = (
        (value_gates[..., None] * d_values_f[:, :, None, :])
        .reshape(rows, HEADS * EXPERTS * HEAD)
        .astype(jnp.bfloat16)
    )
    d_vgate = jnp.sum(expert_values * d_values_f[:, :, None, :], axis=3)
    d_vlogit = (
        (d_vgate * value_pick * value_sig * (1.0 - value_sig))
        .reshape(rows, HEADS * EXPERTS)
        .astype(jnp.bfloat16)
    )
    d_normed = (
        product_nt(d_ologit, w_ogate)
        + product_nt(d_query, w_query)
        + product_nt(d_keys, w_key)
        + product_nt(d_expert, w_value)
        + product_nt(d_vlogit, w_vgate)
    )
    d_field_norm, grad_gain_one = norm_backward(field, factor_one, gain_one, d_normed)
    field_grad = (d_hidden + d_field_norm).astype(jnp.bfloat16)

    pads, starts, total = [], [], 0
    for piece in (d_expert, d_query, d_keys, jnp.concatenate([d_vlogit, d_ologit], 1)):
        starts.append(total)
        pads.append(jnp.pad(piece, ((0, 0), (0, -piece.shape[1] % 128))))
        total += pads[-1].shape[1]
    gates = d_vlogit.shape[1]
    spare = starts[3] + 2 * gates
    more = -total % 256
    pads[-1] = jnp.pad(pads[-1], ((0, 0), (0, more)))
    total += more
    extra_left, extra_right = [], []
    for number, gain in enumerate((grad_gain_one, grad_gain_two)):
        for _ in range(3):
            low = gain.astype(jnp.bfloat16)
            gain = gain - low.astype(jnp.float32)
            extra_left.append(low)
            extra_right.append(jnp.arange(total) == spare + number)
    fill = 16 - len(extra_left)
    left = jnp.concatenate([normed, jnp.pad(jnp.stack(extra_left), ((0, fill), (0, 0)))], 0)
    right = jnp.concatenate(
        [
            jnp.concatenate(pads, 1),
            jnp.pad(jnp.stack(extra_right).astype(jnp.bfloat16), ((0, fill), (0, 0))),
        ],
        0,
    )
    in_sent = gradient_rows(sources[0], left, right, 1)
    in_came = grid.swap(in_sent, grid.core)
    in_parts = gradient_rows(sources[1], left, right, 1, in_came)
    in_one = [grid.swap(in_parts[0], grid.plane_a), grid.swap(in_parts[2], grid.plane_b)]

    def finished(parts, one):
        first = second_halving(grid, parts[1], one[0], grid.plane_b)
        second = second_halving(grid, parts[3], one[1], grid.plane_a)
        kept, came = (jnp.concatenate(pair, 1) for pair in zip(first, second))
        return last_sum(grid, kept, came)

    grad_down = finished(down_parts, down_one)
    grad_up = finished(up_parts, up_one)
    grad_out_w = finished(out_parts, out_one)[:, : mixed.shape[1]].T
    grad_in = finished(in_parts, in_one)
    pieces = [
        grad_in[:, starts[1] : starts[1] + w_query.shape[1]],
        grad_in[:, starts[2] : starts[2] + w_key.shape[1]],
        grad_in[:, : w_value.shape[1]],
        grad_in[:, starts[3] : starts[3] + gates],
        grad_in[:, starts[3] + gates : spare],
    ]
    return (
        result.reshape(tokens.shape),
        field_grad.reshape(tokens.shape),
        grad_in[:, spare],
        pieces[0],
        pieces[1],
        pieces[2],
        pieces[3],
        pieces[4],
        grad_out_w,
        grad_in[:, spare + 1],
        grad_up,
        grad_down,
    )


def solution(mesh):
    both = ("seq", "batch")
    stream = P(None, "batch", "seq", None)
    picks = P(None, "batch", "seq", None, None)
    return jax.shard_map(
        body,
        mesh=mesh,
        in_specs=(stream, P(None, "batch", None), picks, picks) + (P(),) * 10 + (stream,),
        out_specs=(
            stream,
            stream,
            P(both),
            P(both, None),
            P(both, None),
            P(both, None),
            P(both, None),
            P(both, None),
            P(None, both),
            P(both),
            P(both, None),
            P(both, None),
        ),
        check_vma=False,
    )
```

```python
import functools
import math

import jax
import jax.numpy as jnp
import numpy as np
from jax import lax
from jax.experimental import pallas as pl
from jax.experimental.pallas import tpu as pltpu
from jax.sharding import PartitionSpec as P

HEADS = 4
HEAD = 112
EXPERTS = 5

eps = 1e-06
VMEM = 56 << 20


def product(left, right):
    return jnp.dot(left, right, preferred_element_type=jnp.float32)


def product_tn(left, right):
    return lax.dot_general(
        left, right, (((0,), (0,)), ((), ())), preferred_element_type=jnp.float32
    )


def product_nt(left, right):
    return lax.dot_general(
        left, right, (((1,), (1,)), ((), ())), preferred_element_type=jnp.float32
    )


def passed_along(value, axis, steps):
    count = lax.axis_size(axis)
    initial, last = (max(0, -steps), min(count, count - steps))
    return lax.ppermute(value, axis, [(source, source + steps) for source in range(initial, last)])


class Grid:
    def __init__(self):
        self.seq, self.batch = lax.axis_size("seq"), lax.axis_size("batch")
        self.count = self.seq * self.batch
        low = self.batch.bit_length() - 1
        self.core, self.plane_a, self.plane_b = 1 << low, 1, 2 << low
        taken = self.core | self.plane_a | self.plane_b
        masks = [m for m in range(self.count) if not m & taken]
        self.rest = masks
        self.me = lax.axis_index("seq") * self.batch + lax.axis_index("batch")

    def swap(self, value, mask):
        both = ("seq", "batch")
        return lax.ppermute(value, both, [(i, i ^ mask) for i in range(self.count)])

    def order(self, first, second, theirs):
        base = self.core if theirs else 0
        masks = [
            base | f | s | m for f in (first, 0) for s in (second, 0) for m in self.rest
        ]
        return self.me ^ jnp.array(masks, jnp.int32)


def after(value, *others):
    return lax.optimization_barrier((value,) + others)[0]


def rows_kernel(adding, src_ref, left_ref, right_ref, *refs):
    turned = refs[-1]
    order, at = pl.program_id(0), pl.program_id(1)

    @pl.when(at == 0)
    def _():
        places = lax.broadcasted_iota(jnp.int32, (turned.shape[0], left_ref.shape[1]), 1)
        picks = (src_ref[0] == places).astype(jnp.float32).astype(jnp.bfloat16)
        turned[...] = product_nt(picks, left_ref[...]).astype(jnp.bfloat16)

    total = product(turned[...], right_ref[...])
    if not adding:
        refs[0][0] = total.astype(jnp.bfloat16)
        return
    total = (total + refs[0][0].astype(jnp.float32)).astype(jnp.bfloat16)
    half = total.shape[0] // 2
    for number in range(2):

        @pl.when(order == number)
        def _():
            refs[1 + 2 * number][...] = total[:half]
            refs[2 + 2 * number][...] = total[half:]


def gradient_rows(src, left, right, steps, came=None):
    tokens, features = left.shape
    columns = right.shape[1] // 2
    size = columns // steps
    rows = src.shape[1]
    in_specs = [
        pl.BlockSpec((1, rows, 1), lambda o, j: (o, 0, 0)),
        pl.BlockSpec((tokens, features), lambda o, j: (0, 0)),
        pl.BlockSpec((tokens, size), lambda o, j: (0, o * steps + j)),
    ]
    operands = [src, left, right]
    paired = pl.BlockSpec((1, rows, size), lambda o, j: (o, 0, j))
    if came is None:
        out_shape = jax.ShapeDtypeStruct((2, rows, columns), jnp.bfloat16)
        out_specs = paired
    else:
        in_specs.append(paired)
        operands.append(came)
        out_shape = [jax.ShapeDtypeStruct((rows // 2, columns), jnp.bfloat16)] * 4
        early = pl.BlockSpec((rows // 2, size), lambda o, j: (0, jnp.where(o == 0, j, steps - 1)))
        late = pl.BlockSpec((rows // 2, size), lambda o, j: (0, jnp.where(o == 0, 0, j)))
        out_specs = [early, early, late, late]
    return pl.pallas_call(
        functools.partial(rows_kernel, came is not None),
        grid=(2, steps),
        in_specs=in_specs,
        out_specs=out_specs,
        out_shape=out_shape,
        scratch_shapes=[pltpu.VMEM((rows, tokens), jnp.bfloat16)],
        compiler_params=pltpu.CompilerParams(vmem_limit_bytes=VMEM),
        cost_estimate=pl.CostEstimate(
            flops=4 * rows * tokens * columns,
            bytes_accessed=2 * (tokens * features + 2 * columns * (tokens + rows)),
            transcendentals=0,
        ),
    )(*operands)


def units_kernel(adding, order_ref, left_ref, right_ref, *refs):
    order, at = pl.program_id(0), pl.program_id(1)
    blocks = order_ref.shape[1] // 2
    chosen = jnp.concatenate(
        [
            left_ref[:, pl.ds(pl.multiple_of(order_ref[order, at * blocks + i] * 128, 128), 128)]
            for i in range(blocks)
        ],
        1,
    )
    total = product_tn(chosen, right_ref[...])
    if not adding:
        refs[0][0] = total.astype(jnp.bfloat16)
        return
    total = (total + refs[0][0].astype(jnp.float32)).astype(jnp.bfloat16)
    for number in range(4):

        @pl.when(order * 2 + at == number)
        def _():
            refs[1 + number][...] = total


def gradient_units(order, left, right, came=None):
    tokens = left.shape[0]
    rows, columns = order.shape[1] * 128, right.shape[1] // 2
    paired = pl.BlockSpec((1, rows // 2, columns), lambda o, j, *_: (o, j, 0))
    in_specs = [
        pl.BlockSpec(left.shape, lambda o, j, *_: (0, 0)),
        pl.BlockSpec((tokens, columns), lambda o, j, *_: (0, o)),
    ]
    operands = [order, left, right]
    if came is None:
        out_shape = jax.ShapeDtypeStruct((2, rows, columns), jnp.bfloat16)
        out_specs = paired
    else:
        in_specs.append(paired)
        operands.append(came)
        out_shape = [jax.ShapeDtypeStruct((rows // 2, columns), jnp.bfloat16)] * 4
        out_specs = [pl.BlockSpec((rows // 2, columns), lambda o, j, *_: (0, 0))] * 4
    return pl.pallas_call(
        functools.partial(units_kernel, came is not None),
        grid_spec=pltpu.PrefetchScalarGridSpec(
            num_scalar_prefetch=1, grid=(2, 2), in_specs=in_specs, out_specs=out_specs
        ),
        out_shape=out_shape,
        compiler_params=pltpu.CompilerParams(vmem_limit_bytes=VMEM),
        cost_estimate=pl.CostEstimate(
            flops=4 * rows * tokens * columns,
            bytes_accessed=2 * (left.size + right.size + 4 * rows * columns),
            transcendentals=0,
        ),
    )(*operands)


def added(kept, came, pieces):
    size = kept.shape[0] // pieces
    return [
        kept[i * size : (i + 1) * size].astype(jnp.float32)
        + came[i * size : (i + 1) * size].astype(jnp.float32)
        for i in range(pieces)
    ]


def second_halving(grid, kept, came, mask):
    sent, own = (part.astype(jnp.bfloat16) for part in added(kept, came, 2))
    return own, grid.swap(sent, mask)


def last_sum(grid, kept, came):
    parts = added(kept, came, len(grid.rest))
    total = parts[0]
    for part, mask in zip(parts[1:], grid.rest[1:]):
        total = total + grid.swap(part.astype(jnp.bfloat16), mask).astype(jnp.float32)
    return total


def split_low(value):
    high = value.astype(jnp.bfloat16)
    return high, (value - high.astype(jnp.float32)).astype(jnp.bfloat16)


def product_two(value, right, how):
    high, low = split_low(value)
    return how(high, right) + how(low, right)


def ones_where(condition):
    return jnp.where(condition, 1.0, 0.0).astype(jnp.bfloat16)


def iota(shape, dimension):
    return lax.broadcasted_iota(jnp.int32, shape, dimension)


LANES = 128
WIDE = HEADS * LANES
MIX = HEADS * EXPERTS * HEAD
GATES = HEADS * EXPERTS
CHUNK = 512


def pieces_of(total):
    return [(at, min(CHUNK, total - at)) for at in range(0, total, CHUNK)]


def spread_block(keys_ref, at, size):
    return ones_where(iota((WIDE, size), 0) == keys_ref[0:1, at : at + size])


def expert_block(keys_ref, at, size, start, twice):
    lane, own = iota((LANES, size), 0), keys_ref[1:2, at : at + size]
    hit = lane == own + start
    if twice:
        hit = hit | (lane == own + (start + GATES))
    return ones_where(hit)


def gate_parts(gates):
    lane = iota(gates.shape, 1)
    high = gates.astype(jnp.bfloat16).astype(jnp.float32)
    low = ((lane >= GATES) & (lane < 2 * GATES)) | (lane >= 3 * GATES)
    return jnp.where(low, gates - high, high).astype(jnp.bfloat16)


def pad_heads(keys_ref, size):
    return ones_where(iota((WIDE, size), 0) == keys_ref[2:3, 0:size])


def normalise(field, gain):
    factor = lax.rsqrt(jnp.mean(field * field, axis=-1, keepdims=True) + eps)
    return field * factor * gain


def normalise_back(field, gain, grad):
    factor = lax.rsqrt(jnp.mean(field * field, axis=-1, keepdims=True) + eps)
    weighted = grad * gain
    gain_grad = jnp.sum(grad * field * factor, axis=0, keepdims=True)
    field_grad = factor * weighted - field * factor**3 * jnp.mean(
        weighted * field, axis=-1, keepdims=True
    )
    return field_grad, gain_grad


def value_kernel(
    tokens, gain, keys, slots, picks, w_gates, w_key, w_value, normed_out, gates_out, experts, kv
):
    normed = normalise(tokens[...].astype(jnp.float32), gain[...]).astype(jnp.bfloat16)
    normed_out[...] = normed
    own_key = product(normed, w_key[...]).astype(jnp.bfloat16)
    kv[0] = product_nt(own_key, pad_heads(keys, own_key.shape[1])).astype(jnp.bfloat16)
    logits = product(normed, w_gates[...])
    number = slots[2 * picks.shape[1] : 2 * picks.shape[1] + 1, :].astype(jnp.float32)
    count = picks.shape[1]
    one = product(picks[...], slots[0:count, :])
    two = product(picks[...], slots[count : 2 * count, :])
    gates = jnp.where((one == number) | (two == number), jax.nn.sigmoid(logits), 0.0)
    gates_out[...] = gates
    parts = gate_parts(gates)
    total = jnp.zeros((normed.shape[0], WIDE), jnp.float32)
    for at, size in pieces_of(MIX):
        own = product(normed, w_value[:, at : at + size])
        experts[:, at : at + size] = own
        weighted = own * product(parts, expert_block(keys, at, size, 0, True))
        total += product_two(weighted, spread_block(keys, at, size), product_nt)
    kv[1] = total.astype(jnp.bfloat16)


def query_kernel(normed, keys, w_query, out):
    query = product(normed[...], w_query[...]).astype(jnp.bfloat16)
    out[...] = product_nt(query, pad_heads(keys, query.shape[1])).astype(jnp.bfloat16)


def masks(seg_cols, seg_rows, at, block):
    own = seg_cols[pl.ds(at * block, block), :]
    rows = seg_rows[at]
    before = own == rows[0:1]
    here = (own == rows[1:2]) & (iota((block, block), 0) >= iota((block, block), 1))
    return before, here


def scores(query, key, allowed):
    return jnp.where(allowed, product_nt(query, key) * HEAD ** (-0.5), -1e30)


def attention_kernel(
    block, query, own, memory, gates, tokens, gain, keys, seg_cols, seg_rows, w_out,
    attended, totals, mixed, hidden, normed,
):
    micro = query.shape[0] // block

    @pl.loop(0, micro)
    def _(at):
        before, here = masks(seg_cols, seg_rows, at, block)
        rows = pl.ds(at * block, block)
        lane = iota((block, LANES), 1)
        tops = jnp.zeros((block, LANES), jnp.float32)
        for head in range(HEADS):
            cols = slice(head * LANES, (head + 1) * LANES)
            q = query[rows, cols]
            s_before = scores(q, memory[0, rows, cols], before)
            s_here = scores(q, own[0, rows, cols], here)
            top = jnp.maximum(
                jnp.max(s_before, axis=-1, keepdims=True), jnp.max(s_here, axis=-1, keepdims=True)
            )
            e_before, e_here = jnp.exp(s_before - top), jnp.exp(s_here - top)
            total = jnp.sum(e_before, axis=-1, keepdims=True) + jnp.sum(
                e_here, axis=-1, keepdims=True
            )
            share = 1.0 / total
            seen = product((e_before * share).astype(jnp.bfloat16), memory[1, rows, cols])
            seen += product((e_here * share).astype(jnp.bfloat16), own[1, rows, cols])
            attended[rows, cols] = seen.astype(jnp.bfloat16)
            tops = jnp.where(lane == head, top + jnp.log(total), tops)
        totals[rows, :] = tops

    parts = gate_parts(gates[...])
    seen = attended[...]
    total = tokens[...].astype(jnp.float32)
    for at, size in pieces_of(MIX):
        spread = product(seen, spread_block(keys, at, size))
        weight = product(parts, expert_block(keys, at, size, 2 * GATES, True))
        piece = (spread * weight).astype(jnp.bfloat16)
        mixed[:, at : at + size] = piece
        total += product(piece, w_out[at : at + size, :])
    mixed[:, MIX:] = jnp.zeros((mixed.shape[0], mixed.shape[1] - MIX), jnp.bfloat16)
    hidden[...] = total
    normed[...] = normalise(total, gain[...]).astype(jnp.bfloat16)


def units_up_kernel(normed, w_up, back, upper, d_pre):
    pre = product(normed[...], w_up[...])
    cdf = 0.5 * (1.0 + lax.erf(pre * (1.0 / math.sqrt(2.0))))
    upper[...] = (pre * cdf).astype(jnp.bfloat16)
    slope = cdf + pre * (jnp.exp(-0.5 * pre * pre) * (1.0 / math.sqrt(2.0 * math.pi)))
    d_pre[...] = (back[...] * slope).astype(jnp.bfloat16)


def units_down_kernel(
    upper, d_pre, w_down, w_up, hidden, d_down, gain, result, d_hidden, d_branch, gain_grad,
    sum_out, sum_back,
):
    at = pl.program_id(0)
    forth = product(upper[...], w_down[...])
    back = product_nt(d_pre[...], w_up[...])

    @pl.when(at == 0)
    def _():
        sum_out[...] = hidden[...] + forth
        sum_back[...] = back

    @pl.when(at > 0)
    def _():
        sum_out[...] += forth
        sum_back[...] += back

    @pl.when(at == pl.num_programs(0) - 1)
    def _():
        result[...] = sum_out[...].astype(jnp.bfloat16)
        grad, gain_grad[...] = normalise_back(hidden[...], gain[...], sum_back[...])
        grad = d_down[...].astype(jnp.float32) + grad
        d_hidden[...] = grad
        d_branch[...] = grad.astype(jnp.bfloat16)


def attention_back_kernel(
    block, d_branch, w_out, gates, attended, query, own, memory, totals, keys, seg_cols, seg_rows,
    d_query, d_key, d_value, d_logit,
    d_seen,
):
    branch, seen, gate = d_branch[...], attended[...], gates[...]
    parts = gate_parts(gate)
    to_seen = jnp.zeros((branch.shape[0], WIDE), jnp.float32)
    to_gate = jnp.zeros((branch.shape[0], LANES), jnp.float32)
    for at, size in pieces_of(MIX):
        d_mixed = product_nt(branch, w_out[at : at + size, :])
        spread = spread_block(keys, at, size)
        weight = product(parts, expert_block(keys, at, size, 2 * GATES, True))
        to_seen += product_two(d_mixed * weight, spread, product_nt)
        to_gate += product_two(
            d_mixed * product(seen, spread),
            expert_block(keys, at, size, 2 * GATES, False),
            product_nt,
        )
    d_logit[...] = (to_gate * gate * (1.0 - gate)).astype(jnp.bfloat16)
    d_seen[...] = to_seen.astype(jnp.bfloat16)
    micro = query.shape[0] // block

    @pl.loop(0, micro)
    def _(at):
        before, here = masks(seg_cols, seg_rows, at, block)
        rows = pl.ds(at * block, block)
        tops = totals[rows, :]
        for head in range(HEADS):
            cols = slice(head * LANES, (head + 1) * LANES)
            q, grad = query[rows, cols], d_seen[rows, cols]
            k_before, k_here = memory[0, rows, cols], own[0, rows, cols]
            top = tops[:, head : head + 1]
            p_before = jnp.exp(scores(q, k_before, before) - top)
            p_here = jnp.exp(scores(q, k_here, here) - top)
            g_before = product_nt(grad, memory[1, rows, cols])
            g_here = product_nt(grad, own[1, rows, cols])
            delta = jnp.sum(p_before * g_before, axis=-1, keepdims=True) + jnp.sum(
                p_here * g_here, axis=-1, keepdims=True
            )
            s_before = (p_before * (g_before - delta)).astype(jnp.bfloat16)
            s_here = (p_here * (g_here - delta)).astype(jnp.bfloat16)
            to_query = product(s_before, k_before) + product(s_here, k_here)
            d_query[rows, cols] = (to_query * HEAD ** (-0.5)).astype(jnp.bfloat16)
            to_key = product_tn(s_here, q) * HEAD ** (-0.5)
            d_key[rows, cols] = to_key.astype(jnp.bfloat16)
            to_value = product_tn(p_here.astype(jnp.bfloat16), grad)
            d_value[rows, cols] = to_value.astype(jnp.bfloat16)


V_AT, Q_AT, K_AT = 0, -(-MIX // LANES) * LANES, -(-MIX // LANES) * LANES + WIDE
IN_COLUMNS = K_AT + WIDE
SPARE = Q_AT + HEADS * HEAD


def inputs_back_kernel(
    d_query, d_key, d_value, d_logit, gates, experts, normed, tokens, d_hidden, gain, gain_two_grad,
    keys, w_gates, w_key, w_value, w_query, input_grad, left, right,
):
    rows = normed.shape[0]
    gate = gates[...]
    parts = gate_parts(gate)
    values = d_value[...]
    to_gate = jnp.zeros((rows, LANES), jnp.float32)
    total = jnp.zeros(tokens.shape, jnp.float32)
    for at, size in pieces_of(MIX):
        spread = product(values, spread_block(keys, at, size))
        weight = product(parts, expert_block(keys, at, size, 0, True))
        d_expert = (spread * weight).astype(jnp.bfloat16)
        right[0:rows, V_AT + at : V_AT + at + size] = d_expert
        to_gate += product_two(
            spread * experts[:, at : at + size],
            expert_block(keys, at, size, 0, False),
            product_nt,
        )
        total += product_nt(d_expert, w_value[:, at : at + size])
    right[0:rows, MIX:Q_AT] = jnp.zeros((rows, Q_AT - MIX), jnp.bfloat16)
    logits = (to_gate * gate * (1.0 - gate)).astype(jnp.bfloat16) + d_logit[...]
    total += product_nt(logits, w_gates[...])
    heads = pad_heads(keys, WIDE)
    size = HEADS * HEAD
    place = ones_where(
        (iota((LANES, WIDE), 1) == iota((LANES, WIDE), 0) + size) & (iota((LANES, WIDE), 0) < 60)
    )
    queries = product(d_query[...], heads)
    total += product_nt(queries[:, :size].astype(jnp.bfloat16), w_query[...])
    right[0:rows, Q_AT:K_AT] = (queries + product(logits, place)).astype(jnp.bfloat16)
    own_keys = product(d_key[...], heads).astype(jnp.bfloat16)
    total += product_nt(own_keys[:, :size], w_key[...])
    right[0:rows, K_AT:IN_COLUMNS] = own_keys
    field = tokens[...].astype(jnp.float32)
    grad, gain_grad = normalise_back(field, gain[...], total)
    input_grad[...] = (d_hidden[...] + grad).astype(jnp.bfloat16)
    left[0:rows, :] = normed[...]
    more = left.shape[0] - rows
    row, column = iota((more, field.shape[1]), 0), iota((more, IN_COLUMNS), 1)
    spare_row = iota((more, IN_COLUMNS), 0)
    extra = jnp.zeros((more, field.shape[1]), jnp.float32)
    for number, value in enumerate((gain_grad, gain_two_grad[...])):
        for part in range(3):
            low = value.astype(jnp.bfloat16).astype(jnp.float32)
            extra = jnp.where(row == 3 * number + part, low, extra)
            value = value - low
    left[rows:, :] = extra.astype(jnp.bfloat16)
    first = (spare_row < 3) & (column == SPARE + 60)
    second = (spare_row >= 3) & (spare_row < 6) & (column == SPARE + 61)
    right[rows:, :] = ones_where(first | second)


def whole(kernel, outs, *operands, flops=0, scratch=()):
    outs = [jax.ShapeDtypeStruct(shape, dtype) for shape, dtype in outs]
    size = sum(a.size * a.dtype.itemsize for a in list(operands) + outs)
    return pl.pallas_call(
        kernel,
        out_shape=outs,
        scratch_shapes=list(scratch),
        compiler_params=pltpu.CompilerParams(vmem_limit_bytes=VMEM),
        cost_estimate=pl.CostEstimate(flops=flops, bytes_accessed=size, transcendentals=0),
    )(*operands)


def body(
    tokens,
    segments,
    value_experts,
    out_experts,
    norm_gain,
    w_query,
    w_key,
    w_value,
    w_vgate,
    w_ogate,
    w_out,
    ffn_gain,
    w_up,
    w_down,
    cotangent,
):
    grid = Grid()
    orders = [
        jnp.stack(
            [
                grid.order(grid.plane_a, grid.plane_b, theirs),
                grid.order(grid.plane_b, grid.plane_a, theirs),
            ]
        )
        for theirs in (True, False)
    ]
    micro, _, block, width = tokens.shape
    rows = micro * block
    hidden_units = w_up.shape[1]
    place = lax.axis_index("seq")
    own_segs = lax.dynamic_slice_in_dim(segments, place * block, block, 2)[:, 0]
    prior_start = jnp.maximum(place - 1, 0) * block
    prior_segs = jnp.where(
        place > 0, lax.dynamic_slice_in_dim(segments, prior_start, block, 2)[:, 0], -1
    )
    gain_one = norm_gain.astype(jnp.float32)[None]
    gain_two = ffn_gain.astype(jnp.float32)[None]
    column = np.arange(-(-MIX // LANES) * LANES)
    head_column = np.arange(WIDE)
    keys = np.full((3, column.size), -1, np.int32)
    keys[0, :MIX] = (column // (EXPERTS * HEAD) * LANES + column % HEAD)[:MIX]
    keys[1, :MIX] = (column // HEAD)[:MIX]
    keys[2, : HEADS * HEAD] = (head_column // HEAD * LANES + head_column % HEAD)[: HEADS * HEAD]
    keys = jnp.asarray(keys)
    lane = np.arange(4 * GATES)
    slots = np.zeros((2 * 16 + 8, LANES), np.float32)
    source = 2 * (lane % GATES // EXPERTS) + 2 * HEADS * (lane // (2 * GATES))
    slots[source, lane] = 1
    slots[16 + source + 1, lane] = 1
    slots[32] = -1
    slots[32, : 4 * GATES] = lane % EXPERTS
    slots = jnp.asarray(slots, jnp.bfloat16)
    picks = jnp.concatenate(
        [value_experts.reshape(rows, 2 * HEADS), out_experts.reshape(rows, 2 * HEADS)], 1
    ).astype(jnp.bfloat16)
    w_gates = jnp.concatenate([w_vgate, w_vgate, w_ogate, w_ogate], 1)
    w_gates = jnp.pad(w_gates, ((0, 0), (0, LANES - w_gates.shape[1])))
    seg_cols = own_segs.reshape(rows, 1)
    seg_rows = jnp.stack([prior_segs, own_segs], 1)

    field = tokens.reshape(rows, width)
    d_down = cotangent.reshape(rows, width)
    low, full = jnp.bfloat16, jnp.float32
    normed, gates, experts, kv = whole(
        value_kernel,
        [((rows, width), low), ((rows, LANES), full), ((rows, MIX), full), ((2, rows, WIDE), low)],
        field, gain_one, keys, slots, picks, w_gates, w_key, w_value,
        flops=2 * rows * MIX * (width + LANES + 2 * WIDE),
    )
    memory = passed_along(kv, "seq", 1)
    back = product_nt(after(d_down, kv), w_down)
    (query,) = whole(
        query_kernel, [((rows, WIDE), low)], after(normed, back), keys, w_query,
        flops=2 * rows * WIDE * (width + WIDE),
    )
    mixed_columns = -(-MIX // 256) * 256
    attended, totals, mixed, hidden, normed_two = whole(
        functools.partial(attention_kernel, block),
        [
            ((rows, WIDE), low),
            ((rows, LANES), full),
            ((rows, mixed_columns), low),
            ((rows, width), full),
            ((rows, width), low),
        ],
        query, kv, memory, gates, field, gain_two, keys, seg_cols, seg_rows, w_out,
        flops=2 * rows * MIX * (width + LANES + WIDE) + 8 * rows * block * WIDE,
    )
    step = 512
    fixed = pl.BlockSpec((rows, width), lambda j: (0, 0))
    across = pl.BlockSpec((rows, step), lambda j: (0, j))
    up_block = pl.BlockSpec((width, step), lambda j: (0, j))
    upper, d_pre = pl.pallas_call(
        units_up_kernel,
        grid=(hidden_units // step,),
        in_specs=[fixed, up_block, across],
        out_specs=[across, across],
        out_shape=[jax.ShapeDtypeStruct((rows, hidden_units), low)] * 2,
        compiler_params=pltpu.CompilerParams(vmem_limit_bytes=VMEM),
        cost_estimate=pl.CostEstimate(
            flops=2 * rows * width * hidden_units,
            bytes_accessed=2 * hidden_units * (width + 4 * rows),
            transcendentals=rows * hidden_units,
        ),
    )(normed_two, w_up, back)

    share = width // grid.count
    sources = [
        (order[:, :, None] * share + jnp.arange(share, dtype=jnp.int32)).reshape(2, -1, 1)
        for order in orders
    ]
    units = hidden_units // grid.count
    if units == 128:
        unit_left, unit_orders = [upper, upper], orders
    else:
        lists = [(o[:, :, None] * units + jnp.arange(units)).reshape(-1) for o in orders]
        unit_left = [upper[:, at] for at in lists]
        unit_orders = [jnp.arange(hidden_units // 128, dtype=jnp.int32).reshape(2, -1)] * 2
    down_sent = gradient_units(unit_orders[0], unit_left[0], d_down)
    down_came = grid.swap(down_sent, grid.core)
    up_sent = gradient_rows(sources[0], after(normed_two, down_sent), d_pre, 2)
    up_came = grid.swap(up_sent, grid.core)
    down_parts = gradient_units(unit_orders[1], unit_left[1], after(d_down, up_sent), down_came)
    down_one = [grid.swap(down_parts[0], grid.plane_a), grid.swap(down_parts[2], grid.plane_b)]
    up_parts = gradient_rows(sources[1], after(normed_two, *down_parts), d_pre, 2, up_came)
    up_one = [grid.swap(up_parts[0], grid.plane_a), grid.swap(up_parts[2], grid.plane_b)]
    d_pre = after(d_pre, *up_parts)
    row_block = pl.BlockSpec((1, width), lambda j: (0, 0))
    result, d_hidden, d_branch, gain_two_grad = pl.pallas_call(
        units_down_kernel,
        grid=(hidden_units // step,),
        in_specs=[
            across,
            across,
            pl.BlockSpec((step, width), lambda j: (j, 0)),
            up_block,
            fixed,
            fixed,
            row_block,
        ],
        out_specs=[fixed, fixed, fixed, row_block],
        out_shape=[
            jax.ShapeDtypeStruct((rows, width), low),
            jax.ShapeDtypeStruct((rows, width), full),
            jax.ShapeDtypeStruct((rows, width), low),
            jax.ShapeDtypeStruct((1, width), full),
        ],
        scratch_shapes=[pltpu.VMEM((rows, width), full)] * 2,
        compiler_params=pltpu.CompilerParams(vmem_limit_bytes=VMEM),
        cost_estimate=pl.CostEstimate(
            flops=4 * rows * width * hidden_units,
            bytes_accessed=4 * hidden_units * (width + rows) + 12 * rows * width,
            transcendentals=0,
        ),
    )(upper, d_pre, w_down, w_up, hidden, d_down, gain_two)
    out_sent = gradient_rows(sources[0], d_branch, mixed, 1)
    out_came = grid.swap(out_sent, grid.core)
    d_query, d_key, d_value, d_logit = whole(
        functools.partial(attention_back_kernel, block),
        [((rows, WIDE), low)] * 3 + [((rows, LANES), low)],
        after(d_branch, out_sent), w_out, gates, attended, query, kv, memory, totals,
        keys, seg_cols, seg_rows,
        flops=2 * rows * MIX * (width + 5 * WIDE) + 20 * rows * block * WIDE,
        scratch=[pltpu.VMEM((rows, WIDE), low)],
    )
    out_parts = gradient_rows(sources[1], after(d_branch, d_query), mixed, 1, out_came)
    out_one = [grid.swap(out_parts[0], grid.plane_a), grid.swap(out_parts[2], grid.plane_b)]
    input_grad, left, right = whole(
        inputs_back_kernel,
        [((rows, width), low), ((rows + 16, width), low), ((rows + 16, IN_COLUMNS), low)],
        d_query, d_key, after(d_value, *out_parts), d_logit, gates, experts, normed, field,
        d_hidden, gain_one, gain_two_grad, keys, w_gates, w_key, w_value, w_query,
        flops=2 * rows * MIX * (width + 3 * WIDE) + 4 * rows * width * WIDE,
    )
    in_sent = gradient_rows(sources[0], left, right, 1)
    in_came = grid.swap(in_sent, grid.core)
    in_parts = gradient_rows(sources[1], left, right, 1, in_came)
    in_one = [grid.swap(in_parts[0], grid.plane_a), grid.swap(in_parts[2], grid.plane_b)]

    def finished(parts, one):
        first = second_halving(grid, parts[1], one[0], grid.plane_b)
        second = second_halving(grid, parts[3], one[1], grid.plane_a)
        kept, came = (jnp.concatenate(pair, 1) for pair in zip(first, second))
        return last_sum(grid, kept, came)

    grad_down = finished(down_parts, down_one)
    grad_up = finished(up_parts, up_one)
    grad_out_w = finished(out_parts, out_one)[:, :MIX].T
    grad_in = finished(in_parts, in_one)

    def taken(at, size):
        return grad_in[:, at : at + size]

    return (
        result.reshape(tokens.shape),
        input_grad.reshape(tokens.shape),
        grad_in[:, SPARE + 60],
        taken(Q_AT, HEADS * HEAD),
        taken(K_AT, HEADS * HEAD),
        taken(V_AT, MIX),
        taken(SPARE, GATES),
        taken(SPARE + 2 * GATES, GATES),
        grad_out_w,
        grad_in[:, SPARE + 61],
        grad_up,
        grad_down,
    )


def solution(mesh):
    both = ("seq", "batch")
    stream = P(None, "batch", "seq", None)
    picks = P(None, "batch", "seq", None, None)
    return jax.shard_map(
        body,
        mesh=mesh,
        in_specs=(stream, P(None, "batch", None), picks, picks) + (P(),) * 10 + (stream,),
        out_specs=(
            stream,
            stream,
            P(both),
            P(both, None),
            P(both, None),
            P(both, None),
            P(both, None),
            P(both, None),
            P(None, both),
            P(both),
            P(both, None),
            P(both, None),
        ),
        check_vma=False,
    )
```

```python
import functools
import math

import jax
import jax.numpy as jnp
import numpy as np
from jax import lax
from jax.experimental import pallas as pl
from jax.experimental.pallas import tpu as pltpu
from jax.sharding import PartitionSpec as P

HEADS = 4
HEAD = 112
EXPERTS = 5

eps = 1e-06
VMEM = 56 << 20
HIDDEN = 4096
BRIEF = pl.CostEstimate(flops=1024, bytes_accessed=1024, transcendentals=0)


def product(left, right):
    return jnp.dot(left, right, preferred_element_type=jnp.float32)


def product_tn(left, right):
    return lax.dot_general(
        left, right, (((0,), (0,)), ((), ())), preferred_element_type=jnp.float32
    )


def product_nt(left, right):
    return lax.dot_general(
        left, right, (((1,), (1,)), ((), ())), preferred_element_type=jnp.float32
    )


def passed_along(value, axis, steps):
    count = lax.axis_size(axis)
    initial, last = (max(0, -steps), min(count, count - steps))
    return lax.ppermute(value, axis, [(source, source + steps) for source in range(initial, last)])


class Grid:
    def __init__(self):
        self.seq, self.batch = lax.axis_size("seq"), lax.axis_size("batch")
        self.count = self.seq * self.batch
        low = self.batch.bit_length() - 1
        self.core, self.plane_a, self.plane_b = 1 << low, 1, 2 << low
        taken = self.core | self.plane_a | self.plane_b
        self.rest = [1 << at for at in range(self.count.bit_length() - 1) if not (1 << at) & taken]
        self.me = lax.axis_index("seq") * self.batch + lax.axis_index("batch")

    def swap(self, value, mask):
        both = ("seq", "batch")
        return lax.ppermute(value, both, [(i, i ^ mask) for i in range(self.count)])

    def order(self, bits):
        masks = [0]
        for bit in bits:
            masks = [mask | own for mask in masks for own in (bit, 0)]
        return self.me ^ jnp.array(masks, jnp.int32)


def after(value, *others):
    return lax.optimization_barrier((value,) + others)[0]


def halves_out(order, total, refs):
    total = total.astype(jnp.bfloat16)
    half = total.shape[0] // 2
    for number in range(2):

        @pl.when(order == number)
        def _():
            refs[2 * number][...] = total[:half]
            refs[2 * number + 1][...] = total[half:]


def turn(src, parts, turned):
    at = 0
    for part in parts:
        places = iota((turned.shape[0], part.shape[1]), 1)
        picked = product_nt(ones_where(src == places), part[...]).astype(jnp.bfloat16)
        turned[:, at : at + part.shape[0]] = picked
        at += part.shape[0]


def rows_kernel(src, left, left_came, right, right_came, *refs):
    turned = refs[-1]

    @pl.when(pl.program_id(1) == 0)
    def _():
        turn(src[0], (left, left_came), turned)

    tokens = left.shape[0]
    total = product(turned[:, :tokens], right[...]) + product(turned[:, tokens:], right_came[...])
    halves_out(pl.program_id(0), total, refs)


def gradient_rows(src, left, right, steps):
    tokens, features = left[0].shape
    columns = right[0].shape[1] // 2
    size = columns // steps
    rows = src.shape[1]
    fixed = pl.BlockSpec((tokens, features), lambda o, j: (0, 0))
    moving = pl.BlockSpec((tokens, size), lambda o, j: (0, o * steps + j))
    early = pl.BlockSpec((rows // 2, size), lambda o, j: (0, jnp.where(o == 0, j, steps - 1)))
    late = pl.BlockSpec((rows // 2, size), lambda o, j: (0, jnp.where(o == 0, 0, j)))
    return pl.pallas_call(
        rows_kernel,
        grid=(2, steps),
        in_specs=[pl.BlockSpec((1, rows, 1), lambda o, j: (o, 0, 0)), fixed, fixed, moving, moving],
        out_specs=[early, early, late, late],
        out_shape=[jax.ShapeDtypeStruct((rows // 2, columns), jnp.bfloat16)] * 4,
        scratch_shapes=[pltpu.VMEM((rows, 2 * tokens), jnp.bfloat16)],
        compiler_params=pltpu.CompilerParams(vmem_limit_bytes=VMEM),
        cost_estimate=BRIEF,
    )(src, *left, *right)


def units_kernel(order_ref, left, left_came, right, right_came, *outs):
    order, at = pl.program_id(0), pl.program_id(1)
    blocks = order_ref.shape[2] // 2

    def chosen(number, ref):
        return jnp.concatenate(
            [
                ref[:, pl.ds(pl.multiple_of(order_ref[number, order, at * blocks + i] * 128, 128), 128)]
                for i in range(blocks)
            ],
            1,
        )

    total = product_tn(chosen(0, left), right[...]) + product_tn(chosen(1, left_came), right_came[...])
    total = total.astype(jnp.bfloat16)
    for number in range(2):

        @pl.when(at == number)
        def _():
            outs[number][...] = total


def gradient_units(order, left, right):
    tokens = left[0].shape[0]
    rows, columns = order.shape[2] * 128, right[0].shape[1] // 2
    moving = pl.BlockSpec((tokens, columns), lambda o, j, *_: (0, o))
    in_specs = [pl.BlockSpec(part.shape, lambda o, j, *_: (0, 0)) for part in left] + [moving] * 2
    return pl.pallas_call(
        units_kernel,
        grid_spec=pltpu.PrefetchScalarGridSpec(
            num_scalar_prefetch=1,
            grid=(2, 2),
            in_specs=in_specs,
            out_specs=[pl.BlockSpec((rows // 2, columns), lambda o, j, *_: (0, o))] * 2,
        ),
        out_shape=[jax.ShapeDtypeStruct((rows // 2, 2 * columns), jnp.bfloat16)] * 2,
        compiler_params=pltpu.CompilerParams(vmem_limit_bytes=VMEM),
        cost_estimate=BRIEF,
    )(order, *left, *right)


def split_low(value):
    high = value.astype(jnp.bfloat16)
    return high, (value - high.astype(jnp.float32)).astype(jnp.bfloat16)


def product_two(value, right, how):
    high, low = split_low(value)
    return how(high, right) + how(low, right)


def ones_where(condition):
    return jnp.where(condition, 1.0, 0.0).astype(jnp.bfloat16)


def iota(shape, dimension):
    return lax.broadcasted_iota(jnp.int32, shape, dimension)


LANES = 128
WIDE = HEADS * LANES
MIX = HEADS * EXPERTS * HEAD
GATES = HEADS * EXPERTS
CHUNK = 512


def pieces_of(total):
    return [(at, min(CHUNK, total - at)) for at in range(0, total, CHUNK)]


def spread_block(keys_ref, at, size):
    return ones_where(iota((WIDE, size), 0) == keys_ref[0:1, at : at + size])


def expert_block(keys_ref, at, size, start, twice):
    lane, own = iota((LANES, size), 0), keys_ref[1:2, at : at + size]
    hit = lane == own + start
    if twice:
        hit = hit | (lane == own + (start + GATES))
    return ones_where(hit)


def gate_parts(gates):
    lane = iota(gates.shape, 1)
    high = gates.astype(jnp.bfloat16).astype(jnp.float32)
    low = ((lane >= GATES) & (lane < 2 * GATES)) | (lane >= 3 * GATES)
    return jnp.where(low, gates - high, high).astype(jnp.bfloat16)


def pad_heads(keys_ref, size):
    return ones_where(iota((WIDE, size), 0) == keys_ref[2:3, 0:size])


def normalise(field, gain):
    factor = lax.rsqrt(jnp.mean(field * field, axis=-1, keepdims=True) + eps)
    return field * factor * gain


def normalise_back(field, gain, grad):
    factor = lax.rsqrt(jnp.mean(field * field, axis=-1, keepdims=True) + eps)
    weighted = grad * gain
    field_grad = factor * weighted - field * factor**3 * jnp.mean(
        weighted * field, axis=-1, keepdims=True
    )
    return field_grad


def value_kernel(
    tokens, gain, keys, slots, picks, w_gates, w_key, w_value,
    normed_out, gates_out, parts_out, experts, kv,
):
    normed = normalise(tokens[...].astype(jnp.float32), gain[...]).astype(jnp.bfloat16)
    normed_out[...] = normed
    own_key = product_nt(normed, w_key[...]).astype(jnp.bfloat16)
    kv[0] = product_nt(own_key, pad_heads(keys, own_key.shape[1])).astype(jnp.bfloat16)
    logits = product_nt(normed, w_gates[...])
    number = slots[2 * picks.shape[1] : 2 * picks.shape[1] + 1, :].astype(jnp.float32)
    count = picks.shape[1]
    one = product(picks[...], slots[0:count, :])
    two = product(picks[...], slots[count : 2 * count, :])
    gates = jnp.where((one == number) | (two == number), jax.nn.sigmoid(logits), 0.0)
    gates_out[...] = gates
    parts = gate_parts(gates)
    parts_out[...] = parts
    total = jnp.zeros((normed.shape[0], WIDE), jnp.float32)
    for at, size in pieces_of(MIX):
        own = product_nt(normed, w_value[at : at + size, :])
        experts[:, at : at + size] = own
        weighted = own * product(parts, expert_block(keys, at, size, 0, True))
        total += product_two(weighted, spread_block(keys, at, size), product_nt)
    kv[1] = total.astype(jnp.bfloat16)


def query_kernel(normed, keys, w_query, d_down, w_down, query, back):
    back[...] = product_nt(d_down[...], w_down[...])

    @pl.when(pl.program_id(0) == 0)
    def _():
        own = product_nt(normed[...], w_query[...]).astype(jnp.bfloat16)
        query[...] = product_nt(own, pad_heads(keys, own.shape[1])).astype(jnp.bfloat16)


def masks(seg_cols, seg_rows, at, block):
    own = seg_cols[pl.ds(at * block, block), :]
    rows = seg_rows[at]
    before = own == rows[0:1]
    here = (own == rows[1:2]) & (iota((block, block), 0) >= iota((block, block), 1))
    return before, here


def scores(query, key, allowed):
    return jnp.where(allowed, product_nt(query, key) * HEAD ** (-0.5), -1e30)


def attention_kernel(
    block, query, own, memory, parts_in, tokens, gain, keys, seg_cols, seg_rows, w_out,
    attended, totals, mixed, hidden, normed,
):
    micro = query.shape[0] // block

    @pl.loop(0, micro)
    def _(at):
        before, here = masks(seg_cols, seg_rows, at, block)
        rows = pl.ds(at * block, block)
        lane = iota((block, LANES), 1)
        tops = jnp.zeros((block, LANES), jnp.float32)
        for head in range(HEADS):
            cols = slice(head * LANES, (head + 1) * LANES)
            q = query[rows, cols]
            s_before = scores(q, memory[0, rows, cols], before)
            s_here = scores(q, own[0, rows, cols], here)
            top = jnp.maximum(
                jnp.max(s_before, axis=-1, keepdims=True), jnp.max(s_here, axis=-1, keepdims=True)
            )
            e_before, e_here = jnp.exp(s_before - top), jnp.exp(s_here - top)
            total = jnp.sum(e_before, axis=-1, keepdims=True) + jnp.sum(
                e_here, axis=-1, keepdims=True
            )
            share = 1.0 / total
            seen = product((e_before * share).astype(jnp.bfloat16), memory[1, rows, cols])
            seen += product((e_here * share).astype(jnp.bfloat16), own[1, rows, cols])
            attended[rows, cols] = seen.astype(jnp.bfloat16)
            tops = jnp.where(lane == head, top + jnp.log(total), tops)
        totals[rows, :] = tops

    parts = parts_in[...]
    seen = attended[...]
    total = tokens[...].astype(jnp.float32)
    for at, size in pieces_of(MIX):
        spread = product(seen, spread_block(keys, at, size))
        weight = product(parts, expert_block(keys, at, size, 2 * GATES, True))
        piece = (spread * weight).astype(jnp.bfloat16)
        mixed[:, at : at + size] = piece
        total += product(piece, w_out[at : at + size, :])
    mixed[:, MIX:] = jnp.zeros((mixed.shape[0], mixed.shape[1] - MIX), jnp.bfloat16)
    hidden[...] = total
    normed[...] = normalise(total, gain[...]).astype(jnp.bfloat16)


def units_up_kernel(side, normed, w_up, back, upper, d_pre, theirs):
    pre = product(normed[...], w_up[...])
    cdf = 0.5 * (1.0 + lax.erf(pre * (1.0 / math.sqrt(2.0))))
    high = (pre * cdf).astype(jnp.bfloat16)
    upper[...] = high
    slope = cdf + pre * (jnp.exp(-0.5 * pre * pre) * (1.0 / math.sqrt(2.0 * math.pi)))
    d_pre[...] = (back[...] * slope).astype(jnp.bfloat16)
    half = high.shape[1] // 2

    @pl.when(side[0] == 0)
    def _():
        theirs[...] = high[:, half:]

    @pl.when(side[0] != 0)
    def _():
        theirs[...] = high[:, :half]


def units_back_kernel(
    d_pre, w_up, hidden, d_down, gain, d_hidden, d_branch, total
):
    at = pl.program_id(0)
    back = product_nt(d_pre[...], w_up[...])

    @pl.when(at == 0)
    def _():
        total[...] = back

    @pl.when(at > 0)
    def _():
        total[...] += back

    @pl.when(at == pl.num_programs(0) - 1)
    def _():
        grad = normalise_back(hidden[...], gain[...], total[...])
        grad = d_down[...].astype(jnp.float32) + grad
        d_hidden[...] = grad
        d_branch[...] = grad.astype(jnp.bfloat16)


def result_kernel(upper, w_down, hidden, result, total):
    at = pl.program_id(0)
    forth = product(upper[...], w_down[...])

    @pl.when(at == 0)
    def _():
        total[...] = hidden[...] + forth

    @pl.when(at > 0)
    def _():
        total[...] += forth

    @pl.when(at == pl.num_programs(0) - 1)
    def _():
        result[...] = total[...].astype(jnp.bfloat16)


def attention_back_kernel(
    block, d_branch, w_out, gates, parts_in, attended, query, own, memory, totals, experts, keys,
    seg_cols, seg_rows, queries_keys, values_gates,
    d_seen, d_query, d_key,
):
    branch, seen, gate, parts = d_branch[...], attended[...], gates[...], parts_in[...]
    to_seen = jnp.zeros((branch.shape[0], WIDE), jnp.float32)
    to_gate = jnp.zeros((branch.shape[0], LANES), jnp.float32)
    for at, size in pieces_of(MIX):
        d_mixed = product_nt(branch, w_out[at : at + size, :])
        spread = spread_block(keys, at, size)
        weight = product(parts, expert_block(keys, at, size, 2 * GATES, True))
        to_seen += product_two(d_mixed * weight, spread, product_nt)
        to_gate += product_two(
            d_mixed * product(seen, spread),
            expert_block(keys, at, size, 2 * GATES, False),
            product_nt,
        )
    d_seen[...] = to_seen.astype(jnp.bfloat16)
    micro = query.shape[0] // block

    @pl.loop(0, micro)
    def _(at):
        before, here = masks(seg_cols, seg_rows, at, block)
        rows = pl.ds(at * block, block)
        tops = totals[rows, :]
        for head in range(HEADS):
            cols = slice(head * LANES, (head + 1) * LANES)
            q, grad = query[rows, cols], d_seen[rows, cols]
            k_before, k_here = memory[0, rows, cols], own[0, rows, cols]
            top = tops[:, head : head + 1]
            p_before = jnp.exp(scores(q, k_before, before) - top)
            p_here = jnp.exp(scores(q, k_here, here) - top)
            g_before = product_nt(grad, memory[1, rows, cols])
            g_here = product_nt(grad, own[1, rows, cols])
            delta = jnp.sum(p_before * g_before, axis=-1, keepdims=True) + jnp.sum(
                p_here * g_here, axis=-1, keepdims=True
            )
            s_before = (p_before * (g_before - delta)).astype(jnp.bfloat16)
            s_here = (p_here * (g_here - delta)).astype(jnp.bfloat16)
            to_query = product(s_before, k_before) + product(s_here, k_here)
            d_query[rows, cols] = (to_query * HEAD ** (-0.5)).astype(jnp.bfloat16)
            to_key = product_tn(s_here, q) * HEAD ** (-0.5)
            d_key[rows, cols] = to_key.astype(jnp.bfloat16)
            to_value = product_tn(p_here.astype(jnp.bfloat16), grad)
            values_gates[rows, cols] = to_value.astype(jnp.bfloat16)

    d_value = values_gates[:, :WIDE]
    for at, size in pieces_of(MIX):
        to_gate += product_two(
            product(d_value, spread_block(keys, at, size)) * experts[:, at : at + size],
            expert_block(keys, at, size, 0, False),
            product_nt,
        )
    values_gates[:, WIDE:] = (to_gate * gate * (1.0 - gate)).astype(jnp.bfloat16)
    both = (WIDE, 2 * HEADS * HEAD)
    from_query = ones_where(iota(both, 0) == keys[2:3, : both[1]])
    from_key = ones_where(iota(both, 0) == keys[3:4, : both[1]])
    total = product(d_query[...], from_query) + product(d_key[...], from_key)
    queries_keys[...] = total.astype(jnp.bfloat16)


V_AT = 0
Q_AT = -(-MIX // LANES) * LANES
K_AT = Q_AT + HEADS * HEAD
G_AT = K_AT + HEADS * HEAD
IN_COLUMNS = G_AT + LANES


def d_experts(values_gates, parts, keys, at, size):
    spread = product(values_gates[:, :WIDE], spread_block(keys, at, size))
    weight = product(parts[...], expert_block(keys, at, size, 0, True))
    return (spread * weight).astype(jnp.bfloat16)


def inputs_kernel(
    src, left, left_came, queries_keys, queries_keys_came, values_gates, values_gates_came,
    parts, parts_came, keys, *refs,
):
    turned = refs[-1]
    half = IN_COLUMNS // 2
    tokens = left.shape[0]
    keep = refs[0].shape[0]

    def put(number, at, total):
        total = total.astype(jnp.bfloat16)
        columns = slice(at - number * half, at - number * half + total.shape[1])
        refs[2 * number][:, columns] = total[:keep]
        refs[2 * number + 1][:, columns] = total[keep:]

    def times(one, two):
        return product(turned[:, :tokens], one) + product(turned[:, tokens:], two)

    for number in range(2):
        turn(src[number], (left, left_came), turned)
        at, stop = number * half, min(MIX, (number + 1) * half)
        while at < stop:
            size = min(CHUNK, stop - at)
            one = d_experts(values_gates, parts, keys, at, size)
            two = d_experts(values_gates_came, parts_came, keys, at, size)
            put(number, at, times(one, two))
            at += size
    put(1, MIX, jnp.zeros((2 * keep, Q_AT - MIX), jnp.float32))
    for at in range(0, 2 * HEADS * HEAD, CHUNK):
        columns = slice(at, min(at + CHUNK, 2 * HEADS * HEAD))
        put(1, Q_AT + at, times(queries_keys[:, columns], queries_keys_came[:, columns]))
    put(1, G_AT, times(values_gates[:, WIDE:], values_gates_came[:, WIDE:]))


def inputs_back_kernel(
    queries_keys, values_gates, parts, keys, tokens, d_hidden, gain, w_gates, w_key, w_value,
    w_query, input_grad, w_both,
):
    size = HEADS * HEAD
    w_both[:size, :] = w_query[...]
    w_both[size:, :] = w_key[...]
    total = product(values_gates[:, WIDE:], w_gates[...])
    total += product(queries_keys[...], w_both[...])
    for at, size in pieces_of(MIX):
        total += product(d_experts(values_gates, parts, keys, at, size), w_value[at : at + size, :])
    grad = normalise_back(tokens[...].astype(jnp.float32), gain[...], total)
    input_grad[...] = (d_hidden[...] + grad).astype(jnp.bfloat16)


def pieced(generate, outs, aligned, *operands):
    if not aligned:
        results = [jnp.zeros(shape, dtype) for shape, dtype in outs]
        for number, row, column, value in generate(*operands):
            value = value.astype(results[number].dtype)
            results[number] = lax.dynamic_update_slice(results[number], value, (row, column))
        return results

    def kernel(*refs):
        given, made = refs[: len(operands)], refs[len(operands) :]
        for number, row, column, value in generate(*given):
            rows, columns = slice(row, row + value.shape[0]), slice(column, column + value.shape[1])
            made[number][rows, columns] = value.astype(made[number].dtype)

    return whole(kernel, outs, *operands)


def summed(pair, rows, columns=slice(None)):
    return sum(part[rows, columns].astype(jnp.float32) for part in pair)


def joined_halves(*refs):
    kept, came = refs[-2:]
    columns, rows = kept.shape[1] // 2, kept.shape[0] // 2
    yield from paired_halves(*refs[:-2])
    tall = refs[0].shape[0] // 2
    start = sum(ref.shape[1] for ref in refs[: len(refs) // 2 - 1 : 2])
    for number in range(2):
        own = slice((1 - number) * columns, (2 - number) * columns)
        for half in range(2):
            for block in range(rows // tall):
                at = half * rows + block * tall
                value = summed((kept, came), slice(at, at + tall), own)
                yield 2 * number + half, 0, start + block * columns, value


def blocks_halves(start, columns, *refs):
    for number in range(2):
        pair = refs[2 - 2 * number : 4 - 2 * number]
        tall = pair[0].shape[0]
        blocks = (pair[0].shape[1] - start) // columns
        for block in range(blocks):
            half, at = divmod(block, blocks // 2)
            own = slice(start + block * columns, start + (block + 1) * columns)
            yield 2 * number + half, at * tall, 0, summed(pair, slice(None), own)


def paired_halves(*refs):
    for number in range(2):
        column = 0
        own = refs[number * len(refs) // 2 : (number + 1) * len(refs) // 2]
        for pair in zip(own[::2], own[1::2]):
            rows = pair[0].shape[0] // 2
            for half in range(2):
                part = slice(half * rows, (half + 1) * rows)
                yield 2 * number + half, 0, column, summed(pair, part)
            column += pair[0].shape[1]


def laid_out(layout, *refs):
    for number, start, size, column in layout:
        pair = refs[2 * number : 2 * number + 2]
        rows = pair[0].shape[0] // 2
        for half in range(2):
            part = slice(half * rows, (half + 1) * rows)
            yield half, 0, column, summed(pair, part, slice(start, start + size))


def most_done(weight, gain, down, down_came, wide, wide_came):
    yield 0, 0, 0, summed((down, down_came), slice(None))
    along = 0.0
    for at in range(0, HIDDEN, 2 * CHUNK):
        columns = slice(at, at + 2 * CHUNK)
        piece = summed((wide, wide_came), slice(None), columns)
        yield 1, 0, at, piece
        along += jnp.sum(piece * weight[:, columns].astype(jnp.float32), axis=1, keepdims=True)
    yield 2, 0, 0, along / gain[:, :]
    yield 3, 0, 0, summed((wide, wide_came), slice(None), slice(HIDDEN, HIDDEN + MIX))


def in_done(weight, gain, *refs):
    ranges = (
        (Q_AT, HEADS * HEAD),
        (K_AT, HEADS * HEAD),
        (V_AT, MIX),
        (G_AT, GATES),
        (G_AT + 2 * GATES, GATES),
    )
    total = summed(refs, slice(None))
    for number, (at, size) in enumerate(ranges):
        yield number, 0, 0, total[:, at : at + size]
    along = jnp.sum(total * weight[:, :].astype(jnp.float32), axis=1, keepdims=True)
    yield len(ranges), 0, 0, along / gain[:, :]


def whole(kernel, outs, *operands, flops=0, scratch=()):
    outs = [jax.ShapeDtypeStruct(shape, dtype) for shape, dtype in outs]
    size = sum(a.size * a.dtype.itemsize for a in list(operands) + outs)
    return pl.pallas_call(
        kernel,
        out_shape=outs,
        scratch_shapes=list(scratch),
        compiler_params=pltpu.CompilerParams(vmem_limit_bytes=VMEM),
        cost_estimate=BRIEF,
    )(*operands)


def body(
    tokens,
    segments,
    value_experts,
    out_experts,
    norm_gain,
    w_query,
    w_key,
    w_value,
    w_vgate,
    w_ogate,
    w_out,
    ffn_gain,
    w_up,
    w_down,
    cotangent,
):
    grid = Grid()
    first, second = grid.plane_a, grid.plane_b
    row_orders = jnp.stack(
        [grid.order([first, second, *grid.rest]), grid.order([second, first, *grid.rest])]
    )
    unit_orders = jnp.stack(
        [
            grid.order([grid.rest[0], first, second, *grid.rest[1:]]),
            grid.order([grid.rest[0], second, first, *grid.rest[1:]]),
        ]
    )
    micro, _, block, width = tokens.shape
    rows = micro * block
    hidden_units = w_up.shape[1]
    place = lax.axis_index("seq")
    own_segs = lax.dynamic_slice_in_dim(segments, place * block, block, 2)[:, 0]
    prior_start = jnp.maximum(place - 1, 0) * block
    prior_segs = jnp.where(
        place > 0, lax.dynamic_slice_in_dim(segments, prior_start, block, 2)[:, 0], -1
    )
    gain_one = norm_gain.astype(jnp.float32)[None]
    gain_two = ffn_gain.astype(jnp.float32)[None]
    column = np.arange(-(-MIX // LANES) * LANES)
    head_column = np.arange(WIDE)
    keys = np.full((4, column.size), -1, np.int32)
    keys[0, :MIX] = (column // (EXPERTS * HEAD) * LANES + column % HEAD)[:MIX]
    keys[1, :MIX] = (column // HEAD)[:MIX]
    keys[2, : HEADS * HEAD] = (head_column // HEAD * LANES + head_column % HEAD)[: HEADS * HEAD]
    keys[3, HEADS * HEAD : 2 * HEADS * HEAD] = keys[2, : HEADS * HEAD]
    keys = jnp.asarray(keys)
    lane = np.arange(4 * GATES)
    slots = np.zeros((2 * 16 + 8, LANES), np.float32)
    source = 2 * (lane % GATES // EXPERTS) + 2 * HEADS * (lane // (2 * GATES))
    slots[source, lane] = 1
    slots[16 + source + 1, lane] = 1
    slots[32] = -1
    slots[32, : 4 * GATES] = lane % EXPERTS
    slots = jnp.asarray(slots, jnp.bfloat16)
    picks = jnp.concatenate(
        [value_experts.reshape(rows, 2 * HEADS), out_experts.reshape(rows, 2 * HEADS)], 1
    ).astype(jnp.bfloat16)
    w_gates = jnp.concatenate([w_vgate.T, w_vgate.T, w_ogate.T, w_ogate.T], 0)
    w_gates = jnp.pad(w_gates, ((0, LANES - w_gates.shape[0]), (0, 0)))
    w_query, w_key, w_value = w_query.T, w_key.T, w_value.T
    share = width // grid.count

    def own_rows(array):
        return lax.dynamic_slice_in_dim(array, grid.me * share, share, 0)

    def own_columns(array):
        return lax.dynamic_slice_in_dim(array, grid.me * share, share, 1).T

    own_up = own_rows(w_up)
    own_gain_one = own_rows(norm_gain.astype(jnp.float32))[:, None]
    own_gain_two = own_rows(ffn_gain.astype(jnp.float32))[:, None]
    own_value = jnp.pad(own_columns(w_value), ((0, 0), (0, -MIX % LANES)))
    own_in = jnp.concatenate([own_columns(w_query), own_columns(w_key)], 1)
    own_gates = jnp.pad(own_columns(w_gates[: 3 * GATES]), ((0, 0), (0, LANES - 3 * GATES)))
    own_in = jnp.concatenate([own_value, own_in, own_gates], 1)
    seg_cols = own_segs.reshape(rows, 1)
    seg_rows = jnp.stack([prior_segs, own_segs], 1)

    field = tokens.reshape(rows, width)
    d_down = cotangent.reshape(rows, width)
    low, full = jnp.bfloat16, jnp.float32
    normed, gates, parts, experts, kv = whole(
        value_kernel,
        [
            ((rows, width), low),
            ((rows, LANES), full),
            ((rows, LANES), low),
            ((rows, MIX), full),
            ((2, rows, WIDE), low),
        ],
        field, gain_one, keys, slots, picks, w_gates, w_key, w_value,
        flops=2 * rows * MIX * (width + LANES + 2 * WIDE),
    )
    memory = passed_along(kv, "seq", 1)

    def paired(value):
        return value, grid.swap(value, grid.core)

    down_pair, normed_pair, parts_pair = paired(d_down), paired(normed), paired(parts)
    step = 512
    fixed = pl.BlockSpec((rows, width), lambda j: (0, 0))
    across = pl.BlockSpec((rows, step), lambda j: (0, j))
    up_block = pl.BlockSpec((width, step), lambda j: (0, j))
    down_block = pl.BlockSpec((step, width), lambda j: (j, 0))
    row_block = pl.BlockSpec((1, width), lambda j: (0, 0))

    def stepped(kernel, in_specs, out_specs, outs, operands, products, scratch=0):
        return pl.pallas_call(
            kernel,
            grid=(hidden_units // step,),
            in_specs=in_specs,
            out_specs=out_specs,
            out_shape=[jax.ShapeDtypeStruct(shape, dtype) for shape, dtype in outs],
            scratch_shapes=[pltpu.VMEM((rows, width), full)] * scratch,
            compiler_params=pltpu.CompilerParams(vmem_limit_bytes=VMEM),
            cost_estimate=BRIEF,
        )(*operands)

    query, back = stepped(
        query_kernel,
        [
            fixed,
            pl.BlockSpec(keys.shape, lambda j: (0, 0)),
            pl.BlockSpec(w_query.shape, lambda j: (0, 0)),
            fixed,
            down_block,
        ],
        [pl.BlockSpec((rows, WIDE), lambda j: (0, 0)), across],
        [((rows, WIDE), low), ((rows, hidden_units), full)],
        (normed, keys, w_query, after(d_down, kv), w_down),
        1,
    )
    mixed_columns = -(-MIX // 256) * 256
    attended, totals, mixed, hidden, normed_two = whole(
        functools.partial(attention_kernel, block),
        [
            ((rows, WIDE), low),
            ((rows, LANES), full),
            ((rows, mixed_columns), low),
            ((rows, width), full),
            ((rows, width), low),
        ],
        query, kv, memory, parts, after(field, normed_pair[1], parts_pair[1], down_pair[1]), gain_two,
        keys, seg_cols, seg_rows, w_out,
        flops=2 * rows * MIX * (width + LANES + WIDE) + 8 * rows * block * WIDE,
    )
    mixed_pair, normed_two_pair = paired(mixed), paired(normed_two)
    units = hidden_units // grid.count
    side = (grid.me // grid.core) % 2
    upper, d_pre, theirs = pl.pallas_call(
        units_up_kernel,
        grid_spec=pltpu.PrefetchScalarGridSpec(
            num_scalar_prefetch=1,
            grid=(hidden_units // step,),
            in_specs=[
                pl.BlockSpec((rows, width), lambda j, _: (0, 0)),
                pl.BlockSpec((width, step), lambda j, _: (0, j)),
                pl.BlockSpec((rows, step), lambda j, _: (0, j)),
            ],
            out_specs=[
                pl.BlockSpec((rows, step), lambda j, _: (0, j)),
                pl.BlockSpec((rows, step), lambda j, _: (0, j)),
                pl.BlockSpec((rows, step // 2), lambda j, _: (0, j)),
            ],
        ),
        out_shape=[
            jax.ShapeDtypeStruct((rows, hidden_units), low),
            jax.ShapeDtypeStruct((rows, hidden_units), low),
            jax.ShapeDtypeStruct((rows, hidden_units // 2), low),
        ],
        compiler_params=pltpu.CompilerParams(vmem_limit_bytes=VMEM),
        cost_estimate=BRIEF,
    )(side.reshape(1), normed_two, w_up, back)

    source = (row_orders[:, :, None] * share + jnp.arange(share, dtype=jnp.int32)).reshape(2, -1, 1)
    within = unit_orders // (2 * grid.core) * grid.core + unit_orders % grid.core
    if units == 128 and grid.core * units * 2 == step:
        unit_blocks = jnp.stack([unit_orders, within])
        upper_pair = upper, grid.swap(theirs, grid.core)
    else:
        place = jnp.arange(units, dtype=jnp.int32)
        half_shards = jnp.arange(grid.count // 2, dtype=jnp.int32)
        half_shards = half_shards // grid.core * (2 * grid.core) + half_shards % grid.core
        half_shards = half_shards + (1 - side) * grid.core
        theirs = upper[:, (half_shards[:, None] * units + place).reshape(-1)]
        came = grid.swap(theirs, grid.core)
        lists = [(o[:, :, None] * units + place).reshape(-1) for o in (unit_orders, within)]
        upper_pair = upper[:, lists[0]], came[:, lists[1]]
        blocks = jnp.arange(hidden_units // 128, dtype=jnp.int32).reshape(2, -1)
        unit_blocks = jnp.stack([blocks, blocks])
    pre_pair = paired(d_pre)

    def plane(parts, one, two):
        return parts[1], grid.swap(parts[0], one), parts[3], grid.swap(parts[2], two)

    aligned = share % 16 == 0

    def stage(generate, rows, widths, gate, *operands):
        outs = [((rows, size), low) for size in widths]
        return pieced(generate, outs, aligned, after(operands[0], *gate), *operands[1:])

    def down_rest(pair, masks, gate):
        sent = None
        for mask in masks:
            layout, column = [], 0
            for number in range(len(pair) // 2):
                layout.append((number, 0, pair[2 * number].shape[1], column))
                column += pair[2 * number].shape[1]
            sent, own = stage(
                functools.partial(laid_out, layout), pair[0].shape[0] // 2, [column] * 2, gate, *pair
            )
            pair = own, grid.swap(sent, mask)
            gate = (sent,)
        return pair, sent

    d_hidden, d_branch = stepped(
        units_back_kernel,
        [across, up_block, fixed, fixed, row_block],
        [fixed, fixed],
        [((rows, width), full), ((rows, width), low)],
        (d_pre, w_up, hidden, d_down, gain_two),
        1,
        1,
    )
    branch_pair = paired(d_branch)
    down_sent, down_kept = gradient_units(
        unit_blocks, upper_pair, (after(d_down, d_branch), down_pair[1])
    )
    down_came = grid.swap(down_sent, grid.rest[0])
    up_parts = gradient_rows(
        source, (after(normed_two, down_sent), normed_two_pair[1]), pre_pair, 2
    )
    up_one = plane(up_parts, first, second)
    out_parts = gradient_rows(source, branch_pair, (after(mixed, *up_parts), mixed_pair[1]), 1)
    out_one = plane(out_parts, first, second)
    queries_keys, values_gates = whole(
        functools.partial(attention_back_kernel, block),
        [((rows, 2 * HEADS * HEAD), low), ((rows, WIDE + LANES), low)],
        after(d_branch, *out_parts), w_out, gates, parts, attended, query, kv, memory, totals,
        experts, keys, seg_cols, seg_rows,
        scratch=[pltpu.VMEM((rows, WIDE), low)] * 3,
    )
    queries_keys_pair, values_gates_pair = paired(queries_keys), paired(values_gates)

    columns = up_parts[0].shape[1], out_parts[0].shape[1]
    tall = up_parts[0].shape[0] // 2
    beside = down_kept.size // 4 // tall
    wide_two = stage(
        joined_halves, tall, [sum(columns) + beside] * 4, (queries_keys,),
        *up_one[:2], *out_one[:2], *up_one[2:], *out_one[2:], down_kept, down_came,
    )
    wide_one = plane(wide_two, second, first)
    half = (share * grid.count // 4, IN_COLUMNS // 2)
    in_parts = whole(
        inputs_kernel,
        [(half, low)] * 4,
        source, after(normed, *wide_two), normed_pair[1], *queries_keys_pair, *values_gates_pair,
        *parts_pair, keys,
        scratch=[pltpu.VMEM((2 * half[0], 2 * rows), low)],
    )
    in_one = plane(in_parts, first, second)
    (result,) = stepped(
        result_kernel,
        [across, down_block, fixed],
        [fixed],
        [((rows, width), low)],
        (upper, w_down, after(hidden, *in_parts)),
        1,
        1,
    )
    layout = [
        (0, 0, columns[0], 0),
        (1, 0, columns[0], columns[0]),
        (0, columns[0], columns[1], 2 * columns[0]),
        (1, columns[0], columns[1], 2 * columns[0] + columns[1]),
    ]
    wide_sent, wide_own = stage(
        functools.partial(laid_out, layout), wide_one[0].shape[0] // 2, [2 * sum(columns)] * 2,
        (result,), *wide_one,
    )
    wide_pair = wide_own, grid.swap(wide_sent, grid.rest[0])
    down_three = stage(
        functools.partial(blocks_halves, sum(columns), width // 2), beside * tall // width,
        [width // 2] * 4, (wide_sent,), *wide_one,
    )
    down_pairs = plane(down_three, second, first)
    in_two = stage(
        paired_halves, half[0] // 2, [half[1]] * 4, down_three, *in_one
    )
    in_pairs = plane(in_two, second, first)
    wide_pair, wide_sent = down_rest(wide_pair, grid.rest[1:], in_two)
    down_pair, down_sent = down_rest(down_pairs, grid.rest[1:], (wide_sent,))
    (input_grad,) = whole(
        inputs_back_kernel,
        [((rows, width), low)],
        queries_keys, values_gates, parts, keys, field, after(d_hidden, down_sent), gain_one,
        w_gates, w_key, w_value, w_query,
        scratch=[pltpu.VMEM((2 * HEADS * HEAD, width), low)],
    )
    in_pair, in_sent = down_rest(in_pairs, grid.rest, (input_grad,))
    grad_down, grad_up, grad_gain_two, grad_out_w = pieced(
        most_done,
        [
            ((units, width), full),
            ((share, hidden_units), full),
            ((share, 1), full),
            ((share, MIX), full),
        ],
        aligned, after(own_up, in_sent), own_gain_two, *down_pair, *wide_pair,
    )
    sizes = (HEADS * HEAD, HEADS * HEAD, MIX, GATES, GATES, 1)
    *grads, grad_gain_one = pieced(
        in_done,
        [((share, size), full) for size in sizes],
        aligned, after(own_in, grad_down), own_gain_one, *in_pair,
    )
    return (
        result.reshape(tokens.shape),
        input_grad.reshape(tokens.shape),
        grad_gain_one[:, 0],
        *grads,
        grad_out_w.T,
        grad_gain_two[:, 0],
        grad_up,
        grad_down,
    )


def solution(mesh):
    both = ("seq", "batch")
    stream = P(None, "batch", "seq", None)
    picks = P(None, "batch", "seq", None, None)
    return jax.shard_map(
        body,
        mesh=mesh,
        in_specs=(stream, P(None, "batch", None), picks, picks) + (P(),) * 10 + (stream,),
        out_specs=(
            stream,
            stream,
            P(both),
            P(both, None),
            P(both, None),
            P(both, None),
            P(both, None),
            P(both, None),
            P(None, both),
            P(both),
            P(both, None),
            P(both, None),
        ),
        check_vma=False,
    )
```

```python
import functools
import math

import jax
import jax.numpy as jnp
import numpy as np
from jax import lax
from jax.experimental import pallas as pl
from jax.experimental.pallas import tpu as pltpu
from jax.sharding import PartitionSpec as P

HEADS = 4
HEAD = 112
EXPERTS = 5

eps = 1e-06
VMEM = 60 << 20
FULL = 60 << 20
GRADIENT = 60 << 20
HIDDEN = 4096
BRIEF = pl.CostEstimate(flops=1024, bytes_accessed=1024, transcendentals=0)


def product(left, right):
    return jnp.dot(left, right, preferred_element_type=jnp.float32)


def product_tn(left, right):
    return lax.dot_general(
        left, right, (((0,), (0,)), ((), ())), preferred_element_type=jnp.float32
    )


def product_nt(left, right):
    return lax.dot_general(
        left, right, (((1,), (1,)), ((), ())), preferred_element_type=jnp.float32
    )


def passed_along(value, axis, steps):
    count = lax.axis_size(axis)
    initial, last = (max(0, -steps), min(count, count - steps))
    return lax.ppermute(value, axis, [(source, source + steps) for source in range(initial, last)])


class Grid:
    def __init__(self):
        self.seq, self.batch = lax.axis_size("seq"), lax.axis_size("batch")
        self.count = self.seq * self.batch
        low = self.batch.bit_length() - 1
        self.core, self.plane_a, self.plane_b = 1 << low, 1, 2 << low
        taken = self.core | self.plane_a | self.plane_b
        self.rest = [1 << at for at in range(self.count.bit_length() - 1) if not (1 << at) & taken]
        self.me = lax.axis_index("seq") * self.batch + lax.axis_index("batch")

    def swap(self, value, mask):
        both = ("seq", "batch")
        return lax.ppermute(value, both, [(i, i ^ mask) for i in range(self.count)])

    def order(self, bits, base=0):
        masks = [base]
        for bit in bits:
            masks = [mask | own for mask in masks for own in (bit, 0)]
        return self.me ^ jnp.array(masks, jnp.int32)


def after(value, *others):
    return lax.optimization_barrier((value,) + others)[0]


def in_order(order, total):
    if order == 0:
        return total
    size = total.shape[0] // 4
    parts = [total[i * size : (i + 1) * size] for i in (0, 2, 1, 3)]
    return jnp.concatenate(parts, 0)


def turn(src, parts, turned):
    at = 0
    for part in parts:
        shape = turned.shape[0], part.shape[1]
        picks = iota(shape, 0) if shape[0] == shape[1] else src
        picked = product_nt(ones_where(picks == iota(shape, 1)), part[...]).astype(jnp.bfloat16)
        turned[:, at : at + part.shape[0]] = picked
        at += part.shape[0]


def units_kernel(order_ref, left, left_came, right, right_came, *outs):
    order, at = pl.program_id(0), pl.program_id(1)
    blocks = order_ref.shape[2] // 2

    def chosen(number, ref):
        return jnp.concatenate(
            [
                ref[:, pl.ds(pl.multiple_of(order_ref[number, order, at * blocks + i] * 128, 128), 128)]
                for i in range(blocks)
            ],
            1,
        )

    total = product_tn(chosen(0, left), right[...]) + product_tn(chosen(1, left_came), right_came[...])
    total = total.astype(jnp.bfloat16)
    for number in range(2):

        @pl.when(at == number)
        def _():
            outs[number][...] = total


def gradient_units(order, left, right):
    tokens = left[0].shape[0]
    rows, columns = order.shape[2] * 128, right[0].shape[1] // 2
    moving = pl.BlockSpec((tokens, columns), lambda o, j, *_: (0, o))
    in_specs = [pl.BlockSpec(part.shape, lambda o, j, *_: (0, 0)) for part in left] + [moving] * 2
    return pl.pallas_call(
        units_kernel,
        grid_spec=pltpu.PrefetchScalarGridSpec(
            num_scalar_prefetch=1,
            grid=(2, 2),
            in_specs=in_specs,
            out_specs=[pl.BlockSpec((rows // 2, columns), lambda o, j, *_: (0, o))] * 2,
        ),
        out_shape=[jax.ShapeDtypeStruct((rows // 2, 2 * columns), jnp.bfloat16)] * 2,
        compiler_params=pltpu.CompilerParams(vmem_limit_bytes=GRADIENT),
        cost_estimate=BRIEF,
    )(order, *left, *right)


def product_low(value, right):
    return product_nt(value.astype(jnp.bfloat16), right)


def ones_where(condition):
    return jnp.where(condition, 1.0, 0.0).astype(jnp.bfloat16)


def iota(shape, dimension):
    return lax.broadcasted_iota(jnp.int32, shape, dimension)


LANES = 128
WIDE = HEADS * LANES
MIX = HEADS * EXPERTS * HEAD
GATES = HEADS * EXPERTS
CHUNK = 512


def pieces_of(total):
    return [(at, min(CHUNK, total - at)) for at in range(0, total, CHUNK)]


def spread_block(keys_ref, at, size):
    return ones_where(iota((WIDE, size), 0) == keys_ref[0:1, at : at + size])


def expert_block(keys_ref, at, size, start, twice):
    lane, own = iota((LANES, size), 0), keys_ref[1:2, at : at + size]
    hit = lane == own + start
    if twice:
        hit = hit | (lane == own + (start + GATES))
    return ones_where(hit)


def gate_parts(gates):
    lane = iota(gates.shape, 1)
    high = gates.astype(jnp.bfloat16).astype(jnp.float32)
    low = ((lane >= GATES) & (lane < 2 * GATES)) | (lane >= 3 * GATES)
    return jnp.where(low, gates - high, high).astype(jnp.bfloat16)


def pad_heads(keys_ref, size):
    return ones_where(iota((WIDE, size), 0) == keys_ref[2:3, 0:size])


def normalise(field, gain):
    factor = lax.rsqrt(jnp.mean(field * field, axis=-1, keepdims=True) + eps)
    return field * factor * gain


def normalise_back(field, gain, grad):
    factor = lax.rsqrt(jnp.mean(field * field, axis=-1, keepdims=True) + eps)
    weighted = grad * gain
    field_grad = factor * weighted - field * factor**3 * jnp.mean(
        weighted * field, axis=-1, keepdims=True
    )
    return field_grad


def value_kernel(
    tokens, gain, keys, slots, picks, w_gates, w_key, w_value,
    normed_out, gates_out, parts_out, experts, kv,
):
    normed = normalise(tokens[...].astype(jnp.float32), gain[...]).astype(jnp.bfloat16)
    normed_out[...] = normed
    own_key = product_nt(normed, w_key[...]).astype(jnp.bfloat16)
    kv[0] = product_nt(own_key, pad_heads(keys, own_key.shape[1])).astype(jnp.bfloat16)
    logits = product_nt(normed, w_gates[...])
    number = slots[2 * picks.shape[1] : 2 * picks.shape[1] + 1, :].astype(jnp.float32)
    count = picks.shape[1]
    one = product(picks[...], slots[0:count, :])
    two = product(picks[...], slots[count : 2 * count, :])
    gates = jnp.where((one == number) | (two == number), jax.nn.sigmoid(logits), 0.0)
    gates_out[...] = gates
    parts = gate_parts(gates)
    parts_out[...] = parts
    total = jnp.zeros((normed.shape[0], WIDE), jnp.float32)
    for at, size in pieces_of(MIX):
        own = product_nt(normed, w_value[at : at + size, :])
        experts[:, at : at + size] = own.astype(jnp.bfloat16)
        weighted = own * product(parts, expert_block(keys, at, size, 0, True))
        total += product_low(weighted, spread_block(keys, at, size))
    kv[1] = total.astype(jnp.bfloat16)


def query_kernel(normed, keys, w_query, query):
    own = product_nt(normed[...], w_query[...]).astype(jnp.bfloat16)
    query[...] = product_nt(own, pad_heads(keys, own.shape[1])).astype(jnp.bfloat16)


def masks(seg_cols, seg_rows, at, block):
    own = seg_cols[pl.ds(at * block, block), :]
    rows = seg_rows[at]
    before = own == rows[0:1]
    here = (own == rows[1:2]) & (iota((block, block), 0) >= iota((block, block), 1))
    return before, here


def scores(query, key, allowed):
    return jnp.where(allowed, product_nt(query, key) * HEAD ** (-0.5), -1e30)


def attention_kernel(
    block, query, own, memory, parts_in, tokens, gain, keys, seg_cols, seg_rows, w_out,
    attended, totals, mixed, hidden, normed,
):
    micro = query.shape[0] // block

    @pl.loop(0, micro)
    def _(at):
        before, here = masks(seg_cols, seg_rows, at, block)
        rows = pl.ds(at * block, block)
        lane = iota((block, LANES), 1)
        tops = jnp.zeros((block, LANES), jnp.float32)
        for head in range(HEADS):
            cols = slice(head * LANES, (head + 1) * LANES)
            q = query[rows, cols]
            s_before = scores(q, memory[0, rows, cols], before)
            s_here = scores(q, own[0, rows, cols], here)
            top = jnp.maximum(
                jnp.max(s_before, axis=-1, keepdims=True), jnp.max(s_here, axis=-1, keepdims=True)
            )
            e_before, e_here = jnp.exp(s_before - top), jnp.exp(s_here - top)
            total = jnp.sum(e_before, axis=-1, keepdims=True) + jnp.sum(
                e_here, axis=-1, keepdims=True
            )
            share = 1.0 / total
            seen = product((e_before * share).astype(jnp.bfloat16), memory[1, rows, cols])
            seen += product((e_here * share).astype(jnp.bfloat16), own[1, rows, cols])
            attended[rows, cols] = seen.astype(jnp.bfloat16)
            tops = jnp.where(lane == head, top + jnp.log(total), tops)
        totals[rows, :] = tops

    parts = parts_in[...]
    seen = attended[...]
    total = tokens[...].astype(jnp.float32)
    for at, size in pieces_of(MIX):
        spread = product(seen, spread_block(keys, at, size))
        weight = product(parts, expert_block(keys, at, size, 2 * GATES, True))
        piece = (spread * weight).astype(jnp.bfloat16)
        mixed[:, at : at + size] = piece
        total += product(piece, w_out[at : at + size, :])
    mixed[:, MIX:] = jnp.zeros((mixed.shape[0], mixed.shape[1] - MIX), jnp.bfloat16)
    hidden[...] = total
    normed[...] = normalise(total, gain[...]).astype(jnp.bfloat16)


def units_up_kernel(group, side, normed, w_up, d_down, w_down, upper, d_pre, theirs):
    pre = product(normed[...], w_up[...])
    back = product_nt(d_down[...], w_down[...])
    cdf = 0.5 * (1.0 + lax.erf(pre * (1.0 / math.sqrt(2.0))))
    high = (pre * cdf).astype(jnp.bfloat16)
    upper[...] = high
    slope = cdf + pre * (jnp.exp(-0.5 * pre * pre) * (1.0 / math.sqrt(2.0 * math.pi)))
    d_pre[...] = (back * slope).astype(jnp.bfloat16)
    for number in range(2):

        @pl.when(side[0] == number)
        def _():
            for at in range(0, high.shape[1], 2 * group):
                start = at + (1 - number) * group
                theirs[:, at // 2 : at // 2 + group] = high[:, start : start + group]


def units_back_kernel(
    d_pre, w_up, hidden, d_down, gain, src, d_hidden, d_branch, theirs, total
):
    at = pl.program_id(0)
    back = product_nt(d_pre[...], w_up[...])

    @pl.when(at == 0)
    def _():
        total[...] = back

    @pl.when(at > 0)
    def _():
        total[...] += back

    @pl.when(at == pl.num_programs(0) - 1)
    def _():
        grad = normalise_back(hidden[...], gain[...], total[...])
        grad = d_down[...].astype(jnp.float32) + grad
        d_hidden[...] = grad
        branch = grad.astype(jnp.bfloat16)
        d_branch[...] = branch
        shape = src.shape[0], branch.shape[1]
        picks = ones_where(src[...] == iota(shape, 1))
        theirs[...] = product_nt(branch, picks).astype(jnp.bfloat16)


def result_kernel(upper, w_down, hidden, result, total):
    at = pl.program_id(0)
    forth = product(upper[...], w_down[...])

    @pl.when(at == 0)
    def _():
        total[...] = hidden[...] + forth

    @pl.when(at > 0)
    def _():
        total[...] += forth

    @pl.when(at == pl.num_programs(0) - 1)
    def _():
        result[...] = total[...].astype(jnp.bfloat16)


def attention_back_kernel(
    block, d_branch, w_out, gates, parts_in, attended, query, own, memory, totals, experts, keys,
    seg_cols, seg_rows, queries_keys, values_gates,
    d_seen, d_query, d_key,
):
    branch, seen, gate, parts = d_branch[...], attended[...], gates[...], parts_in[...]
    to_seen = jnp.zeros((branch.shape[0], WIDE), jnp.float32)
    to_gate = jnp.zeros((branch.shape[0], LANES), jnp.float32)
    for at, size in pieces_of(MIX):
        d_mixed = product_nt(branch, w_out[at : at + size, :])
        spread = spread_block(keys, at, size)
        weight = product(parts, expert_block(keys, at, size, 2 * GATES, True))
        to_seen += product_low(d_mixed * weight, spread)
        to_gate += product_low(
            d_mixed * product(seen, spread), expert_block(keys, at, size, 2 * GATES, False)
        )
    d_seen[...] = to_seen.astype(jnp.bfloat16)
    micro = query.shape[0] // block

    @pl.loop(0, micro)
    def _(at):
        before, here = masks(seg_cols, seg_rows, at, block)
        rows = pl.ds(at * block, block)
        tops = totals[rows, :]
        for head in range(HEADS):
            cols = slice(head * LANES, (head + 1) * LANES)
            q, grad = query[rows, cols], d_seen[rows, cols]
            k_before, k_here = memory[0, rows, cols], own[0, rows, cols]
            top = tops[:, head : head + 1]
            p_before = jnp.exp(scores(q, k_before, before) - top)
            p_here = jnp.exp(scores(q, k_here, here) - top)
            g_before = product_nt(grad, memory[1, rows, cols])
            g_here = product_nt(grad, own[1, rows, cols])
            delta = jnp.sum(p_before * g_before, axis=-1, keepdims=True) + jnp.sum(
                p_here * g_here, axis=-1, keepdims=True
            )
            s_before = (p_before * (g_before - delta)).astype(jnp.bfloat16)
            s_here = (p_here * (g_here - delta)).astype(jnp.bfloat16)
            to_query = product(s_before, k_before) + product(s_here, k_here)
            d_query[rows, cols] = (to_query * HEAD ** (-0.5)).astype(jnp.bfloat16)
            to_key = product_tn(s_here, q) * HEAD ** (-0.5)
            d_key[rows, cols] = to_key.astype(jnp.bfloat16)
            to_value = product_tn(p_here.astype(jnp.bfloat16), grad)
            values_gates[rows, cols] = to_value.astype(jnp.bfloat16)

    d_value = values_gates[:, :WIDE]
    for at, size in pieces_of(MIX):
        to_gate += product_low(
            product(d_value, spread_block(keys, at, size)) * experts[:, at : at + size],
            expert_block(keys, at, size, 0, False),
        )
    values_gates[:, WIDE:] = (to_gate * gate * (1.0 - gate)).astype(jnp.bfloat16)
    both = (WIDE, 2 * HEADS * HEAD)
    from_query = ones_where(iota(both, 0) == keys[2:3, : both[1]])
    from_key = ones_where(iota(both, 0) == keys[3:4, : both[1]])
    total = product(d_query[...], from_query) + product(d_key[...], from_key)
    queries_keys[...] = total.astype(jnp.bfloat16)


V_AT = 0
Q_AT = -(-MIX // LANES) * LANES
K_AT = Q_AT + HEADS * HEAD
G_AT = K_AT + HEADS * HEAD
IN_COLUMNS = G_AT + LANES


def d_experts(values_gates, parts, keys, at, size):
    spread = product(values_gates[:, :WIDE], spread_block(keys, at, size))
    weight = product(parts[...], expert_block(keys, at, size, 0, True))
    return (spread * weight).astype(jnp.bfloat16)


def put_into(refs, half):
    def put(number, at, total):
        total = in_order(number, total.astype(jnp.bfloat16))
        keep = total.shape[0] // 2
        columns = slice(at - number * half, at - number * half + total.shape[1])
        refs[2 * number][:, columns] = total[:keep]
        refs[2 * number + 1][:, columns] = total[keep:]

    return put


def halves_of(total, half):
    for number in range(2):
        at, stop = number * half, min(total, (number + 1) * half)
        while at < stop:
            size = min(CHUNK, stop - at)
            yield number, at, size
            at += size


def wide_kernel(
    src, left, left_came, right, right_came, branch, branch_came, mixed, seen_came, parts_came, keys,
    *refs,
):
    turned, turned_branch = refs[-2:]
    tokens = left.shape[0]
    order = pl.program_id(0)
    ups, outs = right.shape[1], mixed.shape[1]

    @pl.when(order == 0)
    def _():
        turn(src[...], (left, left_came), turned)
        turn(src[...], (branch, branch_came), turned_branch)

    for number in range(2):

        @pl.when(order == number)
        def _():
            def put(at, total):
                total = in_order(number, total.astype(jnp.bfloat16))
                keep = total.shape[0] // 2
                columns = slice(at, at + total.shape[1])
                refs[2 * number][:, columns] = total[:keep]
                refs[2 * number + 1][:, columns] = total[keep:]

            for at in range(0, ups, 2 * CHUNK):
                columns = slice(at, at + 2 * CHUNK)
                total = product(turned[:, :tokens], right[:, columns])
                put(at, total + product(turned[:, tokens:], right_came[:, columns]))
            at, stop = 0, min(outs, MIX - number * outs)
            while at < stop:
                size = min(CHUNK, stop - at)
                start = number * outs + at
                spread = product(seen_came[...], spread_block(keys, start, size))
                weight = product(parts_came[...], expert_block(keys, start, size, 2 * GATES, True))
                came = (spread * weight).astype(jnp.bfloat16)
                total = product(turned_branch[:, :tokens], mixed[:, at : at + size])
                put(ups + at, total + product(turned_branch[:, tokens:], came))
                at += size
            if at < outs:
                put(ups + at, jnp.zeros((turned.shape[0], outs - at), jnp.float32))


def gradient_wide(src, left, right, branch, mixed, seen_came, parts_came, keys):
    tokens, rows = left[0].shape[0], src.shape[0]
    ups, outs = right[0].shape[1] // 2, mixed.shape[1] // 2
    operands = (src, *left, *right, *branch, mixed, seen_came, parts_came, keys)

    def fixed(array):
        return pl.BlockSpec(array.shape, lambda o: (0, 0))

    specs = [fixed(array) for array in operands]
    specs[3] = specs[4] = pl.BlockSpec((tokens, ups), lambda o: (0, o))
    specs[7] = pl.BlockSpec((tokens, outs), lambda o: (0, o))
    shape = (rows // 2, ups + outs)
    return pl.pallas_call(
        wide_kernel,
        grid=(2,),
        in_specs=specs,
        out_specs=[pl.BlockSpec(shape, lambda o: (0, 0))] * 4,
        out_shape=[jax.ShapeDtypeStruct(shape, jnp.bfloat16)] * 4,
        scratch_shapes=[pltpu.VMEM((rows, 2 * tokens), jnp.bfloat16)] * 2,
        compiler_params=pltpu.CompilerParams(vmem_limit_bytes=GRADIENT),
        cost_estimate=BRIEF,
    )(*operands)


def inputs_kernel(
    src, left, left_came, queries_keys, queries_keys_came, values_gates, values_gates_came,
    parts, parts_came, keys, *refs,
):
    turned = refs[-1]
    half = IN_COLUMNS // 2
    tokens = left.shape[0]
    put = put_into(refs, half)

    def times(one, two):
        return product(turned[:, :tokens], one) + product(turned[:, tokens:], two)

    turn(src[...], (left, left_came), turned)
    for number, at, size in halves_of(MIX, half):
        one = d_experts(values_gates, parts, keys, at, size)
        two = d_experts(values_gates_came, parts_came, keys, at, size)
        put(number, at, times(one, two))
    put(1, MIX, jnp.zeros((turned.shape[0], Q_AT - MIX), jnp.float32))
    for at in range(0, 2 * HEADS * HEAD, CHUNK):
        columns = slice(at, min(at + CHUNK, 2 * HEADS * HEAD))
        put(1, Q_AT + at, times(queries_keys[:, columns], queries_keys_came[:, columns]))
    put(1, G_AT, times(values_gates[:, WIDE:], values_gates_came[:, WIDE:]))


def inputs_back_kernel(
    queries_keys, values_gates, parts, keys, tokens, d_hidden, gain, w_gates, w_key, w_value,
    w_query, places, input_grad, own_in, w_both,
):
    size = HEADS * HEAD
    w_both[:size, :] = w_query[...]
    w_both[size:, :] = w_key[...]
    total = product(values_gates[:, WIDE:], w_gates[...])
    total += product(queries_keys[...], w_both[...])
    for at, size in pieces_of(MIX):
        total += product(d_experts(values_gates, parts, keys, at, size), w_value[at : at + size, :])
    picks = ones_where(places[...] == iota((places.shape[0], tokens.shape[1]), 1))
    for at, weight in ((V_AT, w_value), (Q_AT, w_both), (G_AT, w_gates)):
        own = product_nt(picks, weight[...]).astype(jnp.bfloat16)
        own_in[:, at : at + own.shape[1]] = own
    own_in[:, MIX:Q_AT] = jnp.zeros((places.shape[0], Q_AT - MIX), jnp.bfloat16)
    grad = normalise_back(tokens[...].astype(jnp.float32), gain[...], total)
    input_grad[...] = (d_hidden[...] + grad).astype(jnp.bfloat16)


def pieced(generate, outs, aligned, *operands):
    if not aligned:
        results = [jnp.zeros(shape, dtype) for shape, dtype in outs]
        for number, row, column, value in generate(*operands):
            value = value.astype(results[number].dtype)
            results[number] = lax.dynamic_update_slice(results[number], value, (row, column))
        return results

    def kernel(*refs):
        given, made = refs[: len(operands)], refs[len(operands) :]
        for number, row, column, value in generate(*given):
            rows, columns = slice(row, row + value.shape[0]), slice(column, column + value.shape[1])
            made[number][rows, columns] = value.astype(made[number].dtype)

    return whole(kernel, outs, *operands, grant=FULL)


def summed(pair, rows, columns=slice(None)):
    return sum(part[rows, columns].astype(jnp.float32) for part in pair)


def forked(kept, came):
    columns, rows = kept.shape[1] // 2, kept.shape[0] // 2
    for number in range(2):
        own = slice(number * columns, (number + 1) * columns)
        for half in range(2):
            part = slice(half * rows, (half + 1) * rows)
            yield 2 * number + half, 0, 0, summed((kept, came), part, own)


def paired_halves(*refs):
    for number in range(2):
        column = 0
        own = refs[number * len(refs) // 2 : (number + 1) * len(refs) // 2]
        for pair in zip(own[::2], own[1::2]):
            rows = pair[0].shape[0] // 2
            for half in range(2):
                part = slice(half * rows, (half + 1) * rows)
                yield 2 * number + half, 0, column, summed(pair, part)
            column += pair[0].shape[1]


def laid_out(layout, *refs):
    for number, start, size, column in layout:
        pair = refs[2 * number : 2 * number + 2]
        rows = pair[0].shape[0] // 2
        for half in range(2):
            part = slice(half * rows, (half + 1) * rows)
            yield half, 0, column, summed(pair, part, slice(start, start + size))


def as_row(column):
    size = column.shape[0]
    return jnp.sum(jnp.where(iota((size, size), 0) == iota((size, size), 1), column, 0.0), 0, keepdims=True)


def last_halves(width, wide_size, *refs):
    rows = refs[0].shape[0] // 2
    for half in range(2):
        part = slice(half * rows, (half + 1) * rows)
        yield half, 0, 0, summed(refs[:2], part, slice(0, wide_size))
        if len(refs) == 2:
            blocks = (refs[0].shape[1] - wide_size) // width // 2
            for block in range(blocks):
                at = wide_size + (half * blocks + block) * width
                for low in range(2):
                    value = summed(refs, slice(low * rows, (low + 1) * rows), slice(at, at + width))
                    yield half, 0, wide_size + (2 * block + low) * width, value
            continue
        for number in range(2):
            pair = refs[2 + 2 * number : 4 + 2 * number]
            tall = pair[0].shape[0] // 2
            for block in range(tall // rows):
                at = half * tall + block * rows
                yield half, 0, wide_size + block * width + number * width // 2, summed(
                    pair, slice(at, at + rows)
                )


def most_done(width, wide_size, weight, gain, wide, wide_came):
    rows = wide.shape[0]
    for block in range((wide.shape[1] - wide_size) // width):
        columns = slice(wide_size + block * width, wide_size + (block + 1) * width)
        yield 0, block * rows, 0, summed((wide, wide_came), slice(None), columns)
    along = 0.0
    for at in range(0, HIDDEN, 2 * CHUNK):
        columns = slice(at, at + 2 * CHUNK)
        piece = summed((wide, wide_came), slice(None), columns)
        yield 1, 0, at, piece
        along += jnp.sum(piece * weight[:, columns].astype(jnp.float32), axis=1, keepdims=True)
    yield 2, 0, 0, as_row(along / gain[:, :])
    yield 3, 0, 0, summed((wide, wide_came), slice(None), slice(HIDDEN, HIDDEN + MIX))


def in_done(weight, gain, *refs):
    total = summed(refs, slice(None))
    for number, (at, size) in enumerate(((Q_AT, HEADS * HEAD), (K_AT, HEADS * HEAD), (V_AT, MIX))):
        yield number, 0, 0, total[:, at : at + size]
    gates = total[:, G_AT:].T
    yield 3, 0, 0, gates[:GATES]
    yield 4, 0, 0, gates[2 * GATES : 3 * GATES]
    along = jnp.sum(total * weight[:, :].astype(jnp.float32), axis=1, keepdims=True)
    yield 5, 0, 0, as_row(along / gain[:, :])


def whole(kernel, outs, *operands, scratch=(), grant=VMEM):
    outs = [jax.ShapeDtypeStruct(shape, dtype) for shape, dtype in outs]
    size = sum(a.size * a.dtype.itemsize for a in list(operands) + outs)
    return pl.pallas_call(
        kernel,
        out_shape=outs,
        scratch_shapes=list(scratch),
        compiler_params=pltpu.CompilerParams(vmem_limit_bytes=grant),
        cost_estimate=BRIEF,
    )(*operands)


def body(
    tokens,
    segments,
    value_experts,
    out_experts,
    norm_gain,
    w_query,
    w_key,
    w_value,
    w_vgate,
    w_ogate,
    w_out,
    ffn_gain,
    w_up,
    w_down,
    cotangent,
):
    grid = Grid()
    first, second = grid.plane_a, grid.plane_b
    row_order = grid.order([first, second, *grid.rest])
    unit_orders = jnp.stack(
        [
            grid.order([grid.rest[0], first, second, *grid.rest[1:]]),
            grid.order([grid.rest[0], second, first, *grid.rest[1:]]),
        ]
    )
    micro, _, block, width = tokens.shape
    rows = micro * block
    hidden_units = w_up.shape[1]
    place = lax.axis_index("seq")
    own_segs = lax.dynamic_slice_in_dim(segments, place * block, block, 2)[:, 0]
    prior_start = jnp.maximum(place - 1, 0) * block
    prior_segs = jnp.where(
        place > 0, lax.dynamic_slice_in_dim(segments, prior_start, block, 2)[:, 0], -1
    )
    gain_one = norm_gain.astype(jnp.float32)[None]
    gain_two = ffn_gain.astype(jnp.float32)[None]
    column = np.arange(-(-MIX // LANES) * LANES)
    head_column = np.arange(WIDE)
    keys = np.full((4, column.size), -1, np.int32)
    keys[0, :MIX] = (column // (EXPERTS * HEAD) * LANES + column % HEAD)[:MIX]
    keys[1, :MIX] = (column // HEAD)[:MIX]
    keys[2, : HEADS * HEAD] = (head_column // HEAD * LANES + head_column % HEAD)[: HEADS * HEAD]
    keys[3, HEADS * HEAD : 2 * HEADS * HEAD] = keys[2, : HEADS * HEAD]
    keys = jnp.asarray(keys)
    lane = np.arange(4 * GATES)
    slots = np.zeros((2 * 16 + 8, LANES), np.float32)
    source = 2 * (lane % GATES // EXPERTS) + 2 * HEADS * (lane // (2 * GATES))
    slots[source, lane] = 1
    slots[16 + source + 1, lane] = 1
    slots[32] = -1
    slots[32, : 4 * GATES] = lane % EXPERTS
    slots = jnp.asarray(slots, jnp.bfloat16)
    picks = jnp.concatenate(
        [value_experts.reshape(rows, 2 * HEADS), out_experts.reshape(rows, 2 * HEADS)], 1
    ).astype(jnp.bfloat16)
    w_gates = jnp.concatenate([w_vgate.T, w_vgate.T, w_ogate.T, w_ogate.T], 0)
    w_gates = jnp.pad(w_gates, ((0, LANES - w_gates.shape[0]), (0, 0)))
    w_query, w_key, w_value = w_query.T, w_key.T, w_value.T
    share = width // grid.count

    def own_rows(array):
        return lax.dynamic_slice_in_dim(array, grid.me * share, share, 0)

    seg_cols = own_segs.reshape(rows, 1)
    seg_rows = jnp.stack([prior_segs, own_segs], 1)

    field = tokens.reshape(rows, width)
    d_down = cotangent.reshape(rows, width)
    low, full = jnp.bfloat16, jnp.float32
    normed, gates, parts, experts, kv = whole(
        value_kernel,
        [
            ((rows, width), low),
            ((rows, LANES), full),
            ((rows, LANES), low),
            ((rows, MIX), low),
            ((2, rows, WIDE), low),
        ],
        field, gain_one, keys, slots, picks, w_gates, w_key, w_value,
    )
    memory = passed_along(kv, "seq", 1)

    def paired(value):
        return value, grid.swap(value, grid.core)

    down_pair, normed_pair, parts_pair = paired(d_down), paired(normed), paired(parts)
    step = 1024
    fixed = pl.BlockSpec((rows, width), lambda j: (0, 0))
    across = pl.BlockSpec((rows, step), lambda j: (0, j))
    up_block = pl.BlockSpec((width, step), lambda j: (0, j))
    down_block = pl.BlockSpec((step, width), lambda j: (j, 0))
    row_block = pl.BlockSpec((1, width), lambda j: (0, 0))

    def stepped(kernel, in_specs, out_specs, outs, operands, products, scratch=0):
        return pl.pallas_call(
            kernel,
            grid=(hidden_units // step,),
            in_specs=in_specs,
            out_specs=out_specs,
            out_shape=[jax.ShapeDtypeStruct(shape, dtype) for shape, dtype in outs],
            scratch_shapes=[pltpu.VMEM((rows, width), full)] * scratch,
            compiler_params=pltpu.CompilerParams(vmem_limit_bytes=VMEM),
            cost_estimate=BRIEF,
        )(*operands)

    (query,) = whole(query_kernel, [((rows, WIDE), low)], after(normed, kv), keys, w_query)
    mixed_columns = -(-MIX // 256) * 256
    attended, totals, mixed, hidden, normed_two = whole(
        functools.partial(attention_kernel, block),
        [
            ((rows, WIDE), low),
            ((rows, LANES), full),
            ((rows, mixed_columns), low),
            ((rows, width), full),
            ((rows, width), low),
        ],
        query, kv, memory, parts, after(field, normed_pair[1], parts_pair[1], down_pair[1]), gain_two,
        keys, seg_cols, seg_rows, w_out,
    )
    seen_came, normed_two_pair = grid.swap(attended, grid.core), paired(normed_two)
    units = hidden_units // grid.count
    side = (grid.me // grid.core) % 2
    upper, d_pre, theirs = pl.pallas_call(
        functools.partial(units_up_kernel, grid.core * units),
        grid_spec=pltpu.PrefetchScalarGridSpec(
            num_scalar_prefetch=1,
            grid=(hidden_units // step,),
            in_specs=[
                pl.BlockSpec((rows, width), lambda j, _: (0, 0)),
                pl.BlockSpec((width, step), lambda j, _: (0, j)),
                pl.BlockSpec((rows, width), lambda j, _: (0, 0)),
                pl.BlockSpec((step, width), lambda j, _: (j, 0)),
            ],
            out_specs=[
                pl.BlockSpec((rows, step), lambda j, _: (0, j)),
                pl.BlockSpec((rows, step), lambda j, _: (0, j)),
                pl.BlockSpec((rows, step // 2), lambda j, _: (0, j)),
            ],
        ),
        out_shape=[
            jax.ShapeDtypeStruct((rows, hidden_units), low),
            jax.ShapeDtypeStruct((rows, hidden_units), low),
            jax.ShapeDtypeStruct((rows, hidden_units // 2), low),
        ],
        compiler_params=pltpu.CompilerParams(vmem_limit_bytes=VMEM),
        cost_estimate=BRIEF,
    )(side.reshape(1), normed_two, w_up, d_down, w_down)

    source = (row_order[:, None] * share + jnp.arange(share, dtype=jnp.int32)).reshape(-1, 1)
    within = unit_orders // (2 * grid.core) * grid.core + unit_orders % grid.core
    if units == 128:
        unit_blocks = jnp.stack([unit_orders, within])
        came = grid.swap(theirs, grid.core)
        upper_pair = upper, came
    else:
        place = jnp.arange(units, dtype=jnp.int32)
        half_shards = jnp.arange(grid.count // 2, dtype=jnp.int32)
        half_shards = half_shards // grid.core * (2 * grid.core) + half_shards % grid.core
        half_shards = half_shards + (1 - side) * grid.core
        theirs = upper[:, (half_shards[:, None] * units + place).reshape(-1)]
        came = grid.swap(theirs, grid.core)
        lists = [(o[:, :, None] * units + place).reshape(-1) for o in (unit_orders, within)]
        upper_pair = upper[:, lists[0]], came[:, lists[1]]
        blocks = jnp.arange(hidden_units // 128, dtype=jnp.int32).reshape(2, -1)
        unit_blocks = jnp.stack([blocks, blocks])
    pre_pair = paired(d_pre)

    def plane(parts, one, two):
        return parts[1], grid.swap(parts[0], one), parts[3], grid.swap(parts[2], two)

    aligned = share % 16 == 0

    def stage(generate, rows, widths, gate, *operands):
        outs = [((rows, size), low) for size in widths]
        return pieced(generate, outs, aligned, after(operands[0], *gate), *operands[1:])

    def down_rest(pair, masks, gate):
        sent = None
        for mask in masks:
            layout, column = [], 0
            for number in range(len(pair) // 2):
                layout.append((number, 0, pair[2 * number].shape[1], column))
                column += pair[2 * number].shape[1]
            sent, own = stage(
                functools.partial(laid_out, layout), pair[0].shape[0] // 2, [column] * 2, gate, *pair
            )
            pair = own, grid.swap(sent, mask)
            gate = (sent,)
        return pair, sent

    their_order = grid.order([first, second, *grid.rest], grid.core)
    their_source = (their_order[:, None] * share + jnp.arange(share, dtype=jnp.int32)).reshape(-1, 1)
    d_hidden, d_branch, branch_theirs = stepped(
        units_back_kernel,
        [across, up_block, fixed, fixed, row_block, pl.BlockSpec(source.shape, lambda j: (0, 0))],
        [fixed, fixed, pl.BlockSpec((rows, width // 2), lambda j: (0, 0))],
        [((rows, width), full), ((rows, width), low), ((rows, width // 2), low)],
        (d_pre, w_up, hidden, d_down, gain_two, their_source),
        1,
        1,
    )
    wide_parts = gradient_wide(
        source, normed_two_pair, pre_pair, (d_branch, grid.swap(branch_theirs, grid.core)), mixed,
        seen_came, parts_pair[1], keys,
    )
    wide_zero = plane(wide_parts, first, second)
    down_sent, down_kept = gradient_units(
        unit_blocks, (after(upper_pair[0], *wide_parts), upper_pair[1]), down_pair
    )
    down_came = grid.swap(down_sent, grid.rest[0])
    queries_keys, values_gates = whole(
        functools.partial(attention_back_kernel, block),
        [((rows, 2 * HEADS * HEAD), low), ((rows, WIDE + LANES), low)],
        after(d_branch, down_sent), w_out, gates, parts, attended, query, kv, memory, totals,
        experts, keys, seg_cols, seg_rows,
        scratch=[pltpu.VMEM((rows, WIDE), low)] * 3,
    )
    queries_keys_pair, values_gates_pair = paired(queries_keys), paired(values_gates)

    (result,) = stepped(
        result_kernel,
        [across, down_block, fixed],
        [fixed],
        [((rows, width), low)],
        (upper, w_down, after(hidden, queries_keys)),
        1,
        1,
    )
    columns = hidden_units // 2, mixed.shape[1] // 2
    wide_two = stage(
        paired_halves, wide_parts[0].shape[0] // 2, [sum(columns)] * 4, (result,), *wide_zero
    )
    wide_one = plane(wide_two, second, first)
    half = (share * grid.count // 4, IN_COLUMNS // 2)
    in_parts = whole(
        inputs_kernel,
        [(half, low)] * 4,
        source, after(normed, *wide_two), normed_pair[1], *queries_keys_pair, *values_gates_pair,
        *parts_pair, keys,
        scratch=[pltpu.VMEM((2 * half[0], 2 * rows), low)],
    )
    in_one = plane(in_parts, first, second)
    layout = [
        (0, 0, columns[0], 0),
        (1, 0, columns[0], columns[0]),
        (0, columns[0], columns[1], 2 * columns[0]),
        (1, columns[0], columns[1], 2 * columns[0] + columns[1]),
    ]
    wide_sent, wide_own = stage(
        functools.partial(laid_out, layout), wide_one[0].shape[0] // 2, [2 * sum(columns)] * 2,
        in_parts, *wide_one,
    )
    wide_pair = wide_own, grid.swap(wide_sent, grid.rest[0])
    down_two = stage(
        forked, down_kept.shape[0] // 2, [width // 2] * 4, (wide_sent,), down_kept, down_came
    )
    down_one = plane(down_two, first, second)
    places = (grid.me * share + jnp.arange(share, dtype=jnp.int32))[:, None]
    input_grad, own_in = whole(
        inputs_back_kernel,
        [((rows, width), low), ((share, IN_COLUMNS), low)],
        queries_keys, values_gates, parts, keys, field, after(d_hidden, *down_two), gain_one,
        w_gates, w_key, w_value, w_query, places,
        scratch=[pltpu.VMEM((2 * HEADS * HEAD, width), low)],
    )
    in_two = stage(paired_halves, half[0] // 2, [half[1]] * 4, (input_grad,), *in_one)
    in_pairs = plane(in_two, second, first)
    down_three = stage(
        paired_halves, down_one[0].shape[0] // 2, [width // 2] * 4, in_two, *down_one
    )
    down_pairs = plane(down_three, second, first)
    gate = down_three
    down_left, wide_left = down_pairs, wide_pair
    for mask in grid.rest[1:]:
        tall = wide_left[0].shape[0] // 2
        wide_size = 2 * sum(columns)
        sent, own = stage(
            functools.partial(last_halves, width, wide_size), tall,
            [wide_size + width * units // share] * 2, gate, *wide_left, *down_left,
        )
        wide_left, down_left, gate = (own, grid.swap(sent, mask)), (), (sent,)
    all_pair = wide_left
    in_pair, in_sent = down_rest(in_pairs, grid.rest, gate)
    own_up = own_rows(w_up)
    own_gain_one = own_rows(norm_gain.astype(jnp.float32))[:, None]
    own_gain_two = own_rows(ffn_gain.astype(jnp.float32))[:, None]
    grad_down, grad_up, grad_gain_two, grad_out_w = pieced(
        functools.partial(most_done, width, 2 * sum(columns)),
        [
            ((units, width), full),
            ((share, hidden_units), full),
            ((1, share), full),
            ((share, MIX), full),
        ],
        aligned, after(own_up, in_sent), own_gain_two, *all_pair,
    )
    shapes = [(share, size) for size in (HEADS * HEAD, HEADS * HEAD, MIX)]
    shapes += [(GATES, share), (GATES, share), (1, share)]
    *grads, grad_vgate, grad_ogate, grad_gain_one = pieced(
        in_done,
        [(shape, full) for shape in shapes],
        aligned, after(own_in, grad_down), own_gain_one, *in_pair,
    )
    return (
        result.reshape(tokens.shape),
        input_grad.reshape(tokens.shape),
        grad_gain_one[0],
        *grads,
        grad_vgate.T,
        grad_ogate.T,
        grad_out_w.T,
        grad_gain_two[0],
        grad_up,
        grad_down,
    )


def solution(mesh):
    both = ("seq", "batch")
    stream = P(None, "batch", "seq", None)
    picks = P(None, "batch", "seq", None, None)
    return jax.shard_map(
        body,
        mesh=mesh,
        in_specs=(stream, P(None, "batch", None), picks, picks) + (P(),) * 10 + (stream,),
        out_specs=(
            stream,
            stream,
            P(both),
            P(both, None),
            P(both, None),
            P(both, None),
            P(both, None),
            P(both, None),
            P(None, both),
            P(both),
            P(both, None),
            P(both, None),
        ),
        check_vma=False,
    )
```

```python
import functools
import math

import jax
import jax.numpy as jnp
import numpy as np
from jax import lax
from jax.experimental import pallas as pl
from jax.experimental.pallas import tpu as pltpu
from jax.sharding import PartitionSpec as P

HEADS = 4
HEAD = 112
EXPERTS = 5

eps = 1e-06
VMEM = 60 << 20
FULL = 60 << 20
GRADIENT = 60 << 20
HIDDEN = 4096
BRIEF = pl.CostEstimate(flops=1024, bytes_accessed=1024, transcendentals=0)


def product(left, right):
    return jnp.dot(left, right, preferred_element_type=jnp.float32)


def product_tn(left, right):
    return lax.dot_general(
        left, right, (((0,), (0,)), ((), ())), preferred_element_type=jnp.float32
    )


def product_nt(left, right):
    return lax.dot_general(
        left, right, (((1,), (1,)), ((), ())), preferred_element_type=jnp.float32
    )


def passed_along(value, axis, steps):
    count = lax.axis_size(axis)
    initial, last = (max(0, -steps), min(count, count - steps))
    return lax.ppermute(value, axis, [(source, source + steps) for source in range(initial, last)])


class Grid:
    def __init__(self):
        self.seq, self.batch = lax.axis_size("seq"), lax.axis_size("batch")
        self.count = self.seq * self.batch
        low = self.batch.bit_length() - 1
        self.core, self.plane_a, self.plane_b = 1 << low, 1, 2 << low
        taken = self.core | self.plane_a | self.plane_b
        self.rest = [1 << at for at in range(self.count.bit_length() - 1) if not (1 << at) & taken]
        self.me = lax.axis_index("seq") * self.batch + lax.axis_index("batch")

    def swap(self, value, mask):
        both = ("seq", "batch")
        return lax.ppermute(value, both, [(i, i ^ mask) for i in range(self.count)])

    def order(self, bits, base=0):
        masks = [base]
        for bit in bits:
            masks = [mask | own for mask in masks for own in (bit, 0)]
        return self.me ^ jnp.array(masks, jnp.int32)


def after(value, *others):
    return lax.optimization_barrier((value,) + others)[0]


def in_order(order, total):
    if order == 0:
        return total
    size = total.shape[0] // 4
    parts = [total[i * size : (i + 1) * size] for i in (0, 2, 1, 3)]
    return jnp.concatenate(parts, 0)


def turn(src, parts, turned):
    at = 0
    for part in parts:
        shape = turned.shape[0], part.shape[1]
        picks = iota(shape, 0) if shape[0] == shape[1] else src
        picked = product_nt(ones_where(picks == iota(shape, 1)), part[...]).astype(jnp.bfloat16)
        turned[:, at : at + part.shape[0]] = picked
        at += part.shape[0]


def units_kernel(order_ref, left, left_came, right, right_came, *outs):
    order, at = pl.program_id(0), pl.program_id(1)
    blocks = order_ref.shape[2] // 2

    def chosen(number, ref):
        return jnp.concatenate(
            [
                ref[:, pl.ds(pl.multiple_of(order_ref[number, order, at * blocks + i] * 128, 128), 128)]
                for i in range(blocks)
            ],
            1,
        )

    total = product_tn(chosen(0, left), right[...]) + product_tn(chosen(1, left_came), right_came[...])
    total = total.astype(jnp.bfloat16)
    for number in range(2):

        @pl.when(at == number)
        def _():
            outs[number][...] = total


def gradient_units(order, left, right):
    tokens = left[0].shape[0]
    rows, columns = order.shape[2] * 128, right[0].shape[1] // 2
    moving = pl.BlockSpec((tokens, columns), lambda o, j, *_: (0, o))
    in_specs = [pl.BlockSpec(part.shape, lambda o, j, *_: (0, 0)) for part in left] + [moving] * 2
    return pl.pallas_call(
        units_kernel,
        grid_spec=pltpu.PrefetchScalarGridSpec(
            num_scalar_prefetch=1,
            grid=(2, 2),
            in_specs=in_specs,
            out_specs=[pl.BlockSpec((rows // 2, columns), lambda o, j, *_: (0, o))] * 2,
        ),
        out_shape=[jax.ShapeDtypeStruct((rows // 2, 2 * columns), jnp.bfloat16)] * 2,
        compiler_params=pltpu.CompilerParams(vmem_limit_bytes=GRADIENT),
        cost_estimate=BRIEF,
    )(order, *left, *right)


def product_low(value, right):
    return product_nt(value.astype(jnp.bfloat16), right)


def ones_where(condition):
    return jnp.where(condition, 1.0, 0.0).astype(jnp.bfloat16)


def iota(shape, dimension):
    return lax.broadcasted_iota(jnp.int32, shape, dimension)


LANES = 128
WIDE = HEADS * LANES
MIX = HEADS * EXPERTS * HEAD
GATES = HEADS * EXPERTS
CHUNK = 512


def pieces_of(total):
    return [(at, min(CHUNK, total - at)) for at in range(0, total, CHUNK)]


def spread_block(keys_ref, at, size):
    return ones_where(iota((WIDE, size), 0) == keys_ref[0:1, at : at + size])


def expert_block(keys_ref, at, size, start, twice):
    lane, own = iota((LANES, size), 0), keys_ref[1:2, at : at + size]
    hit = lane == own + start
    if twice:
        hit = hit | (lane == own + (start + GATES))
    return ones_where(hit)


def gate_parts(gates):
    lane = iota(gates.shape, 1)
    high = gates.astype(jnp.bfloat16).astype(jnp.float32)
    low = ((lane >= GATES) & (lane < 2 * GATES)) | (lane >= 3 * GATES)
    return jnp.where(low, gates - high, high).astype(jnp.bfloat16)


def pad_heads(keys_ref, size):
    return ones_where(iota((WIDE, size), 0) == keys_ref[2:3, 0:size])


def normalise(field, gain):
    factor = lax.rsqrt(jnp.mean(field * field, axis=-1, keepdims=True) + eps)
    return field * factor * gain


def normalise_back(field, gain, grad):
    factor = lax.rsqrt(jnp.mean(field * field, axis=-1, keepdims=True) + eps)
    weighted = grad * gain
    field_grad = factor * weighted - field * factor**3 * jnp.mean(
        weighted * field, axis=-1, keepdims=True
    )
    return field_grad


def value_kernel(
    tokens, gain, keys, slots, value_picks, out_picks, w_vgate, w_ogate, w_key, w_value,
    normed_out, gates_out, parts_out, experts, kv, w_gates,
    one, two,
):
    w_value.start()
    normed = normalise(tokens[...].astype(jnp.float32), gain[...].astype(jnp.float32))
    normed = normed.astype(jnp.bfloat16)
    normed_out[...] = normed
    own_key = product_nt(normed, w_key[...]).astype(jnp.bfloat16)
    kv[0] = product_nt(own_key, pad_heads(keys, own_key.shape[1])).astype(jnp.bfloat16)
    lane, gate = iota((LANES, GATES), 0), iota((LANES, GATES), 1)
    for_values = ones_where((lane == gate) | (lane == gate + GATES))
    for_outs = ones_where((lane == gate + 2 * GATES) | (lane == gate + 3 * GATES))
    low = product(for_values, w_vgate[...]) + product(for_outs, w_ogate[...])
    w_gates[...] = low.astype(jnp.bfloat16)
    logits = product_nt(normed, w_gates[...])
    count = 4 * HEADS
    block = value_picks.shape[3]
    for micro in range(value_picks.shape[0]):
        rows = slice(micro * block, (micro + 1) * block)
        for start, chosen in enumerate((value_picks, out_picks)):
            for head in range(HEADS):
                picks = chosen[micro, head].astype(jnp.float32).astype(jnp.bfloat16)
                at = 2 * (start * HEADS + head)
                first = product_tn(picks, slots[at : at + 2, :])
                second = product_tn(picks, slots[count + at : count + at + 2, :])
                one[rows, :] = first if at == 0 else one[rows, :] + first
                two[rows, :] = second if at == 0 else two[rows, :] + second
    number = slots[2 * count : 2 * count + 1, :].astype(jnp.float32)
    hit = (one[...] == number) | (two[...] == number)
    gates = jnp.where(hit, jax.nn.sigmoid(logits), 0.0)
    gates_out[...] = gates
    parts = gate_parts(gates)
    parts_out[...] = parts
    total = jnp.zeros((normed.shape[0], WIDE), jnp.float32)
    for at, size in pieces_of(MIX):
        own = product_nt(normed, w_value.rows(at, size))
        experts[:, at : at + size] = own.astype(jnp.bfloat16)
        weighted = own * product(parts, expert_block(keys, at, size, 0, True))
        total += product_low(weighted, spread_block(keys, at, size))
    kv[1] = total.astype(jnp.bfloat16)


def query_kernel(normed, keys, w_query, d_down, parts, query, both):
    own = product_nt(normed[...], w_query[...]).astype(jnp.bfloat16)
    query[...] = product_nt(own, pad_heads(keys, own.shape[1])).astype(jnp.bfloat16)
    width = normed.shape[1]
    both[:, :width] = d_down[...]
    both[:, width : 2 * width] = normed[...]
    both[:, 2 * width :] = parts[...]


def masks(seg_cols, seg_rows, at, block):
    own = seg_cols[pl.ds(at * block, block), :]
    rows = seg_rows[at]
    before = own == rows[0:1]
    here = (own == rows[1:2]) & (iota((block, block), 0) >= iota((block, block), 1))
    return before, here


def scores(query, key, allowed):
    return jnp.where(allowed, product_nt(query, key) * HEAD ** (-0.5), -1e30)


def attention_kernel(
    block, query, own, memory, parts_in, tokens, gain, keys, seg_cols, seg_rows, w_out,
    attended, totals, mixed, hidden, normed, both,
):
    micro = query.shape[0] // block
    w_out.start()

    @pl.loop(0, micro)
    def _(at):
        before, here = masks(seg_cols, seg_rows, at, block)
        rows = pl.ds(at * block, block)
        lane = iota((block, LANES), 1)
        tops = jnp.zeros((block, LANES), jnp.float32)
        for head in range(HEADS):
            cols = slice(head * LANES, (head + 1) * LANES)
            q = query[rows, cols]
            s_before = scores(q, memory[0, rows, cols], before)
            s_here = scores(q, own[0, rows, cols], here)
            top = jnp.maximum(
                jnp.max(s_before, axis=-1, keepdims=True), jnp.max(s_here, axis=-1, keepdims=True)
            )
            e_before, e_here = jnp.exp(s_before - top), jnp.exp(s_here - top)
            total = jnp.sum(e_before, axis=-1, keepdims=True) + jnp.sum(
                e_here, axis=-1, keepdims=True
            )
            share = 1.0 / total
            seen = product((e_before * share).astype(jnp.bfloat16), memory[1, rows, cols])
            seen += product((e_here * share).astype(jnp.bfloat16), own[1, rows, cols])
            attended[rows, cols] = seen.astype(jnp.bfloat16)
            tops = jnp.where(lane == head, top + jnp.log(total), tops)
        totals[rows, :] = tops

    parts = parts_in[...]
    seen = attended[...]
    total = tokens[...].astype(jnp.float32)
    for at, size in pieces_of(MIX):
        spread = product(seen, spread_block(keys, at, size))
        weight = product(parts, expert_block(keys, at, size, 2 * GATES, True))
        piece = (spread * weight).astype(jnp.bfloat16)
        mixed[:, at : at + size] = piece
        total += product(piece, w_out.rows(at, size))
    mixed[:, MIX:] = jnp.zeros((mixed.shape[0], mixed.shape[1] - MIX), jnp.bfloat16)
    hidden[...] = total
    low = normalise(total, gain[...].astype(jnp.float32)).astype(jnp.bfloat16)
    normed[...] = low
    both[:, : low.shape[1]] = low
    both[:, low.shape[1] :] = seen


def units_up_kernel(group, side, normed, w_up, d_down, w_down, upper, d_pre, theirs):
    pre = product(normed[...], w_up[...])
    back = product_nt(d_down[...], w_down[...])
    cdf = 0.5 * (1.0 + lax.erf(pre * (1.0 / math.sqrt(2.0))))
    high = (pre * cdf).astype(jnp.bfloat16)
    upper[...] = high
    slope = cdf + pre * (jnp.exp(-0.5 * pre * pre) * (1.0 / math.sqrt(2.0 * math.pi)))
    d_pre[...] = (back * slope).astype(jnp.bfloat16)
    for number in range(2):

        @pl.when(side[0] == number)
        def _():
            for at in range(0, high.shape[1], 2 * group):
                start = at + (1 - number) * group
                theirs[:, at // 2 : at // 2 + group] = high[:, start : start + group]


def units_back_kernel(
    d_pre, w_up, hidden, d_down, gain, src, d_hidden, d_branch, theirs, total
):
    at = pl.program_id(0)
    back = product_nt(d_pre[...], w_up[...])

    @pl.when(at == 0)
    def _():
        total[...] = back

    @pl.when(at > 0)
    def _():
        total[...] += back

    @pl.when(at == pl.num_programs(0) - 1)
    def _():
        grad = normalise_back(hidden[...], gain[...].astype(jnp.float32), total[...])
        grad = d_down[...].astype(jnp.float32) + grad
        d_hidden[...] = grad
        branch = grad.astype(jnp.bfloat16)
        d_branch[...] = branch
        shape = src.shape[0], branch.shape[1]
        picks = ones_where(src[...] == iota(shape, 1))
        theirs[...] = product_nt(branch, picks).astype(jnp.bfloat16)


def result_kernel(upper, w_down, hidden, result, total):
    at = pl.program_id(0)
    forth = product(upper[...], w_down[...])

    @pl.when(at == 0)
    def _():
        total[...] = hidden[...] + forth

    @pl.when(at > 0)
    def _():
        total[...] += forth

    @pl.when(at == pl.num_programs(0) - 1)
    def _():
        result[...] = total[...].astype(jnp.bfloat16)


def attention_back_kernel(
    block, d_branch, w_out, gates, parts_in, attended, query, own, memory, totals, experts, keys,
    seg_cols, seg_rows, small,
    d_seen, d_query, d_key,
):
    w_out.start()
    branch, seen, gate, parts = d_branch[...], attended[...], gates[...], parts_in[...]
    to_seen = jnp.zeros((branch.shape[0], WIDE), jnp.float32)
    to_gate = jnp.zeros((branch.shape[0], LANES), jnp.float32)
    for at, size in pieces_of(MIX):
        d_mixed = product_nt(branch, w_out.rows(at, size))
        if at == 0:
            for operand in (query, own, memory, totals, experts):
                operand.start()
        spread = spread_block(keys, at, size)
        weight = product(parts, expert_block(keys, at, size, 2 * GATES, True))
        to_seen += product_low(d_mixed * weight, spread)
        to_gate += product_low(
            d_mixed * product(seen, spread), expert_block(keys, at, size, 2 * GATES, False)
        )
    d_seen[...] = to_seen.astype(jnp.bfloat16)
    query, own, memory, totals = query.all(), own.all(), memory.all(), totals.all()
    micro = query.shape[0] // block

    @pl.loop(0, micro)
    def _(at):
        before, here = masks(seg_cols, seg_rows, at, block)
        rows = pl.ds(at * block, block)
        tops = totals[rows, :]
        for head in range(HEADS):
            cols = slice(head * LANES, (head + 1) * LANES)
            q, grad = query[rows, cols], d_seen[rows, cols]
            k_before, k_here = memory[0, rows, cols], own[0, rows, cols]
            top = tops[:, head : head + 1]
            p_before = jnp.exp(scores(q, k_before, before) - top)
            p_here = jnp.exp(scores(q, k_here, here) - top)
            g_before = product_nt(grad, memory[1, rows, cols])
            g_here = product_nt(grad, own[1, rows, cols])
            delta = jnp.sum(p_before * g_before, axis=-1, keepdims=True) + jnp.sum(
                p_here * g_here, axis=-1, keepdims=True
            )
            s_before = (p_before * (g_before - delta)).astype(jnp.bfloat16)
            s_here = (p_here * (g_here - delta)).astype(jnp.bfloat16)
            to_query = product(s_before, k_before) + product(s_here, k_here)
            d_query[rows, cols] = (to_query * HEAD ** (-0.5)).astype(jnp.bfloat16)
            to_key = product_tn(s_here, q) * HEAD ** (-0.5)
            d_key[rows, cols] = to_key.astype(jnp.bfloat16)
            to_value = product_tn(p_here.astype(jnp.bfloat16), grad)
            small[rows, cols] = to_value.astype(jnp.bfloat16)

    d_value = small[:, :WIDE]
    experts = experts.all()
    for at, size in pieces_of(MIX):
        to_gate += product_low(
            product(d_value, spread_block(keys, at, size)) * experts[:, at : at + size],
            expert_block(keys, at, size, 0, False),
        )
    small[:, WIDE:QK_AT] = (to_gate * gate * (1.0 - gate)).astype(jnp.bfloat16)
    both = (WIDE, 2 * HEADS * HEAD)
    from_query = ones_where(iota(both, 0) == keys[2:3, : both[1]])
    from_key = ones_where(iota(both, 0) == keys[3:4, : both[1]])
    total = product(d_query[...], from_query) + product(d_key[...], from_key)
    small[:, QK_AT:] = total.astype(jnp.bfloat16)


QK_AT = WIDE + LANES
V_AT = 0
Q_AT = -(-MIX // LANES) * LANES
K_AT = Q_AT + HEADS * HEAD
G_AT = K_AT + HEADS * HEAD
IN_COLUMNS = G_AT + LANES


def d_experts(small, parts, keys, at, size):
    spread = product(small[:, :WIDE], spread_block(keys, at, size))
    weight = product(parts[...], expert_block(keys, at, size, 0, True))
    return (spread * weight).astype(jnp.bfloat16)


def put_into(refs, half):
    def put(number, at, total):
        total = in_order(number, total.astype(jnp.bfloat16))
        keep = total.shape[0] // 2
        columns = slice(at - number * half, at - number * half + total.shape[1])
        refs[2 * number][:, columns] = total[:keep]
        refs[2 * number + 1][:, columns] = total[keep:]

    return put


def halves_of(total, half):
    for number in range(2):
        at, stop = number * half, min(total, (number + 1) * half)
        while at < stop:
            size = min(CHUNK, stop - at)
            yield number, at, size
            at += size


def wide_kernel(
    src, left, second_came, right, right_came, branch, branch_came, mixed, both_came, keys, *refs,
):
    turned, turned_branch = refs[-2:]
    tokens, width = left.shape
    left_came, seen_came = second_came.at[:, :width], second_came.at[:, width:]
    parts_came = both_came.at[:, 2 * width :]
    order = pl.program_id(0)
    ups, outs = right.shape[1], mixed.shape[1]

    @pl.when(order == 0)
    def _():
        turn(src[...], (left, left_came), turned)
        turn(src[...], (branch, branch_came), turned_branch)

    for number in range(2):

        @pl.when(order == number)
        def _():
            def put(at, total):
                total = in_order(number, total.astype(jnp.bfloat16))
                keep = total.shape[0] // 2
                columns = slice(at, at + total.shape[1])
                refs[2 * number][:, columns] = total[:keep]
                refs[2 * number + 1][:, columns] = total[keep:]

            for at in range(0, ups, 2 * CHUNK):
                columns = slice(at, at + 2 * CHUNK)
                total = product(turned[:, :tokens], right[:, columns])
                put(at, total + product(turned[:, tokens:], right_came[:, columns]))
            at, stop = 0, min(outs, MIX - number * outs)
            while at < stop:
                size = min(CHUNK, stop - at)
                start = number * outs + at
                spread = product(seen_came[...], spread_block(keys, start, size))
                weight = product(parts_came[...], expert_block(keys, start, size, 2 * GATES, True))
                came = (spread * weight).astype(jnp.bfloat16)
                total = product(turned_branch[:, :tokens], mixed[:, at : at + size])
                put(ups + at, total + product(turned_branch[:, tokens:], came))
                at += size
            if at < outs:
                put(ups + at, jnp.zeros((turned.shape[0], outs - at), jnp.float32))


def gradient_wide(src, left, right, branch, mixed, both_came, keys):
    tokens, rows = left[0].shape[0], src.shape[0]
    ups, outs = right[0].shape[1] // 2, mixed.shape[1] // 2
    operands = (src, *left, *right, *branch, mixed, both_came, keys)

    def fixed(array):
        return pl.BlockSpec(array.shape, lambda o: (0, 0))

    specs = [fixed(array) for array in operands]
    specs[3] = specs[4] = pl.BlockSpec((tokens, ups), lambda o: (0, o))
    specs[7] = pl.BlockSpec((tokens, outs), lambda o: (0, o))
    shape = (rows // 2, ups + outs)
    return pl.pallas_call(
        wide_kernel,
        grid=(2,),
        in_specs=specs,
        out_specs=[pl.BlockSpec(shape, lambda o: (0, 0))] * 4,
        out_shape=[jax.ShapeDtypeStruct(shape, jnp.bfloat16)] * 4,
        scratch_shapes=[pltpu.VMEM((rows, 2 * tokens), jnp.bfloat16)] * 2,
        compiler_params=pltpu.CompilerParams(vmem_limit_bytes=GRADIENT),
        cost_estimate=BRIEF,
    )(*operands)


def inputs_kernel(
    src, left, both_came, small, small_came, parts, keys, *refs,
):
    turned = refs[-1]
    half = IN_COLUMNS // 2
    tokens, width = left.shape
    left_came = both_came.at[:, width : 2 * width]
    parts_came = both_came.at[:, 2 * width :]
    put = put_into(refs, half)

    def times(one, two):
        return product(turned[:, :tokens], one) + product(turned[:, tokens:], two)

    turn(src[...], (left, left_came), turned)
    for number, at, size in halves_of(MIX, half):
        one = d_experts(small, parts, keys, at, size)
        two = d_experts(small_came, parts_came, keys, at, size)
        put(number, at, times(one, two))
    put(1, MIX, jnp.zeros((turned.shape[0], Q_AT - MIX), jnp.float32))
    for at in range(0, 2 * HEADS * HEAD, CHUNK):
        columns = slice(QK_AT + at, QK_AT + min(at + CHUNK, 2 * HEADS * HEAD))
        put(1, Q_AT + at, times(small[:, columns], small_came[:, columns]))
    put(1, G_AT, times(small[:, WIDE:QK_AT], small_came[:, WIDE:QK_AT]))


def inputs_back_kernel(
    small, parts, keys, tokens, d_hidden, gain, w_gates, w_key, w_value,
    w_query, places, input_grad, own_in, w_both,
):
    w_value.start()
    size = HEADS * HEAD
    w_both[:size, :] = w_query[...]
    w_both[size:, :] = w_key[...]
    total = product(small[:, WIDE:QK_AT], w_gates[...])
    total += product(small[:, QK_AT:], w_both[...])
    tokens.start()
    d_hidden.start()
    for at, size in pieces_of(MIX):
        total += product(d_experts(small, parts, keys, at, size), w_value.rows(at, size))
    picks = ones_where(places[...] == iota((places.shape[0], tokens.shape[1]), 1))
    for at, weight in ((V_AT, w_value.all()), (Q_AT, w_both), (G_AT, w_gates)):
        own = product_nt(picks, weight[...]).astype(jnp.bfloat16)
        own_in[:, at : at + own.shape[1]] = own
    own_in[:, MIX:Q_AT] = jnp.zeros((places.shape[0], Q_AT - MIX), jnp.bfloat16)
    grad = normalise_back(tokens.all()[...].astype(jnp.float32), gain[...].astype(jnp.float32), total)
    input_grad[...] = (d_hidden.all()[...] + grad).astype(jnp.bfloat16)


def pieced(generate, outs, aligned, *operands):
    if not aligned:
        results = [jnp.zeros(shape, dtype) for shape, dtype in outs]
        for number, row, column, value in generate(*operands):
            value = value.astype(results[number].dtype)
            results[number] = lax.dynamic_update_slice(results[number], value, (row, column))
        return results

    def kernel(*refs):
        given, made = refs[: len(operands)], refs[len(operands) :]
        for number, row, column, value in generate(*given):
            rows, columns = slice(row, row + value.shape[0]), slice(column, column + value.shape[1])
            made[number][rows, columns] = value.astype(made[number].dtype)

    return whole(kernel, outs, *operands, grant=FULL)


def summed(pair, rows, columns=slice(None)):
    return sum(part[rows, columns].astype(jnp.float32) for part in pair)


def forked(kept, came):
    columns, rows = kept.shape[1] // 2, kept.shape[0] // 2
    for number in range(2):
        own = slice(number * columns, (number + 1) * columns)
        for half in range(2):
            part = slice(half * rows, (half + 1) * rows)
            yield 2 * number + half, 0, 0, summed((kept, came), part, own)


def paired_halves(*refs):
    for number in range(2):
        column = 0
        own = refs[number * len(refs) // 2 : (number + 1) * len(refs) // 2]
        for pair in zip(own[::2], own[1::2]):
            rows = pair[0].shape[0] // 2
            for half in range(2):
                part = slice(half * rows, (half + 1) * rows)
                yield 2 * number + half, 0, column, summed(pair, part)
            column += pair[0].shape[1]


def laid_out(layout, *refs):
    for number, start, size, column in layout:
        pair = refs[2 * number : 2 * number + 2]
        rows = pair[0].shape[0] // 2
        for half in range(2):
            part = slice(half * rows, (half + 1) * rows)
            yield half, 0, column, summed(pair, part, slice(start, start + size))


def as_row(column):
    size = column.shape[0]
    return jnp.sum(jnp.where(iota((size, size), 0) == iota((size, size), 1), column, 0.0), 0, keepdims=True)


def last_halves(width, wide_size, *refs):
    rows = refs[0].shape[0] // 2
    for half in range(2):
        part = slice(half * rows, (half + 1) * rows)
        yield half, 0, 0, summed(refs[:2], part, slice(0, wide_size))
        if len(refs) == 2:
            blocks = (refs[0].shape[1] - wide_size) // width // 2
            for block in range(blocks):
                at = wide_size + (half * blocks + block) * width
                for low in range(2):
                    value = summed(refs, slice(low * rows, (low + 1) * rows), slice(at, at + width))
                    yield half, 0, wide_size + (2 * block + low) * width, value
            continue
        for number in range(2):
            pair = refs[2 + 2 * number : 4 + 2 * number]
            tall = pair[0].shape[0] // 2
            for block in range(tall // rows):
                at = half * tall + block * rows
                yield half, 0, wide_size + block * width + number * width // 2, summed(
                    pair, slice(at, at + rows)
                )


def most_done(width, wide_size, weight, gain, wide, wide_came):
    rows = wide.shape[0]
    for block in range((wide.shape[1] - wide_size) // width):
        columns = slice(wide_size + block * width, wide_size + (block + 1) * width)
        yield 0, block * rows, 0, summed((wide, wide_came), slice(None), columns)
    along = 0.0
    for at in range(0, HIDDEN, 2 * CHUNK):
        columns = slice(at, at + 2 * CHUNK)
        piece = summed((wide, wide_came), slice(None), columns)
        yield 1, 0, at, piece
        along += jnp.sum(piece * weight[:, columns].astype(jnp.float32), axis=1, keepdims=True)
    yield 2, 0, 0, as_row(along / gain[:, :])
    yield 3, 0, 0, summed((wide, wide_came), slice(None), slice(HIDDEN, HIDDEN + MIX))


def in_done(weight, gain, *refs):
    total = summed(refs, slice(None))
    for number, (at, size) in enumerate(((Q_AT, HEADS * HEAD), (K_AT, HEADS * HEAD), (V_AT, MIX))):
        yield number, 0, 0, total[:, at : at + size]
    gates = total[:, G_AT:].T
    yield 3, 0, 0, gates[:GATES]
    yield 4, 0, 0, gates[2 * GATES : 3 * GATES]
    along = jnp.sum(total * weight[:, :].astype(jnp.float32), axis=1, keepdims=True)
    yield 5, 0, 0, as_row(along / gain[:, :])


class Late:
    def __init__(self, source, target, sems):
        self.source, self.target, self.sems = source, target, sems
        self.shape, self.copies = target.shape, None

    def start(self):
        if len(self.shape) == 3:
            self.copies = [pltpu.make_async_copy(self.source, self.target, self.sems.at[0])]
        else:
            self.copies = [
                pltpu.make_async_copy(
                    self.source.at[pl.ds(at, size)], self.target.at[pl.ds(at, size)], self.sems.at[number]
                )
                for number, (at, size) in enumerate(pieces_of(self.shape[0]))
            ]
        for copy in self.copies:
            copy.start()

    def rows(self, at, size):
        number = at // CHUNK
        if self.copies[number] is not None:
            self.copies[number].wait()
            self.copies[number] = None
        return self.target[at : at + size]

    def all(self):
        for number, copy in enumerate(self.copies):
            if copy is not None:
                copy.wait()
                self.copies[number] = None
        return self.target


def whole(kernel, outs, *operands, scratch=(), grant=VMEM, late=()):
    outs = [jax.ShapeDtypeStruct(shape, dtype) for shape, dtype in outs]
    given, made, kept = len(operands), len(outs), len(scratch)
    buffers = [pltpu.VMEM(operands[number].shape, operands[number].dtype) for number in late]
    sems = [pltpu.SemaphoreType.DMA((len(pieces_of(operands[number].shape[-2])),)) for number in late]

    def run(*refs):
        refs = list(refs)
        extra = refs[given + made + kept :]
        for place, number in enumerate(late):
            refs[number] = Late(refs[number], extra[place], extra[len(late) + place])
        kernel(*refs[: given + made + kept])

    specs = [
        pl.BlockSpec(memory_space=pl.ANY if number in late else pltpu.VMEM) for number in range(given)
    ]
    return pl.pallas_call(
        run,
        out_shape=outs,
        in_specs=specs,
        out_specs=[pl.BlockSpec(memory_space=pltpu.VMEM)] * made,
        scratch_shapes=list(scratch) + buffers + sems,
        compiler_params=pltpu.CompilerParams(vmem_limit_bytes=grant),
        cost_estimate=BRIEF,
    )(*operands)


def body(
    tokens,
    segments,
    value_experts,
    out_experts,
    norm_gain,
    w_query,
    w_key,
    w_value,
    w_vgate,
    w_ogate,
    w_out,
    ffn_gain,
    w_up,
    w_down,
    cotangent,
):
    grid = Grid()
    first, second = grid.plane_a, grid.plane_b
    row_order = grid.order([first, second, *grid.rest])
    unit_orders = jnp.stack(
        [
            grid.order([grid.rest[0], first, second, *grid.rest[1:]]),
            grid.order([grid.rest[0], second, first, *grid.rest[1:]]),
        ]
    )
    micro, _, block, width = tokens.shape
    rows = micro * block
    hidden_units = w_up.shape[1]
    place = lax.axis_index("seq")
    own_segs = lax.dynamic_slice_in_dim(segments, place * block, block, 2)[:, 0]
    prior_start = jnp.maximum(place - 1, 0) * block
    prior_segs = jnp.where(
        place > 0, lax.dynamic_slice_in_dim(segments, prior_start, block, 2)[:, 0], -1
    )
    gain_one, gain_two = norm_gain[None], ffn_gain[None]
    column = np.arange(-(-MIX // LANES) * LANES)
    head_column = np.arange(WIDE)
    keys = np.full((4, column.size), -1, np.int32)
    keys[0, :MIX] = (column // (EXPERTS * HEAD) * LANES + column % HEAD)[:MIX]
    keys[1, :MIX] = (column // HEAD)[:MIX]
    keys[2, : HEADS * HEAD] = (head_column // HEAD * LANES + head_column % HEAD)[: HEADS * HEAD]
    keys[3, HEADS * HEAD : 2 * HEADS * HEAD] = keys[2, : HEADS * HEAD]
    keys = jnp.asarray(keys)
    lane = np.arange(4 * GATES)
    slots = np.zeros((2 * 16 + 8, LANES), np.float32)
    source = 2 * (lane % GATES // EXPERTS) + 2 * HEADS * (lane // (2 * GATES))
    slots[source, lane] = 1
    slots[16 + source + 1, lane] = 1
    slots[32] = -1
    slots[32, : 4 * GATES] = lane % EXPERTS
    slots = jnp.asarray(slots, jnp.bfloat16)
    value_picks, out_picks = (
        jnp.transpose(picks[:, 0], (0, 2, 3, 1))
        for picks in (value_experts, out_experts)
    )
    w_query, w_key, w_value = w_query.T, w_key.T, w_value.T
    share = width // grid.count

    def own_rows(array):
        return lax.dynamic_slice_in_dim(array, grid.me * share, share, 0)

    seg_cols = own_segs.reshape(rows, 1)
    seg_rows = jnp.stack([prior_segs, own_segs], 1)

    field = tokens.reshape(rows, width)
    d_down = cotangent.reshape(rows, width)
    low, full = jnp.bfloat16, jnp.float32
    normed, gates, parts, experts, kv, w_gates = whole(
        value_kernel,
        [
            ((rows, width), low),
            ((rows, LANES), full),
            ((rows, LANES), low),
            ((rows, MIX), low),
            ((2, rows, WIDE), low),
            ((LANES, width), low),
        ],
        field, gain_one, keys, slots, value_picks, out_picks, w_vgate.T, w_ogate.T, w_key, w_value,
        late=(9,),
        scratch=[pltpu.VMEM((rows, LANES), full)] * 2,
    )
    memory = passed_along(kv, "seq", 1)

    def paired(value):
        return value, grid.swap(value, grid.core)

    step = 1024
    fixed = pl.BlockSpec((rows, width), lambda j: (0, 0))
    across = pl.BlockSpec((rows, step), lambda j: (0, j))
    up_block = pl.BlockSpec((width, step), lambda j: (0, j))
    down_block = pl.BlockSpec((step, width), lambda j: (j, 0))
    row_block = pl.BlockSpec((1, width), lambda j: (0, 0))

    def stepped(kernel, in_specs, out_specs, outs, operands, products, scratch=0):
        return pl.pallas_call(
            kernel,
            grid=(hidden_units // step,),
            in_specs=in_specs,
            out_specs=out_specs,
            out_shape=[jax.ShapeDtypeStruct(shape, dtype) for shape, dtype in outs],
            scratch_shapes=[pltpu.VMEM((rows, width), full)] * scratch,
            compiler_params=pltpu.CompilerParams(vmem_limit_bytes=VMEM),
            cost_estimate=BRIEF,
        )(*operands)

    query, both = whole(
        query_kernel,
        [((rows, WIDE), low), ((rows, 2 * width + LANES), low)],
        after(normed, kv, seg_cols, seg_rows), keys, w_query, d_down, parts,
    )
    both_came = grid.swap(after(both, memory), grid.core)
    down_pair = d_down, both_came
    mixed_columns = -(-MIX // 256) * 256
    attended, totals, mixed, hidden, normed_two, second_both = whole(
        functools.partial(attention_kernel, block),
        [
            ((rows, WIDE), low),
            ((rows, LANES), full),
            ((rows, mixed_columns), low),
            ((rows, width), full),
            ((rows, width), low),
            ((rows, width + WIDE), low),
        ],
        query, kv, memory, parts, field, gain_two,
        keys, seg_cols, seg_rows, w_out, late=(9,),
    )
    normed_two_pair = normed_two, grid.swap(second_both, grid.core)
    units = hidden_units // grid.count
    side = (grid.me // grid.core) % 2
    upper, d_pre, theirs = pl.pallas_call(
        functools.partial(units_up_kernel, grid.core * units),
        grid_spec=pltpu.PrefetchScalarGridSpec(
            num_scalar_prefetch=1,
            grid=(hidden_units // step,),
            in_specs=[
                pl.BlockSpec((rows, width), lambda j, _: (0, 0)),
                pl.BlockSpec((width, step), lambda j, _: (0, j)),
                pl.BlockSpec((rows, width), lambda j, _: (0, 0)),
                pl.BlockSpec((step, width), lambda j, _: (j, 0)),
            ],
            out_specs=[
                pl.BlockSpec((rows, step), lambda j, _: (0, j)),
                pl.BlockSpec((rows, step), lambda j, _: (0, j)),
                pl.BlockSpec((rows, step // 2), lambda j, _: (0, j)),
            ],
        ),
        out_shape=[
            jax.ShapeDtypeStruct((rows, hidden_units), low),
            jax.ShapeDtypeStruct((rows, hidden_units), low),
            jax.ShapeDtypeStruct((rows, hidden_units // 2), low),
        ],
        compiler_params=pltpu.CompilerParams(vmem_limit_bytes=VMEM),
        cost_estimate=BRIEF,
    )(side.reshape(1), normed_two, w_up, after(d_down, both_came), w_down)

    source = (row_order[:, None] * share + jnp.arange(share, dtype=jnp.int32)).reshape(-1, 1)
    within = unit_orders // (2 * grid.core) * grid.core + unit_orders % grid.core
    if units == 128:
        unit_blocks = jnp.stack([unit_orders, within])
        came = grid.swap(theirs, grid.core)
        upper_pair = upper, came
    else:
        place = jnp.arange(units, dtype=jnp.int32)
        half_shards = jnp.arange(grid.count // 2, dtype=jnp.int32)
        half_shards = half_shards // grid.core * (2 * grid.core) + half_shards % grid.core
        half_shards = half_shards + (1 - side) * grid.core
        theirs = upper[:, (half_shards[:, None] * units + place).reshape(-1)]
        came = grid.swap(theirs, grid.core)
        lists = [(o[:, :, None] * units + place).reshape(-1) for o in (unit_orders, within)]
        upper_pair = upper[:, lists[0]], came[:, lists[1]]
        blocks = jnp.arange(hidden_units // 128, dtype=jnp.int32).reshape(2, -1)
        unit_blocks = jnp.stack([blocks, blocks])
    pre_pair = paired(d_pre)

    def plane(parts, one, two):
        return parts[1], grid.swap(parts[0], one), parts[3], grid.swap(parts[2], two)

    aligned = share % 16 == 0

    def stage(generate, rows, widths, gate, *operands):
        outs = [((rows, size), low) for size in widths]
        return pieced(generate, outs, aligned, after(operands[0], *gate), *operands[1:])

    def down_rest(pair, masks, gate):
        sent = None
        for mask in masks:
            layout, column = [], 0
            for number in range(len(pair) // 2):
                layout.append((number, 0, pair[2 * number].shape[1], column))
                column += pair[2 * number].shape[1]
            sent, own = stage(
                functools.partial(laid_out, layout), pair[0].shape[0] // 2, [column] * 2, gate, *pair
            )
            pair = own, grid.swap(sent, mask)
            gate = (sent,)
        return pair, sent

    their_order = grid.order([first, second, *grid.rest], grid.core)
    their_source = (their_order[:, None] * share + jnp.arange(share, dtype=jnp.int32)).reshape(-1, 1)
    d_hidden, d_branch, branch_theirs = stepped(
        units_back_kernel,
        [across, up_block, fixed, fixed, row_block, pl.BlockSpec(source.shape, lambda j: (0, 0))],
        [fixed, fixed, pl.BlockSpec((rows, width // 2), lambda j: (0, 0))],
        [((rows, width), full), ((rows, width), low), ((rows, width // 2), low)],
        (d_pre, w_up, hidden, d_down, gain_two, their_source),
        1,
        1,
    )
    wide_parts = gradient_wide(
        source, normed_two_pair, pre_pair, (d_branch, grid.swap(branch_theirs, grid.core)), mixed,
        both_came, keys,
    )
    wide_zero = plane(wide_parts, first, second)
    down_sent, down_kept = gradient_units(
        unit_blocks, (after(upper_pair[0], *wide_parts), upper_pair[1]), down_pair
    )
    down_came = grid.swap(down_sent, grid.rest[0])
    (small,) = whole(
        functools.partial(attention_back_kernel, block),
        [((rows, QK_AT + 2 * HEADS * HEAD), low)],
        after(d_branch, down_sent), w_out, gates, parts, attended, query, kv, memory, totals,
        experts, keys, seg_cols, seg_rows, late=(1, 5, 6, 7, 8, 9),
        scratch=[pltpu.VMEM((rows, WIDE), low)] * 3,
    )
    small_pair = paired(small)

    columns = hidden_units // 2, mixed.shape[1] // 2
    wide_two = stage(
        paired_halves, wide_parts[0].shape[0] // 2, [sum(columns)] * 4, (small,), *wide_zero
    )
    wide_one = plane(wide_two, second, first)
    half = (share * grid.count // 4, IN_COLUMNS // 2)
    in_parts = whole(
        inputs_kernel,
        [(half, low)] * 4,
        source, after(normed, *wide_two), both_came, *small_pair, parts, keys,
        scratch=[pltpu.VMEM((2 * half[0], 2 * rows), low)],
    )
    in_one = plane(in_parts, first, second)
    layout = [
        (0, 0, columns[0], 0),
        (1, 0, columns[0], columns[0]),
        (0, columns[0], columns[1], 2 * columns[0]),
        (1, columns[0], columns[1], 2 * columns[0] + columns[1]),
    ]
    wide_sent, wide_own = stage(
        functools.partial(laid_out, layout), wide_one[0].shape[0] // 2, [2 * sum(columns)] * 2,
        in_parts, *wide_one,
    )
    wide_pair = wide_own, grid.swap(wide_sent, grid.rest[0])
    down_two = stage(
        forked, down_kept.shape[0] // 2, [width // 2] * 4, (wide_sent,), down_kept, down_came
    )
    down_one = plane(down_two, first, second)
    (result,) = stepped(
        result_kernel,
        [across, down_block, fixed],
        [fixed],
        [((rows, width), low)],
        (upper, w_down, after(hidden, *down_two)),
        1,
        1,
    )
    in_two = stage(paired_halves, half[0] // 2, [half[1]] * 4, (result,), *in_one)
    in_pairs = plane(in_two, second, first)
    down_three = stage(
        paired_halves, down_one[0].shape[0] // 2, [width // 2] * 4, in_two, *down_one
    )
    down_pairs = plane(down_three, second, first)
    gate = down_three
    down_left, wide_left = down_pairs, wide_pair
    for mask in grid.rest[1:]:
        tall = wide_left[0].shape[0] // 2
        wide_size = 2 * sum(columns)
        sent, own = stage(
            functools.partial(last_halves, width, wide_size), tall,
            [wide_size + width * units // share] * 2, gate, *wide_left, *down_left,
        )
        wide_left, down_left, gate = (own, grid.swap(sent, mask)), (), (sent,)
    all_pair = wide_left
    in_pair, in_sent = down_rest(in_pairs, grid.rest[:1], gate)
    places = (grid.me * share + jnp.arange(share, dtype=jnp.int32))[:, None]
    input_grad, own_in = whole(
        inputs_back_kernel,
        [((rows, width), low), ((share, IN_COLUMNS), low)],
        small, parts, keys, field, after(d_hidden, in_sent), gain_one,
        w_gates, w_key, w_value, w_query, places,
        late=(3, 4, 8),
        scratch=[pltpu.VMEM((2 * HEADS * HEAD, width), low)],
    )
    in_pair, in_sent = down_rest(in_pair, grid.rest[1:], (input_grad,))
    own_up = own_rows(w_up)
    own_gain_one = own_rows(norm_gain.astype(jnp.float32))[:, None]
    own_gain_two = own_rows(ffn_gain.astype(jnp.float32))[:, None]
    grad_down, grad_up, grad_gain_two, grad_out_w = pieced(
        functools.partial(most_done, width, 2 * sum(columns)),
        [
            ((units, width), full),
            ((share, hidden_units), full),
            ((1, share), full),
            ((share, MIX), full),
        ],
        aligned, after(own_up, in_sent), own_gain_two, *all_pair,
    )
    shapes = [(share, size) for size in (HEADS * HEAD, HEADS * HEAD, MIX)]
    shapes += [(GATES, share), (GATES, share), (1, share)]
    *grads, grad_vgate, grad_ogate, grad_gain_one = pieced(
        in_done,
        [(shape, full) for shape in shapes],
        aligned, after(own_in, grad_down), own_gain_one, *in_pair,
    )
    return (
        result.reshape(tokens.shape),
        input_grad.reshape(tokens.shape),
        grad_gain_one[0],
        *grads,
        grad_vgate.T,
        grad_ogate.T,
        grad_out_w.T,
        grad_gain_two[0],
        grad_up,
        grad_down,
    )


def solution(mesh):
    both = ("seq", "batch")
    stream = P(None, "batch", "seq", None)
    picks = P(None, "batch", "seq", None, None)
    return jax.shard_map(
        body,
        mesh=mesh,
        in_specs=(stream, P(None, "batch", None), picks, picks) + (P(),) * 10 + (stream,),
        out_specs=(
            stream,
            stream,
            P(both),
            P(both, None),
            P(both, None),
            P(both, None),
            P(both, None),
            P(both, None),
            P(None, both),
            P(both),
            P(both, None),
            P(both, None),
        ),
        check_vma=False,
    )
```

```python
import functools
import math

import jax
import jax.numpy as jnp
import numpy as np
from jax import lax
from jax.experimental import pallas as pl
from jax.experimental.pallas import tpu as pltpu
from jax.sharding import PartitionSpec as P

HEADS = 4
HEAD = 112
EXPERTS = 5

eps = 1e-06
VMEM = 56 << 20
FULL = 60 << 20
GRADIENT = 48 << 20
HIDDEN = 4096
BRIEF = pl.CostEstimate(flops=1024, bytes_accessed=1024, transcendentals=0)


def product(left, right):
    return jnp.dot(left, right, preferred_element_type=jnp.float32)


def product_tn(left, right):
    return lax.dot_general(
        left, right, (((0,), (0,)), ((), ())), preferred_element_type=jnp.float32
    )


def product_nt(left, right):
    return lax.dot_general(
        left, right, (((1,), (1,)), ((), ())), preferred_element_type=jnp.float32
    )


def passed_along(value, axis, steps):
    count = lax.axis_size(axis)
    initial, last = (max(0, -steps), min(count, count - steps))
    return lax.ppermute(value, axis, [(source, source + steps) for source in range(initial, last)])


class Grid:
    def __init__(self):
        self.seq, self.batch = lax.axis_size("seq"), lax.axis_size("batch")
        self.count = self.seq * self.batch
        low = self.batch.bit_length() - 1
        self.core, self.plane_a, self.plane_b = 1 << low, 1, 2 << low
        taken = self.core | self.plane_a | self.plane_b
        self.rest = [1 << at for at in range(self.count.bit_length() - 1) if not (1 << at) & taken]
        self.me = lax.axis_index("seq") * self.batch + lax.axis_index("batch")

    def swap(self, value, mask):
        both = ("seq", "batch")
        return lax.ppermute(value, both, [(i, i ^ mask) for i in range(self.count)])

    def order(self, bits, base=0):
        masks = [base]
        for bit in bits:
            masks = [mask | own for mask in masks for own in (bit, 0)]
        return self.me ^ jnp.array(masks, jnp.int32)


def after(value, *others):
    return lax.optimization_barrier((value,) + others)[0]


def in_order(order, total):
    if order == 0:
        return total
    size = total.shape[0] // 4
    parts = [total[i * size : (i + 1) * size] for i in (0, 2, 1, 3)]
    return jnp.concatenate(parts, 0)


def turn(src, parts, turned):
    at = 0
    for part in parts:
        shape = turned.shape[0], part.shape[1]
        picks = iota(shape, 0) if shape[0] == shape[1] else src
        picked = product_nt(ones_where(picks == iota(shape, 1)), part[...]).astype(jnp.bfloat16)
        turned[:, at : at + part.shape[0]] = picked
        at += part.shape[0]


def units_kernel(order_ref, left, left_came, right, right_came, *outs):
    order, at = pl.program_id(0), pl.program_id(1)
    blocks = order_ref.shape[2] // 2

    def chosen(number, ref):
        return jnp.concatenate(
            [
                ref[:, pl.ds(pl.multiple_of(order_ref[number, order, at * blocks + i] * 128, 128), 128)]
                for i in range(blocks)
            ],
            1,
        )

    total = product_tn(chosen(0, left), right[...]) + product_tn(chosen(1, left_came), right_came[...])
    total = total.astype(jnp.bfloat16)
    for number in range(2):

        @pl.when(at == number)
        def _():
            outs[number][...] = total


def gradient_units(order, left, right):
    tokens = left[0].shape[0]
    rows, columns = order.shape[2] * 128, right[0].shape[1] // 2
    moving = pl.BlockSpec((tokens, columns), lambda o, j, *_: (0, o))
    in_specs = [pl.BlockSpec(part.shape, lambda o, j, *_: (0, 0)) for part in left] + [moving] * 2
    return pl.pallas_call(
        units_kernel,
        grid_spec=pltpu.PrefetchScalarGridSpec(
            num_scalar_prefetch=1,
            grid=(2, 2),
            in_specs=in_specs,
            out_specs=[pl.BlockSpec((rows // 2, columns), lambda o, j, *_: (0, o))] * 2,
        ),
        out_shape=[jax.ShapeDtypeStruct((rows // 2, 2 * columns), jnp.bfloat16)] * 2,
        compiler_params=pltpu.CompilerParams(vmem_limit_bytes=GRADIENT),
        cost_estimate=BRIEF,
    )(order, *left, *right)


def product_low(value, right):
    return product_nt(value.astype(jnp.bfloat16), right)


def ones_where(condition):
    return jnp.where(condition, 1.0, 0.0).astype(jnp.bfloat16)


def iota(shape, dimension):
    return lax.broadcasted_iota(jnp.int32, shape, dimension)


LANES = 128
WIDE = HEADS * LANES
MIX = HEADS * EXPERTS * HEAD
GATES = HEADS * EXPERTS
CHUNK = 512


def pieces_of(total):
    return [(at, min(CHUNK, total - at)) for at in range(0, total, CHUNK)]


def spread_block(keys_ref, at, size):
    return ones_where(iota((WIDE, size), 0) == keys_ref[0:1, at : at + size])


def expert_block(keys_ref, at, size, start, twice):
    lane, own = iota((LANES, size), 0), keys_ref[1:2, at : at + size]
    hit = lane == own + start
    if twice:
        hit = hit | (lane == own + (start + GATES))
    return ones_where(hit)


def gate_parts(gates):
    lane = iota(gates.shape, 1)
    high = gates.astype(jnp.bfloat16).astype(jnp.float32)
    low = ((lane >= GATES) & (lane < 2 * GATES)) | (lane >= 3 * GATES)
    return jnp.where(low, gates - high, high).astype(jnp.bfloat16)


def pad_heads(keys_ref, size):
    return ones_where(iota((WIDE, size), 0) == keys_ref[2:3, 0:size])


def normalise(field, gain):
    factor = lax.rsqrt(jnp.mean(field * field, axis=-1, keepdims=True) + eps)
    return field * factor * gain


def normalise_back(field, gain, grad):
    factor = lax.rsqrt(jnp.mean(field * field, axis=-1, keepdims=True) + eps)
    weighted = grad * gain
    field_grad = factor * weighted - field * factor**3 * jnp.mean(
        weighted * field, axis=-1, keepdims=True
    )
    return field_grad


def key_kernel(tokens, gain, keys, w_key, normed_out, key):
    normed = normalise(tokens[...].astype(jnp.float32), gain[...].astype(jnp.float32))
    normed = normed.astype(jnp.bfloat16)
    normed_out[...] = normed
    own = product_nt(normed, w_key[...]).astype(jnp.bfloat16)
    key[...] = product_nt(own, pad_heads(keys, own.shape[1])).astype(jnp.bfloat16)


def value_kernel(
    normed_in, keys, slots, value_picks, out_picks, w_vgate, w_ogate, w_value,
    gates_out, parts_out, experts, value, w_gates,
    one, two,
):
    w_value.start()
    normed = normed_in[...]
    lane, gate = iota((LANES, GATES), 0), iota((LANES, GATES), 1)
    for_values = ones_where((lane == gate) | (lane == gate + GATES))
    for_outs = ones_where((lane == gate + 2 * GATES) | (lane == gate + 3 * GATES))
    low = product(for_values, w_vgate[...]) + product(for_outs, w_ogate[...])
    w_gates[...] = low.astype(jnp.bfloat16)
    logits = product_nt(normed, w_gates[...])
    count = 4 * HEADS
    block = value_picks.shape[3]
    for micro in range(value_picks.shape[0]):
        rows = slice(micro * block, (micro + 1) * block)
        for start, chosen in enumerate((value_picks, out_picks)):
            for head in range(HEADS):
                picks = chosen[micro, head].astype(jnp.float32).astype(jnp.bfloat16)
                at = 2 * (start * HEADS + head)
                first = product_tn(picks, slots[at : at + 2, :])
                second = product_tn(picks, slots[count + at : count + at + 2, :])
                one[rows, :] = first if at == 0 else one[rows, :] + first
                two[rows, :] = second if at == 0 else two[rows, :] + second
    number = slots[2 * count : 2 * count + 1, :].astype(jnp.float32)
    hit = (one[...] == number) | (two[...] == number)
    gates = jnp.where(hit, jax.nn.sigmoid(logits), 0.0)
    gates_out[...] = gates
    parts = gate_parts(gates)
    parts_out[...] = parts
    total = jnp.zeros((normed.shape[0], WIDE), jnp.float32)
    for at, size in pieces_of(MIX):
        own = product_nt(normed, w_value.rows(at, size))
        experts[:, at : at + size] = own.astype(jnp.bfloat16)
        weighted = own * product(parts, expert_block(keys, at, size, 0, True))
        total += product_low(weighted, spread_block(keys, at, size))
    value[...] = total.astype(jnp.bfloat16)


def query_kernel(normed, keys, w_query, d_down, parts, query, both):
    own = product_nt(normed[...], w_query[...]).astype(jnp.bfloat16)
    query[...] = product_nt(own, pad_heads(keys, own.shape[1])).astype(jnp.bfloat16)
    width = normed.shape[1]
    both[:, :width] = d_down[...]
    both[:, width : 2 * width] = normed[...]
    both[:, 2 * width :] = parts[...]


def masks(seg_cols, seg_rows, at, block):
    own = seg_cols[pl.ds(at * block, block), :]
    rows = seg_rows[at]
    before = own == rows[0:1]
    here = (own == rows[1:2]) & (iota((block, block), 0) >= iota((block, block), 1))
    return before, here


def scores(query, key, allowed):
    return jnp.where(allowed, product_nt(query, key) * HEAD ** (-0.5), -1e30)


def attention_kernel(
    block, query, own_key, own_value, memory_key, memory_value, parts_in, tokens, gain, keys, seg_cols, seg_rows, w_out,
    attended, totals, mixed, hidden, both,
):
    micro = query.shape[0] // block
    w_out.start()

    @pl.loop(0, micro)
    def _(at):
        before, here = masks(seg_cols, seg_rows, at, block)
        rows = pl.ds(at * block, block)
        lane = iota((block, LANES), 1)
        tops = jnp.zeros((block, LANES), jnp.float32)
        for head in range(HEADS):
            cols = slice(head * LANES, (head + 1) * LANES)
            q = query[rows, cols]
            s_before = scores(q, memory_key[rows, cols], before)
            s_here = scores(q, own_key[rows, cols], here)
            top = jnp.maximum(
                jnp.max(s_before, axis=-1, keepdims=True), jnp.max(s_here, axis=-1, keepdims=True)
            )
            e_before, e_here = jnp.exp(s_before - top), jnp.exp(s_here - top)
            total = jnp.sum(e_before, axis=-1, keepdims=True) + jnp.sum(
                e_here, axis=-1, keepdims=True
            )
            share = 1.0 / total
            seen = product((e_before * share).astype(jnp.bfloat16), memory_value[rows, cols])
            seen += product((e_here * share).astype(jnp.bfloat16), own_value[rows, cols])
            attended[rows, cols] = seen.astype(jnp.bfloat16)
            tops = jnp.where(lane == head, top + jnp.log(total), tops)
        totals[rows, :] = tops

    parts = parts_in[...]
    seen = attended[...]
    total = tokens[...].astype(jnp.float32)
    for at, size in pieces_of(MIX):
        spread = product(seen, spread_block(keys, at, size))
        weight = product(parts, expert_block(keys, at, size, 2 * GATES, True))
        piece = (spread * weight).astype(jnp.bfloat16)
        mixed[:, at : at + size] = piece
        total += product(piece, w_out.rows(at, size))
    mixed[:, MIX:] = jnp.zeros((mixed.shape[0], mixed.shape[1] - MIX), jnp.bfloat16)
    hidden[...] = total
    low = normalise(total, gain[...].astype(jnp.float32)).astype(jnp.bfloat16)
    both[:, : low.shape[1]] = low
    both[:, low.shape[1] :] = seen


def units_up_kernel(group, side, normed, w_up, d_down, w_down, upper, d_pre, theirs):
    pre = product(normed[...], w_up[...])
    back = product_nt(d_down[...], w_down[...])
    cdf = 0.5 * (1.0 + lax.erf(pre * (1.0 / math.sqrt(2.0))))
    high = (pre * cdf).astype(jnp.bfloat16)
    upper[...] = high
    slope = cdf + pre * (jnp.exp(-0.5 * pre * pre) * (1.0 / math.sqrt(2.0 * math.pi)))
    d_pre[...] = (back * slope).astype(jnp.bfloat16)
    for number in range(2):

        @pl.when(side[0] == number)
        def _():
            for at in range(0, high.shape[1], 2 * group):
                start = at + (1 - number) * group
                theirs[:, at // 2 : at // 2 + group] = high[:, start : start + group]


class Arrival:
    def __init__(self, source, target, sem):
        self.copy = pltpu.make_async_copy(source, target, sem)

    def start(self):
        self.copy.start()

    def wait(self):
        self.copy.wait()


def units_back_kernel(
    d_pre, w_up, hidden_at, d_down_at, gain, src, d_hidden, d_branch, theirs, total, hidden, d_down, sems
):
    at = pl.program_id(0)
    arrivals = (
        Arrival(hidden_at, hidden, sems.at[0]),
        Arrival(d_down_at, d_down, sems.at[1]),
    )

    @pl.when(at == 0)
    def _():
        for arrival in arrivals:
            arrival.start()

    back = product_nt(d_pre[...], w_up[...])

    @pl.when(at == 0)
    def _():
        total[...] = back

    @pl.when(at > 0)
    def _():
        total[...] += back

    @pl.when(at == pl.num_programs(0) - 1)
    def _():
        for arrival in arrivals:
            arrival.wait()
        grad = normalise_back(hidden[...], gain[...].astype(jnp.float32), total[...])
        grad = d_down[...].astype(jnp.float32) + grad
        d_hidden[...] = grad
        branch = grad.astype(jnp.bfloat16)
        d_branch[...] = branch
        shape = src.shape[0], branch.shape[1]
        picks = ones_where(src[...] == iota(shape, 1))
        theirs[...] = product_nt(branch, picks).astype(jnp.bfloat16)


def result_kernel(upper, w_down, hidden, result, total):
    at = pl.program_id(0)
    forth = product(upper[...], w_down[...])

    @pl.when(at == 0)
    def _():
        total[...] = hidden[...] + forth

    @pl.when(at > 0)
    def _():
        total[...] += forth

    @pl.when(at == pl.num_programs(0) - 1)
    def _():
        result[...] = total[...].astype(jnp.bfloat16)


def attention_back_kernel(
    block, d_branch, w_out, gates, parts_in, attended, query, own_key, own_value, memory_key,
    memory_value, totals, experts, keys,
    seg_cols, seg_rows, small,
    d_seen, d_query, d_key,
):
    w_out.start()
    branch, seen, gate, parts = d_branch[...], attended[...], gates[...], parts_in[...]
    to_seen = jnp.zeros((branch.shape[0], WIDE), jnp.float32)
    to_gate = jnp.zeros((branch.shape[0], LANES), jnp.float32)
    for at, size in pieces_of(MIX):
        d_mixed = product_nt(branch, w_out.rows(at, size))
        if at == 0:
            for operand in (query, own_key, own_value, memory_key, memory_value, totals, experts):
                operand.start()
        spread = spread_block(keys, at, size)
        weight = product(parts, expert_block(keys, at, size, 2 * GATES, True))
        to_seen += product_low(d_mixed * weight, spread)
        to_gate += product_low(
            d_mixed * product(seen, spread), expert_block(keys, at, size, 2 * GATES, False)
        )
    d_seen[...] = to_seen.astype(jnp.bfloat16)
    query, own_key, own_value = query.all(), own_key.all(), own_value.all()
    memory_key, memory_value, totals = memory_key.all(), memory_value.all(), totals.all()
    micro = query.shape[0] // block

    @pl.loop(0, micro)
    def _(at):
        before, here = masks(seg_cols, seg_rows, at, block)
        rows = pl.ds(at * block, block)
        tops = totals[rows, :]
        for head in range(HEADS):
            cols = slice(head * LANES, (head + 1) * LANES)
            q, grad = query[rows, cols], d_seen[rows, cols]
            k_before, k_here = memory_key[rows, cols], own_key[rows, cols]
            top = tops[:, head : head + 1]
            p_before = jnp.exp(scores(q, k_before, before) - top)
            p_here = jnp.exp(scores(q, k_here, here) - top)
            g_before = product_nt(grad, memory_value[rows, cols])
            g_here = product_nt(grad, own_value[rows, cols])
            delta = jnp.sum(p_before * g_before, axis=-1, keepdims=True) + jnp.sum(
                p_here * g_here, axis=-1, keepdims=True
            )
            s_before = (p_before * (g_before - delta)).astype(jnp.bfloat16)
            s_here = (p_here * (g_here - delta)).astype(jnp.bfloat16)
            to_query = product(s_before, k_before) + product(s_here, k_here)
            d_query[rows, cols] = (to_query * HEAD ** (-0.5)).astype(jnp.bfloat16)
            to_key = product_tn(s_here, q) * HEAD ** (-0.5)
            d_key[rows, cols] = to_key.astype(jnp.bfloat16)
            to_value = product_tn(p_here.astype(jnp.bfloat16), grad)
            small[rows, cols] = to_value.astype(jnp.bfloat16)

    d_value = small[:, :WIDE]
    experts = experts.all()
    for at, size in pieces_of(MIX):
        to_gate += product_low(
            product(d_value, spread_block(keys, at, size)) * experts[:, at : at + size],
            expert_block(keys, at, size, 0, False),
        )
    small[:, WIDE:QK_AT] = (to_gate * gate * (1.0 - gate)).astype(jnp.bfloat16)
    both = (WIDE, 2 * HEADS * HEAD)
    from_query = ones_where(iota(both, 0) == keys[2:3, : both[1]])
    from_key = ones_where(iota(both, 0) == keys[3:4, : both[1]])
    total = product(d_query[...], from_query) + product(d_key[...], from_key)
    small[:, QK_AT:] = total.astype(jnp.bfloat16)


QK_AT = WIDE + LANES
V_AT = 0
Q_AT = -(-MIX // LANES) * LANES
K_AT = Q_AT + HEADS * HEAD
G_AT = K_AT + HEADS * HEAD
IN_COLUMNS = G_AT + LANES


def d_experts(small, parts, keys, at, size):
    spread = product(small[:, :WIDE], spread_block(keys, at, size))
    weight = product(parts[...], expert_block(keys, at, size, 0, True))
    return (spread * weight).astype(jnp.bfloat16)


def put_into(refs, half):
    def put(number, at, total):
        total = in_order(number, total.astype(jnp.bfloat16))
        keep = total.shape[0] // 2
        columns = slice(at - number * half, at - number * half + total.shape[1])
        refs[2 * number][:, columns] = total[:keep]
        refs[2 * number + 1][:, columns] = total[keep:]

    return put


def halves_of(total, half):
    for number in range(2):
        at, stop = number * half, min(total, (number + 1) * half)
        while at < stop:
            size = min(CHUNK, stop - at)
            yield number, at, size
            at += size


def wide_kernel(
    src, keys, left_at, second_at, right_at, right_came_at, branch_at, branch_came_at, mixed_at, both_at,
    *refs,
):
    made, held = refs[:4], refs[4:14]
    left, second_came, right, right_came, branch, branch_came, mixed, parts_came = held[:8]
    turned, turned_branch = held[8:10]
    buffers, sems, out_sems = refs[14:18], refs[18], refs[19]
    tokens, width = left.shape
    left_came, seen_came = second_came.at[:, :width], second_came.at[:, width:]
    step = 2 * CHUNK
    ups, outs = right.shape[1] // 2, mixed.shape[1] // 2
    first = [
        Arrival(left_at.at[:, pl.ds(0, width)], left, sems.at[0]),
        Arrival(second_at, second_came, sems.at[1]),
    ]
    rights = []
    for number in range(2 * ups // step):
        columns = pl.ds(number * step, step)
        rights.append(
            [
                Arrival(right_at.at[:, columns], right.at[:, columns], sems.at[2 + 2 * number]),
                Arrival(right_came_at.at[:, columns], right_came.at[:, columns], sems.at[3 + 2 * number]),
            ]
        )
    at = 2 + 2 * len(rights)
    lanes = pl.ds(both_at.shape[1] - LANES, LANES)
    others = [
        Arrival(branch_at, branch, sems.at[at]),
        Arrival(branch_came_at, branch_came, sems.at[at + 1]),
        Arrival(both_at.at[:, lanes], parts_came, sems.at[at + 2]),
        Arrival(mixed_at, mixed, sems.at[at + 3]),
    ]
    for arrival in first:
        arrival.start()
    for arrival in first:
        arrival.wait()
    half = len(rights) // 2
    for arrival in sum(rights[:half], []) + others + sum(rights[half:], []):
        arrival.start()
    turn(src[...], (left, left_came), turned)
    leaving = []

    def leave(number, columns):
        for which in (2 * number, 2 * number + 1):
            copy = pltpu.make_async_copy(
                buffers[which].at[:, columns], made[which].at[:, columns], out_sems.at[len(leaving)]
            )
            copy.start()
            leaving.append(copy)

    for number in range(2):

        def put(at, total):
            total = in_order(number, total.astype(jnp.bfloat16))
            keep = total.shape[0] // 2
            columns = slice(at, at + total.shape[1])
            buffers[2 * number][:, columns] = total[:keep]
            buffers[2 * number + 1][:, columns] = total[keep:]

        for place in range(ups // step):
            for arrival in rights[number * half + place]:
                arrival.wait()
            columns = slice(number * ups + place * step, number * ups + (place + 1) * step)
            total = product(turned[:, :tokens], right[:, columns])
            put(place * step, total + product(turned[:, tokens:], right_came[:, columns]))
        leave(number, pl.ds(0, ups))
        if number == 0:
            for arrival in others:
                arrival.wait()
            turn(src[...], (branch, branch_came), turned_branch)
        at, stop = 0, min(outs, MIX - number * outs)
        while at < stop:
            size = min(CHUNK, stop - at)
            start = number * outs + at
            spread = product(seen_came[...], spread_block(keys, start, size))
            weight = product(parts_came[...], expert_block(keys, start, size, 2 * GATES, True))
            came = (spread * weight).astype(jnp.bfloat16)
            total = product(turned_branch[:, :tokens], mixed[:, start : start + size])
            put(ups + at, total + product(turned_branch[:, tokens:], came))
            at += size
        if at < outs:
            put(ups + at, jnp.zeros((turned.shape[0], outs - at), jnp.float32))
        leave(number, pl.ds(ups, outs))
    for copy in leaving:
        copy.wait()


def gradient_wide(src, left, right, branch, mixed, both_came, keys):
    tokens, rows = left[0].shape[0], src.shape[0]
    ups, outs = right[0].shape[1] // 2, mixed.shape[1] // 2
    copied = (*left, *right, *branch, mixed, both_came)
    shape = (rows // 2, ups + outs)
    held = [pltpu.VMEM(array.shape, array.dtype) for array in copied[:-1]]
    held[0] = pltpu.VMEM((tokens, branch[0].shape[1]), jnp.bfloat16)
    held.append(pltpu.VMEM((tokens, LANES), jnp.bfloat16))
    arrivals = 2 + 2 * (2 * ups // (2 * CHUNK)) + 4
    return pl.pallas_call(
        wide_kernel,
        in_specs=[pl.BlockSpec(memory_space=pltpu.VMEM)] * 2
        + [pl.BlockSpec(memory_space=pl.ANY)] * len(copied),
        out_specs=[pl.BlockSpec(memory_space=pl.ANY)] * 4,
        out_shape=[jax.ShapeDtypeStruct(shape, jnp.bfloat16)] * 4,
        scratch_shapes=held
        + [pltpu.VMEM((rows, 2 * tokens), jnp.bfloat16)] * 2
        + [pltpu.VMEM(shape, jnp.bfloat16)] * 4
        + [pltpu.SemaphoreType.DMA((arrivals,)), pltpu.SemaphoreType.DMA((8,))],
        compiler_params=pltpu.CompilerParams(vmem_limit_bytes=GRADIENT),
        cost_estimate=BRIEF,
    )(src, keys, *copied)


def inputs_kernel(
    src, left, both_came, small, small_came, parts, keys, *refs,
):
    turned = refs[-1]
    half = IN_COLUMNS // 2
    tokens, width = left.shape
    left_came = both_came.at[:, width : 2 * width]
    parts_came = both_came.at[:, 2 * width :]
    put = put_into(refs, half)

    def times(one, two):
        return product(turned[:, :tokens], one) + product(turned[:, tokens:], two)

    turn(src[...], (left, left_came), turned)
    for number, at, size in halves_of(MIX, half):
        one = d_experts(small, parts, keys, at, size)
        two = d_experts(small_came, parts_came, keys, at, size)
        put(number, at, times(one, two))
    put(1, MIX, jnp.zeros((turned.shape[0], Q_AT - MIX), jnp.float32))
    for at in range(0, 2 * HEADS * HEAD, CHUNK):
        columns = slice(QK_AT + at, QK_AT + min(at + CHUNK, 2 * HEADS * HEAD))
        put(1, Q_AT + at, times(small[:, columns], small_came[:, columns]))
    put(1, G_AT, times(small[:, WIDE:QK_AT], small_came[:, WIDE:QK_AT]))


def inputs_back_kernel(
    small, parts, keys, tokens, d_hidden, gain, w_gates, w_key, w_value,
    w_query, places, input_grad, own_in, w_both,
):
    w_value.start()
    size = HEADS * HEAD
    w_both[:size, :] = w_query[...]
    w_both[size:, :] = w_key[...]
    total = product(small[:, WIDE:QK_AT], w_gates[...])
    total += product(small[:, QK_AT:], w_both[...])
    tokens.start()
    d_hidden.start()
    for at, size in pieces_of(MIX):
        total += product(d_experts(small, parts, keys, at, size), w_value.rows(at, size))
    picks = ones_where(places[...] == iota((places.shape[0], tokens.shape[1]), 1))
    for at, weight in ((V_AT, w_value.all()), (Q_AT, w_both), (G_AT, w_gates)):
        own = product_nt(picks, weight[...]).astype(jnp.bfloat16)
        own_in[:, at : at + own.shape[1]] = own
    own_in[:, MIX:Q_AT] = jnp.zeros((places.shape[0], Q_AT - MIX), jnp.bfloat16)
    grad = normalise_back(tokens.all()[...].astype(jnp.float32), gain[...].astype(jnp.float32), total)
    input_grad[...] = (d_hidden.all()[...] + grad).astype(jnp.bfloat16)


def pieced(generate, outs, aligned, *operands):
    if not aligned:
        results = [jnp.zeros(shape, dtype) for shape, dtype in outs]
        for number, row, column, value in generate(*operands):
            value = value.astype(results[number].dtype)
            results[number] = lax.dynamic_update_slice(results[number], value, (row, column))
        return results

    def kernel(*refs):
        given, made = refs[: len(operands)], refs[len(operands) :]
        for number, row, column, value in generate(*given):
            rows, columns = slice(row, row + value.shape[0]), slice(column, column + value.shape[1])
            made[number][rows, columns] = value.astype(made[number].dtype)

    return whole(kernel, outs, *operands, grant=FULL)


def summed(pair, rows, columns=slice(None)):
    return sum(part[rows, columns].astype(jnp.float32) for part in pair)


def forked(kept, came):
    columns, rows = kept.shape[1] // 2, kept.shape[0] // 2
    for number in range(2):
        own = slice(number * columns, (number + 1) * columns)
        for half in range(2):
            part = slice(half * rows, (half + 1) * rows)
            yield 2 * number + half, 0, 0, summed((kept, came), part, own)


def paired_halves(*refs):
    for number in range(2):
        column = 0
        own = refs[number * len(refs) // 2 : (number + 1) * len(refs) // 2]
        for pair in zip(own[::2], own[1::2]):
            rows = pair[0].shape[0] // 2
            for half in range(2):
                part = slice(half * rows, (half + 1) * rows)
                yield 2 * number + half, 0, column, summed(pair, part)
            column += pair[0].shape[1]


def laid_out(layout, *refs):
    for number, start, size, column in layout:
        pair = refs[2 * number : 2 * number + 2]
        rows = pair[0].shape[0] // 2
        for half in range(2):
            part = slice(half * rows, (half + 1) * rows)
            yield half, 0, column, summed(pair, part, slice(start, start + size))


def as_row(column):
    size = column.shape[0]
    return jnp.sum(jnp.where(iota((size, size), 0) == iota((size, size), 1), column, 0.0), 0, keepdims=True)


def as_row(column):
    size = column.shape[0]
    return jnp.sum(jnp.where(iota((size, size), 0) == iota((size, size), 1), column, 0.0), 0, keepdims=True)


def last_halves(width, wide_size, *refs):
    rows = refs[0].shape[0] // 2
    for half in range(2):
        part = slice(half * rows, (half + 1) * rows)
        yield half, 0, 0, summed(refs[:2], part, slice(0, wide_size))
        if len(refs) == 2:
            blocks = (refs[0].shape[1] - wide_size) // width // 2
            for block in range(blocks):
                at = wide_size + (half * blocks + block) * width
                for low in range(2):
                    value = summed(refs, slice(low * rows, (low + 1) * rows), slice(at, at + width))
                    yield half, 0, wide_size + (2 * block + low) * width, value
            continue
        for number in range(2):
            pair = refs[2 + 2 * number : 4 + 2 * number]
            tall = pair[0].shape[0] // 2
            for block in range(tall // rows):
                at = half * tall + block * rows
                yield half, 0, wide_size + block * width + number * width // 2, summed(
                    pair, slice(at, at + rows)
                )


def most_done(weight, gain, down, down_came, wide, wide_came):
    yield 0, 0, 0, summed((down, down_came), slice(None))
    along = 0.0
    for at in range(0, HIDDEN, 2 * CHUNK):
        columns = slice(at, at + 2 * CHUNK)
        piece = summed((wide, wide_came), slice(None), columns)
        yield 1, 0, at, piece
        along += jnp.sum(piece * weight[:, columns].astype(jnp.float32), axis=1, keepdims=True)
    yield 2, 0, 0, as_row(along / gain[:, :])
    yield 3, 0, 0, summed((wide, wide_came), slice(None), slice(HIDDEN, HIDDEN + MIX))


def in_done(weight, gain, *refs):
    total = summed(refs, slice(None))
    for number, (at, size) in enumerate(((Q_AT, HEADS * HEAD), (K_AT, HEADS * HEAD), (V_AT, MIX))):
        yield number, 0, 0, total[:, at : at + size]
    gates = total[:, G_AT:].T
    yield 3, 0, 0, gates[:GATES]
    yield 4, 0, 0, gates[2 * GATES : 3 * GATES]
    along = jnp.sum(total * weight[:, :].astype(jnp.float32), axis=1, keepdims=True)
    yield 5, 0, 0, as_row(along / gain[:, :])


class Late:
    def __init__(self, source, target, sems):
        self.source, self.target, self.sems = source, target, sems
        self.shape, self.copies = target.shape, None

    def start(self):
        if len(self.shape) == 3:
            self.copies = [pltpu.make_async_copy(self.source, self.target, self.sems.at[0])]
        else:
            self.copies = [
                pltpu.make_async_copy(
                    self.source.at[pl.ds(at, size)], self.target.at[pl.ds(at, size)], self.sems.at[number]
                )
                for number, (at, size) in enumerate(pieces_of(self.shape[0]))
            ]
        for copy in self.copies:
            copy.start()

    def rows(self, at, size):
        number = at // CHUNK
        if self.copies[number] is not None:
            self.copies[number].wait()
            self.copies[number] = None
        return self.target[at : at + size]

    def all(self):
        for number, copy in enumerate(self.copies):
            if copy is not None:
                copy.wait()
                self.copies[number] = None
        return self.target


def whole(kernel, outs, *operands, scratch=(), grant=VMEM, late=()):
    outs = [jax.ShapeDtypeStruct(shape, dtype) for shape, dtype in outs]
    given, made, kept = len(operands), len(outs), len(scratch)
    buffers = [pltpu.VMEM(operands[number].shape, operands[number].dtype) for number in late]
    sems = [pltpu.SemaphoreType.DMA((len(pieces_of(operands[number].shape[-2])),)) for number in late]

    def run(*refs):
        refs = list(refs)
        extra = refs[given + made + kept :]
        for place, number in enumerate(late):
            refs[number] = Late(refs[number], extra[place], extra[len(late) + place])
        kernel(*refs[: given + made + kept])

    specs = [
        pl.BlockSpec(memory_space=pl.ANY if number in late else pltpu.VMEM) for number in range(given)
    ]
    return pl.pallas_call(
        run,
        out_shape=outs,
        in_specs=specs,
        out_specs=[pl.BlockSpec(memory_space=pltpu.VMEM)] * made,
        scratch_shapes=list(scratch) + buffers + sems,
        compiler_params=pltpu.CompilerParams(vmem_limit_bytes=grant),
        cost_estimate=BRIEF,
    )(*operands)


def body(
    tokens,
    segments,
    value_experts,
    out_experts,
    norm_gain,
    w_query,
    w_key,
    w_value,
    w_vgate,
    w_ogate,
    w_out,
    ffn_gain,
    w_up,
    w_down,
    cotangent,
):
    grid = Grid()
    first, second = grid.plane_a, grid.plane_b
    row_order = grid.order([first, second, *grid.rest])
    unit_orders = jnp.stack(
        [
            grid.order([grid.rest[0], first, second, *grid.rest[1:]]),
            grid.order([grid.rest[0], second, first, *grid.rest[1:]]),
        ]
    )
    micro, _, block, width = tokens.shape
    rows = micro * block
    hidden_units = w_up.shape[1]
    place = lax.axis_index("seq")
    own_segs = lax.dynamic_slice_in_dim(segments, place * block, block, 2)[:, 0]
    prior_start = jnp.maximum(place - 1, 0) * block
    prior_segs = jnp.where(
        place > 0, lax.dynamic_slice_in_dim(segments, prior_start, block, 2)[:, 0], -1
    )
    gain_one, gain_two = norm_gain[None], ffn_gain[None]
    column = np.arange(-(-MIX // LANES) * LANES)
    head_column = np.arange(WIDE)
    keys = np.full((4, column.size), -1, np.int32)
    keys[0, :MIX] = (column // (EXPERTS * HEAD) * LANES + column % HEAD)[:MIX]
    keys[1, :MIX] = (column // HEAD)[:MIX]
    keys[2, : HEADS * HEAD] = (head_column // HEAD * LANES + head_column % HEAD)[: HEADS * HEAD]
    keys[3, HEADS * HEAD : 2 * HEADS * HEAD] = keys[2, : HEADS * HEAD]
    keys = jnp.asarray(keys)
    lane = np.arange(4 * GATES)
    slots = np.zeros((2 * 16 + 8, LANES), np.float32)
    source = 2 * (lane % GATES // EXPERTS) + 2 * HEADS * (lane // (2 * GATES))
    slots[source, lane] = 1
    slots[16 + source + 1, lane] = 1
    slots[32] = -1
    slots[32, : 4 * GATES] = lane % EXPERTS
    slots = jnp.asarray(slots, jnp.bfloat16)
    value_picks, out_picks = (
        jnp.transpose(picks[:, 0], (0, 2, 3, 1))
        for picks in (value_experts, out_experts)
    )
    w_query, w_key, w_value = w_query.T, w_key.T, w_value.T
    share = width // grid.count

    def own_rows(array):
        return lax.dynamic_slice_in_dim(array, grid.me * share, share, 0)

    seg_cols = own_segs.reshape(rows, 1)
    seg_rows = jnp.stack([prior_segs, own_segs], 1)

    field = tokens.reshape(rows, width)
    d_down = cotangent.reshape(rows, width)
    low, full = jnp.bfloat16, jnp.float32
    normed, key = whole(
        key_kernel, [((rows, width), low), ((rows, WIDE), low)], field, gain_one, keys, w_key
    )
    memory_key = passed_along(key, "seq", 1)
    gates, parts, experts, value, w_gates = whole(
        value_kernel,
        [
            ((rows, LANES), full),
            ((rows, LANES), low),
            ((rows, MIX), low),
            ((rows, WIDE), low),
            ((LANES, width), low),
        ],
        after(normed, key), keys, slots, value_picks, out_picks, w_vgate.T, w_ogate.T, w_value,
        late=(7,),
        scratch=[pltpu.VMEM((rows, LANES), full)] * 2,
    )
    memory_value = passed_along(value, "seq", 1)
    own_memory = key, value, memory_key, memory_value

    def paired(value):
        return value, grid.swap(value, grid.core)

    step = 1024
    fixed = pl.BlockSpec((rows, width), lambda j: (0, 0))
    across = pl.BlockSpec((rows, step), lambda j: (0, j))
    up_block = pl.BlockSpec((width, step), lambda j: (0, j))
    down_block = pl.BlockSpec((step, width), lambda j: (j, 0))
    row_block = pl.BlockSpec((1, width), lambda j: (0, 0))

    anywhere = pl.BlockSpec(memory_space=pl.ANY)

    def stepped(kernel, in_specs, out_specs, outs, operands, products, scratch=0, more=()):
        return pl.pallas_call(
            kernel,
            grid=(hidden_units // step,),
            in_specs=in_specs,
            out_specs=out_specs,
            out_shape=[jax.ShapeDtypeStruct(shape, dtype) for shape, dtype in outs],
            scratch_shapes=[pltpu.VMEM((rows, width), full)] * scratch + list(more),
            compiler_params=pltpu.CompilerParams(vmem_limit_bytes=VMEM),
            cost_estimate=BRIEF,
        )(*operands)

    query, both = whole(
        query_kernel,
        [((rows, WIDE), low), ((rows, 2 * width + LANES), low)],
        after(normed, value, memory_key, seg_cols, seg_rows), keys, w_query, d_down, parts,
    )
    both_came = grid.swap(after(both, memory_value), grid.core)
    down_pair = d_down, both_came
    mixed_columns = -(-MIX // 256) * 256
    attended, totals, mixed, hidden, second_both = whole(
        functools.partial(attention_kernel, block),
        [
            ((rows, WIDE), low),
            ((rows, LANES), full),
            ((rows, mixed_columns), low),
            ((rows, width), full),
            ((rows, width + WIDE), low),
        ],
        query, *own_memory, parts, field, gain_two,
        keys, seg_cols, seg_rows, w_out, late=(11,),
    )
    second_pair = second_both, grid.swap(second_both, grid.core)
    units = hidden_units // grid.count
    side = (grid.me // grid.core) % 2
    upper, d_pre, theirs = pl.pallas_call(
        functools.partial(units_up_kernel, grid.core * units),
        grid_spec=pltpu.PrefetchScalarGridSpec(
            num_scalar_prefetch=1,
            grid=(hidden_units // step,),
            in_specs=[
                pl.BlockSpec((rows, width), lambda j, _: (0, 0)),
                pl.BlockSpec((width, step), lambda j, _: (0, j)),
                pl.BlockSpec((rows, width), lambda j, _: (0, 0)),
                pl.BlockSpec((step, width), lambda j, _: (j, 0)),
            ],
            out_specs=[
                pl.BlockSpec((rows, step), lambda j, _: (0, j)),
                pl.BlockSpec((rows, step), lambda j, _: (0, j)),
                pl.BlockSpec((rows, step // 2), lambda j, _: (0, j)),
            ],
        ),
        out_shape=[
            jax.ShapeDtypeStruct((rows, hidden_units), low),
            jax.ShapeDtypeStruct((rows, hidden_units), low),
            jax.ShapeDtypeStruct((rows, hidden_units // 2), low),
        ],
        compiler_params=pltpu.CompilerParams(vmem_limit_bytes=VMEM),
        cost_estimate=BRIEF,
    )(side.reshape(1), second_both, w_up, after(d_down, both_came), w_down)

    source = (row_order[:, None] * share + jnp.arange(share, dtype=jnp.int32)).reshape(-1, 1)
    within = unit_orders // (2 * grid.core) * grid.core + unit_orders % grid.core
    if units == 128:
        unit_blocks = jnp.stack([unit_orders, within])
        came = grid.swap(theirs, grid.core)
        upper_pair = upper, came
    else:
        place = jnp.arange(units, dtype=jnp.int32)
        half_shards = jnp.arange(grid.count // 2, dtype=jnp.int32)
        half_shards = half_shards // grid.core * (2 * grid.core) + half_shards % grid.core
        half_shards = half_shards + (1 - side) * grid.core
        theirs = upper[:, (half_shards[:, None] * units + place).reshape(-1)]
        came = grid.swap(theirs, grid.core)
        lists = [(o[:, :, None] * units + place).reshape(-1) for o in (unit_orders, within)]
        upper_pair = upper[:, lists[0]], came[:, lists[1]]
        blocks = jnp.arange(hidden_units // 128, dtype=jnp.int32).reshape(2, -1)
        unit_blocks = jnp.stack([blocks, blocks])
    pre_pair = paired(d_pre)

    def plane(parts, one, two):
        return parts[1], grid.swap(parts[0], one), parts[3], grid.swap(parts[2], two)

    aligned = share % 16 == 0

    def stage(generate, rows, widths, gate, *operands):
        outs = [((rows, size), low) for size in widths]
        return pieced(generate, outs, aligned, after(operands[0], *gate), *operands[1:])

    def down_rest(pair, masks, gate, used):
        sent = None
        for mask in masks:
            layout, column = [], 0
            for number in range(len(pair) // 2):
                layout.append((number, 0, used, column))
                column += used
            sent, own = stage(
                functools.partial(laid_out, layout), pair[0].shape[0] // 2, [column] * 2, gate, *pair
            )
            pair, used = (own, grid.swap(sent, mask)), column
            gate = (sent,)
        return pair, sent

    their_order = grid.order([first, second, *grid.rest], grid.core)
    their_source = (their_order[:, None] * share + jnp.arange(share, dtype=jnp.int32)).reshape(-1, 1)
    d_hidden, d_branch, branch_theirs = stepped(
        units_back_kernel,
        [across, up_block, anywhere, anywhere, row_block, pl.BlockSpec(source.shape, lambda j: (0, 0))],
        [fixed, fixed, pl.BlockSpec((rows, width // 2), lambda j: (0, 0))],
        [((rows, width), full), ((rows, width), low), ((rows, width // 2), low)],
        (d_pre, w_up, hidden, d_down, gain_two, their_source),
        1,
        1,
        [pltpu.VMEM((rows, width), full), pltpu.VMEM((rows, width), low), pltpu.SemaphoreType.DMA((2,))],
    )
    wide_parts = gradient_wide(
        source, second_pair, pre_pair, (d_branch, grid.swap(branch_theirs, grid.core)), mixed,
        both_came, keys,
    )
    wide_zero = plane(wide_parts, first, second)
    down_sent, down_kept = gradient_units(
        unit_blocks, (after(upper_pair[0], *wide_parts), upper_pair[1]), down_pair
    )
    down_came = grid.swap(down_sent, grid.rest[0])
    (small,) = whole(
        functools.partial(attention_back_kernel, block),
        [((rows, QK_AT + 2 * HEADS * HEAD), low)],
        after(d_branch, down_sent), w_out, gates, parts, attended, query, *own_memory, totals,
        experts, keys, seg_cols, seg_rows, late=(1, 5, 6, 7, 8, 9, 10, 11),
        scratch=[pltpu.VMEM((rows, WIDE), low)] * 3,
    )
    small_pair = paired(small)

    columns = hidden_units // 2, mixed.shape[1] // 2
    wide_two = stage(
        paired_halves, wide_parts[0].shape[0] // 2, [sum(columns)] * 4, (small,), *wide_zero
    )
    wide_one = plane(wide_two, second, first)
    half = (share * grid.count // 4, IN_COLUMNS // 2)
    in_parts = whole(
        inputs_kernel,
        [(half, low)] * 4,
        source, after(normed, *wide_two), both_came, *small_pair, parts, keys,
        scratch=[pltpu.VMEM((2 * half[0], 2 * rows), low)],
    )
    in_one = plane(in_parts, first, second)
    layout = [
        (0, 0, columns[0], 0),
        (1, 0, columns[0], columns[0]),
        (0, columns[0], columns[1], 2 * columns[0]),
        (1, columns[0], columns[1], 2 * columns[0] + columns[1]),
    ]
    wide_sent, wide_own = stage(
        functools.partial(laid_out, layout), wide_one[0].shape[0] // 2, [2 * sum(columns)] * 2,
        in_parts, *wide_one,
    )
    wide_pair = wide_own, grid.swap(wide_sent, grid.rest[0])
    down_two = stage(
        forked, down_kept.shape[0] // 2, [width // 2] * 4, (wide_sent,), down_kept, down_came
    )
    down_one = plane(down_two, first, second)
    (result,) = stepped(
        result_kernel,
        [across, down_block, fixed],
        [fixed],
        [((rows, width), low)],
        (upper, w_down, after(hidden, *down_two)),
        1,
        1,
    )
    in_two = stage(paired_halves, half[0] // 2, [half[1]] * 4, (result,), *in_one)
    in_pairs = plane(in_two, second, first)
    wide_pair, wide_sent = down_rest(wide_pair, grid.rest[1:], in_two, 2 * sum(columns))
    down_three = stage(
        paired_halves, down_one[0].shape[0] // 2, [width // 2] * 4, (wide_sent,), *down_one
    )
    down_pairs = plane(down_three, second, first)
    down_pair, down_sent = down_rest(down_pairs, grid.rest[1:], down_three, width // 2)
    in_pair, in_sent = down_rest(in_pairs, grid.rest[:1], (down_sent,), in_pairs[0].shape[1])
    places = (grid.me * share + jnp.arange(share, dtype=jnp.int32))[:, None]
    input_grad, own_in = whole(
        inputs_back_kernel,
        [((rows, width), low), ((share, IN_COLUMNS), low)],
        small, parts, keys, field, after(d_hidden, in_sent), gain_one,
        w_gates, w_key, w_value, w_query, places,
        late=(3, 4, 8),
        scratch=[pltpu.VMEM((2 * HEADS * HEAD, width), low)],
    )
    in_pair, in_sent = down_rest(in_pair, grid.rest[1:], (input_grad,), in_pair[0].shape[1])
    own_up = own_rows(w_up)
    own_gain_one = own_rows(norm_gain.astype(jnp.float32))[:, None]
    own_gain_two = own_rows(ffn_gain.astype(jnp.float32))[:, None]
    grad_down, grad_up, grad_gain_two, grad_out_w = pieced(
        most_done,
        [
            ((units, width), full),
            ((share, hidden_units), full),
            ((1, share), full),
            ((share, MIX), full),
        ],
        aligned, after(own_up, in_sent), own_gain_two, *down_pair, *wide_pair,
    )
    shapes = [(share, size) for size in (HEADS * HEAD, HEADS * HEAD, MIX)]
    shapes += [(GATES, share), (GATES, share), (1, share)]
    *grads, grad_vgate, grad_ogate, grad_gain_one = pieced(
        in_done,
        [(shape, full) for shape in shapes],
        aligned, after(own_in, grad_down), own_gain_one, *in_pair,
    )
    return (
        result.reshape(tokens.shape),
        input_grad.reshape(tokens.shape),
        grad_gain_one[0],
        *grads,
        grad_vgate.T,
        grad_ogate.T,
        grad_out_w.T,
        grad_gain_two[0],
        grad_up,
        grad_down,
    )


def solution(mesh):
    both = ("seq", "batch")
    stream = P(None, "batch", "seq", None)
    picks = P(None, "batch", "seq", None, None)
    return jax.shard_map(
        body,
        mesh=mesh,
        in_specs=(stream, P(None, "batch", None), picks, picks) + (P(),) * 10 + (stream,),
        out_specs=(
            stream,
            stream,
            P(both),
            P(both, None),
            P(both, None),
            P(both, None),
            P(both, None),
            P(both, None),
            P(None, both),
            P(both),
            P(both, None),
            P(both, None),
        ),
        check_vma=False,
    )
```

```python
import functools
import math

import jax
import jax.numpy as jnp
import numpy as np
from jax import lax
from jax.experimental import pallas as pl
from jax.experimental.pallas import tpu as pltpu
from jax.sharding import PartitionSpec as P

HEADS = 4
HEAD = 112
EXPERTS = 5

eps = 1e-06
VMEM = 56 << 20
FULL = 30 << 20
GRADIENT = 48 << 20
HIDDEN = 4096
BRIEF = pl.CostEstimate(flops=1024, bytes_accessed=1024, transcendentals=0)


def product(left, right):
    return jnp.dot(left, right, preferred_element_type=jnp.float32)


def product_tn(left, right):
    return lax.dot_general(
        left, right, (((0,), (0,)), ((), ())), preferred_element_type=jnp.float32
    )


def product_nt(left, right):
    return lax.dot_general(
        left, right, (((1,), (1,)), ((), ())), preferred_element_type=jnp.float32
    )


def passed_along(value, axis, steps):
    count = lax.axis_size(axis)
    initial, last = (max(0, -steps), min(count, count - steps))
    return lax.ppermute(value, axis, [(source, source + steps) for source in range(initial, last)])


class Grid:
    def __init__(self):
        self.seq, self.batch = lax.axis_size("seq"), lax.axis_size("batch")
        self.count = self.seq * self.batch
        low = self.batch.bit_length() - 1
        self.core, self.plane_a, self.plane_b = 1 << low, 1, 2 << low
        taken = self.core | self.plane_a | self.plane_b
        self.rest = [1 << at for at in range(self.count.bit_length() - 1) if not (1 << at) & taken]
        self.me = lax.axis_index("seq") * self.batch + lax.axis_index("batch")

    def swap(self, value, mask):
        both = ("seq", "batch")
        return lax.ppermute(value, both, [(i, i ^ mask) for i in range(self.count)])

    def order(self, bits, base=0):
        masks = [base]
        for bit in bits:
            masks = [mask | own for mask in masks for own in (bit, 0)]
        return self.me ^ jnp.array(masks, jnp.int32)


def after(value, *others):
    return lax.optimization_barrier((value,) + others)[0]


def in_order(order, total):
    if order == 0:
        return total
    size = total.shape[0] // 4
    parts = [total[i * size : (i + 1) * size] for i in (0, 2, 1, 3)]
    return jnp.concatenate(parts, 0)


def turn(src, parts, turned):
    at = 0
    for part in parts:
        shape = turned.shape[0], part.shape[1]
        picks = iota(shape, 0) if shape[0] == shape[1] else src
        picked = product_nt(ones_where(picks == iota(shape, 1)), part[...]).astype(jnp.bfloat16)
        turned[:, at : at + part.shape[0]] = picked
        at += part.shape[0]


def units_kernel(order_ref, left, left_came, right, right_came, *outs):
    order, at = pl.program_id(0), pl.program_id(1)
    blocks = order_ref.shape[2] // 2

    def chosen(number, ref):
        return jnp.concatenate(
            [
                ref[:, pl.ds(pl.multiple_of(order_ref[number, order, at * blocks + i] * 128, 128), 128)]
                for i in range(blocks)
            ],
            1,
        )

    total = product_tn(chosen(0, left), right[...]) + product_tn(chosen(1, left_came), right_came[...])
    total = total.astype(jnp.bfloat16)
    for number in range(2):

        @pl.when(at == number)
        def _():
            outs[number][...] = total


def gradient_units(order, left, right):
    tokens = left[0].shape[0]
    rows, columns = order.shape[2] * 128, right[0].shape[1] // 2
    moving = pl.BlockSpec((tokens, columns), lambda o, j, *_: (0, o))
    in_specs = [pl.BlockSpec(part.shape, lambda o, j, *_: (0, 0)) for part in left] + [moving] * 2
    return pl.pallas_call(
        units_kernel,
        grid_spec=pltpu.PrefetchScalarGridSpec(
            num_scalar_prefetch=1,
            grid=(2, 2),
            in_specs=in_specs,
            out_specs=[pl.BlockSpec((rows // 2, columns), lambda o, j, *_: (0, o))] * 2,
        ),
        out_shape=[jax.ShapeDtypeStruct((rows // 2, 2 * columns), jnp.bfloat16)] * 2,
        compiler_params=pltpu.CompilerParams(vmem_limit_bytes=GRADIENT),
        cost_estimate=BRIEF,
    )(order, *left, *right)


def product_low(value, right):
    return product_nt(value.astype(jnp.bfloat16), right)


def ones_where(condition):
    return jnp.where(condition, 1.0, 0.0).astype(jnp.bfloat16)


def iota(shape, dimension):
    return lax.broadcasted_iota(jnp.int32, shape, dimension)


LANES = 128
WIDE = HEADS * LANES
MIX = HEADS * EXPERTS * HEAD
GATES = HEADS * EXPERTS
CHUNK = 512


def pieces_of(total):
    return [(at, min(CHUNK, total - at)) for at in range(0, total, CHUNK)]


def spread_block(keys_ref, at, size):
    return ones_where(iota((WIDE, size), 0) == keys_ref[0:1, at : at + size])


def expert_block(keys_ref, at, size, start, twice):
    lane, own = iota((LANES, size), 0), keys_ref[1:2, at : at + size]
    hit = lane == own + start
    if twice:
        hit = hit | (lane == own + (start + GATES))
    return ones_where(hit)


def gate_parts(gates):
    lane = iota(gates.shape, 1)
    high = gates.astype(jnp.bfloat16).astype(jnp.float32)
    low = ((lane >= GATES) & (lane < 2 * GATES)) | (lane >= 3 * GATES)
    return jnp.where(low, gates - high, high).astype(jnp.bfloat16)


def pad_heads(keys_ref, size):
    return ones_where(iota((WIDE, size), 0) == keys_ref[2:3, 0:size])


def normalise(field, gain):
    factor = lax.rsqrt(jnp.mean(field * field, axis=-1, keepdims=True) + eps)
    return field * factor * gain


def normalise_back(field, gain, grad):
    factor = lax.rsqrt(jnp.mean(field * field, axis=-1, keepdims=True) + eps)
    weighted = grad * gain
    field_grad = factor * weighted - field * factor**3 * jnp.mean(
        weighted * field, axis=-1, keepdims=True
    )
    return field_grad


def key_kernel(tokens, gain, keys, w_key, normed_out, key):
    normed = normalise(tokens[...].astype(jnp.float32), gain[...].astype(jnp.float32))
    normed = normed.astype(jnp.bfloat16)
    normed_out[...] = normed
    own = product_nt(normed, w_key[...]).astype(jnp.bfloat16)
    key[...] = product_nt(own, pad_heads(keys, own.shape[1])).astype(jnp.bfloat16)


def value_kernel(
    normed_in, keys, slots, value_picks, out_picks, w_vgate, w_ogate, w_value,
    gates_out, parts_out, experts, value, w_gates,
    one, two,
):
    w_value.start()
    normed = normed_in[...]
    lane, gate = iota((LANES, GATES), 0), iota((LANES, GATES), 1)
    for_values = ones_where((lane == gate) | (lane == gate + GATES))
    for_outs = ones_where((lane == gate + 2 * GATES) | (lane == gate + 3 * GATES))
    low = product(for_values, w_vgate[...]) + product(for_outs, w_ogate[...])
    w_gates[...] = low.astype(jnp.bfloat16)
    logits = product_nt(normed, w_gates[...])
    count = 4 * HEADS
    block = value_picks.shape[3]
    for micro in range(value_picks.shape[0]):
        rows = slice(micro * block, (micro + 1) * block)
        for start, chosen in enumerate((value_picks, out_picks)):
            for head in range(HEADS):
                picks = chosen[micro, head].astype(jnp.float32).astype(jnp.bfloat16)
                at = 2 * (start * HEADS + head)
                first = product_tn(picks, slots[at : at + 2, :])
                second = product_tn(picks, slots[count + at : count + at + 2, :])
                one[rows, :] = first if at == 0 else one[rows, :] + first
                two[rows, :] = second if at == 0 else two[rows, :] + second
    number = slots[2 * count : 2 * count + 1, :].astype(jnp.float32)
    hit = (one[...] == number) | (two[...] == number)
    gates = jnp.where(hit, jax.nn.sigmoid(logits), 0.0)
    gates_out[...] = gates
    parts = gate_parts(gates)
    parts_out[...] = parts
    total = jnp.zeros((normed.shape[0], WIDE), jnp.float32)
    for at, size in pieces_of(MIX):
        own = product_nt(normed, w_value.rows(at, size))
        experts[:, at : at + size] = own.astype(jnp.bfloat16)
        weighted = own * product(parts, expert_block(keys, at, size, 0, True))
        total += product_low(weighted, spread_block(keys, at, size))
    value[...] = total.astype(jnp.bfloat16)


def query_kernel(normed, keys, w_query, d_down, parts, query, both):
    own = product_nt(normed[...], w_query[...]).astype(jnp.bfloat16)
    query[...] = product_nt(own, pad_heads(keys, own.shape[1])).astype(jnp.bfloat16)
    width = normed.shape[1]
    both[:, :width] = d_down[...]
    both[:, width : 2 * width] = normed[...]
    both[:, 2 * width :] = parts[...]


def masks(seg_cols, seg_rows, at, block):
    own = seg_cols[pl.ds(at * block, block), :]
    rows = seg_rows[at]
    before = own == rows[0:1]
    here = (own == rows[1:2]) & (iota((block, block), 0) >= iota((block, block), 1))
    return before, here


def scores(query, key, allowed):
    return jnp.where(allowed, product_nt(query, key) * HEAD ** (-0.5), -1e30)


def attention_kernel(
    block, query, own_key, own_value, memory_key, memory_value, parts_in, tokens, gain, keys, seg_cols, seg_rows, w_out,
    attended, totals, mixed, hidden, both,
):
    micro = query.shape[0] // block
    w_out.start()

    @pl.loop(0, micro)
    def _(at):
        before, here = masks(seg_cols, seg_rows, at, block)
        rows = pl.ds(at * block, block)
        lane = iota((block, LANES), 1)
        tops = jnp.zeros((block, LANES), jnp.float32)
        for head in range(HEADS):
            cols = slice(head * LANES, (head + 1) * LANES)
            q = query[rows, cols]
            s_before = scores(q, memory_key[rows, cols], before)
            s_here = scores(q, own_key[rows, cols], here)
            top = jnp.maximum(
                jnp.max(s_before, axis=-1, keepdims=True), jnp.max(s_here, axis=-1, keepdims=True)
            )
            e_before, e_here = jnp.exp(s_before - top), jnp.exp(s_here - top)
            total = jnp.sum(e_before, axis=-1, keepdims=True) + jnp.sum(
                e_here, axis=-1, keepdims=True
            )
            share = 1.0 / total
            seen = product((e_before * share).astype(jnp.bfloat16), memory_value[rows, cols])
            seen += product((e_here * share).astype(jnp.bfloat16), own_value[rows, cols])
            attended[rows, cols] = seen.astype(jnp.bfloat16)
            tops = jnp.where(lane == head, top + jnp.log(total), tops)
        totals[rows, :] = tops

    parts = parts_in[...]
    seen = attended[...]
    total = tokens[...].astype(jnp.float32)
    for at, size in pieces_of(MIX):
        spread = product(seen, spread_block(keys, at, size))
        weight = product(parts, expert_block(keys, at, size, 2 * GATES, True))
        piece = (spread * weight).astype(jnp.bfloat16)
        mixed[:, at : at + size] = piece
        total += product(piece, w_out.rows(at, size))
    mixed[:, MIX:] = jnp.zeros((mixed.shape[0], mixed.shape[1] - MIX), jnp.bfloat16)
    hidden[...] = total
    low = normalise(total, gain[...].astype(jnp.float32)).astype(jnp.bfloat16)
    both[:, : low.shape[1]] = low
    both[:, low.shape[1] :] = seen


def units_up_kernel(group, side, normed, w_up, d_down, w_down, upper, d_pre, theirs):
    pre = product(normed[...], w_up[...])
    back = product_nt(d_down[...], w_down[...])
    cdf = 0.5 * (1.0 + lax.erf(pre * (1.0 / math.sqrt(2.0))))
    high = (pre * cdf).astype(jnp.bfloat16)
    upper[...] = high
    slope = cdf + pre * (jnp.exp(-0.5 * pre * pre) * (1.0 / math.sqrt(2.0 * math.pi)))
    d_pre[...] = (back * slope).astype(jnp.bfloat16)
    for number in range(2):

        @pl.when(side[0] == number)
        def _():
            for at in range(0, high.shape[1], 2 * group):
                start = at + (1 - number) * group
                theirs[:, at // 2 : at // 2 + group] = high[:, start : start + group]


class Arrival:
    def __init__(self, source, target, sem):
        self.copy = pltpu.make_async_copy(source, target, sem)

    def start(self):
        self.copy.start()

    def wait(self):
        self.copy.wait()


def units_back_kernel(
    d_pre, w_up, hidden_at, d_down_at, gain, src, d_hidden, d_branch, theirs, total, hidden, d_down, sems
):
    at = pl.program_id(0)
    arrivals = (
        Arrival(hidden_at, hidden, sems.at[0]),
        Arrival(d_down_at, d_down, sems.at[1]),
    )

    @pl.when(at == 0)
    def _():
        for arrival in arrivals:
            arrival.start()

    back = product_nt(d_pre[...], w_up[...])

    @pl.when(at == 0)
    def _():
        total[...] = back

    @pl.when(at > 0)
    def _():
        total[...] += back

    @pl.when(at == pl.num_programs(0) - 1)
    def _():
        for arrival in arrivals:
            arrival.wait()
        grad = normalise_back(hidden[...], gain[...].astype(jnp.float32), total[...])
        grad = d_down[...].astype(jnp.float32) + grad
        d_hidden[...] = grad
        branch = grad.astype(jnp.bfloat16)
        d_branch[...] = branch
        shape = src.shape[0], branch.shape[1]
        picks = ones_where(src[...] == iota(shape, 1))
        theirs[...] = product_nt(branch, picks).astype(jnp.bfloat16)


def result_kernel(upper, w_down, hidden, result, total):
    at = pl.program_id(0)
    forth = product(upper[...], w_down[...])

    @pl.when(at == 0)
    def _():
        total[...] = hidden[...] + forth

    @pl.when(at > 0)
    def _():
        total[...] += forth

    @pl.when(at == pl.num_programs(0) - 1)
    def _():
        result[...] = total[...].astype(jnp.bfloat16)


def attention_back_kernel(
    block, d_branch, w_out, gates, parts_in, attended, query, own_key, own_value, memory_key,
    memory_value, totals, experts, keys,
    seg_cols, seg_rows, small,
    d_seen, d_query, d_key,
):
    w_out.start()
    branch, seen, gate, parts = d_branch[...], attended[...], gates[...], parts_in[...]
    to_seen = jnp.zeros((branch.shape[0], WIDE), jnp.float32)
    to_gate = jnp.zeros((branch.shape[0], LANES), jnp.float32)
    for at, size in pieces_of(MIX):
        d_mixed = product_nt(branch, w_out.rows(at, size))
        if at == 0:
            for operand in (query, own_key, own_value, memory_key, memory_value, totals, experts):
                operand.start()
        spread = spread_block(keys, at, size)
        weight = product(parts, expert_block(keys, at, size, 2 * GATES, True))
        to_seen += product_low(d_mixed * weight, spread)
        to_gate += product_low(
            d_mixed * product(seen, spread), expert_block(keys, at, size, 2 * GATES, False)
        )
    d_seen[...] = to_seen.astype(jnp.bfloat16)
    query, own_key, own_value = query.all(), own_key.all(), own_value.all()
    memory_key, memory_value, totals = memory_key.all(), memory_value.all(), totals.all()
    micro = query.shape[0] // block

    @pl.loop(0, micro)
    def _(at):
        before, here = masks(seg_cols, seg_rows, at, block)
        rows = pl.ds(at * block, block)
        tops = totals[rows, :]
        for head in range(HEADS):
            cols = slice(head * LANES, (head + 1) * LANES)
            q, grad = query[rows, cols], d_seen[rows, cols]
            k_before, k_here = memory_key[rows, cols], own_key[rows, cols]
            top = tops[:, head : head + 1]
            p_before = jnp.exp(scores(q, k_before, before) - top)
            p_here = jnp.exp(scores(q, k_here, here) - top)
            g_before = product_nt(grad, memory_value[rows, cols])
            g_here = product_nt(grad, own_value[rows, cols])
            delta = jnp.sum(p_before * g_before, axis=-1, keepdims=True) + jnp.sum(
                p_here * g_here, axis=-1, keepdims=True
            )
            s_before = (p_before * (g_before - delta)).astype(jnp.bfloat16)
            s_here = (p_here * (g_here - delta)).astype(jnp.bfloat16)
            to_query = product(s_before, k_before) + product(s_here, k_here)
            d_query[rows, cols] = (to_query * HEAD ** (-0.5)).astype(jnp.bfloat16)
            to_key = product_tn(s_here, q) * HEAD ** (-0.5)
            d_key[rows, cols] = to_key.astype(jnp.bfloat16)
            to_value = product_tn(p_here.astype(jnp.bfloat16), grad)
            small[rows, cols] = to_value.astype(jnp.bfloat16)

    d_value = small[:, :WIDE]
    experts = experts.all()
    for at, size in pieces_of(MIX):
        to_gate += product_low(
            product(d_value, spread_block(keys, at, size)) * experts[:, at : at + size],
            expert_block(keys, at, size, 0, False),
        )
    small[:, WIDE:QK_AT] = (to_gate * gate * (1.0 - gate)).astype(jnp.bfloat16)
    both = (WIDE, 2 * HEADS * HEAD)
    from_query = ones_where(iota(both, 0) == keys[2:3, : both[1]])
    from_key = ones_where(iota(both, 0) == keys[3:4, : both[1]])
    total = product(d_query[...], from_query) + product(d_key[...], from_key)
    small[:, QK_AT:] = total.astype(jnp.bfloat16)


QK_AT = WIDE + LANES
V_AT = 0
Q_AT = -(-MIX // LANES) * LANES
K_AT = Q_AT + HEADS * HEAD
G_AT = K_AT + HEADS * HEAD
IN_COLUMNS = G_AT + LANES


def d_experts(small, parts, keys, at, size):
    spread = product(small[:, :WIDE], spread_block(keys, at, size))
    weight = product(parts[...], expert_block(keys, at, size, 0, True))
    return (spread * weight).astype(jnp.bfloat16)


def put_into(refs, half):
    def put(number, at, total):
        total = in_order(number, total.astype(jnp.bfloat16))
        keep = total.shape[0] // 2
        columns = slice(at - number * half, at - number * half + total.shape[1])
        refs[2 * number][:, columns] = total[:keep]
        refs[2 * number + 1][:, columns] = total[keep:]

    return put


def halves_of(total, half):
    for number in range(2):
        at, stop = number * half, min(total, (number + 1) * half)
        while at < stop:
            size = min(CHUNK, stop - at)
            yield number, at, size
            at += size


def wide_kernel(
    src, keys, left_at, second_at, right_at, right_came_at, branch_at, branch_came_at, mixed_at, both_at,
    *refs,
):
    made, held = refs[:4], refs[4:14]
    left, second_came, right, right_came, branch, branch_came, mixed, parts_came = held[:8]
    turned, turned_branch = held[8:10]
    buffers, sems, out_sems = refs[14:18], refs[18], refs[19]
    tokens, width = left.shape
    left_came, seen_came = second_came.at[:, :width], second_came.at[:, width:]
    step = 2 * CHUNK
    ups, outs = right.shape[1] // 2, mixed.shape[1] // 2
    first = [
        Arrival(left_at.at[:, pl.ds(0, width)], left, sems.at[0]),
        Arrival(second_at, second_came, sems.at[1]),
    ]
    rights = []
    for number in range(2 * ups // step):
        columns = pl.ds(number * step, step)
        rights.append(
            [
                Arrival(right_at.at[:, columns], right.at[:, columns], sems.at[2 + 2 * number]),
                Arrival(right_came_at.at[:, columns], right_came.at[:, columns], sems.at[3 + 2 * number]),
            ]
        )
    at = 2 + 2 * len(rights)
    lanes = pl.ds(both_at.shape[1] - LANES, LANES)
    others = [
        Arrival(branch_at, branch, sems.at[at]),
        Arrival(branch_came_at, branch_came, sems.at[at + 1]),
        Arrival(both_at.at[:, lanes], parts_came, sems.at[at + 2]),
        Arrival(mixed_at, mixed, sems.at[at + 3]),
    ]
    for arrival in first:
        arrival.start()
    for arrival in first:
        arrival.wait()
    half = len(rights) // 2
    for arrival in sum(rights[:half], []) + others + sum(rights[half:], []):
        arrival.start()
    turn(src[...], (left, left_came), turned)
    leaving = []

    def leave(number, columns):
        for which in (2 * number, 2 * number + 1):
            copy = pltpu.make_async_copy(
                buffers[which].at[:, columns], made[which].at[:, columns], out_sems.at[len(leaving)]
            )
            copy.start()
            leaving.append(copy)

    for number in range(2):

        def put(at, total):
            total = in_order(number, total.astype(jnp.bfloat16))
            keep = total.shape[0] // 2
            columns = slice(at, at + total.shape[1])
            buffers[2 * number][:, columns] = total[:keep]
            buffers[2 * number + 1][:, columns] = total[keep:]

        for place in range(ups // step):
            for arrival in rights[number * half + place]:
                arrival.wait()
            columns = slice(number * ups + place * step, number * ups + (place + 1) * step)
            total = product(turned[:, :tokens], right[:, columns])
            put(place * step, total + product(turned[:, tokens:], right_came[:, columns]))
        leave(number, pl.ds(0, ups))
        if number == 0:
            for arrival in others:
                arrival.wait()
            turn(src[...], (branch, branch_came), turned_branch)
        at, stop = 0, min(outs, MIX - number * outs)
        while at < stop:
            size = min(CHUNK, stop - at)
            start = number * outs + at
            spread = product(seen_came[...], spread_block(keys, start, size))
            weight = product(parts_came[...], expert_block(keys, start, size, 2 * GATES, True))
            came = (spread * weight).astype(jnp.bfloat16)
            total = product(turned_branch[:, :tokens], mixed[:, start : start + size])
            put(ups + at, total + product(turned_branch[:, tokens:], came))
            at += size
        if at < outs:
            put(ups + at, jnp.zeros((turned.shape[0], outs - at), jnp.float32))
        leave(number, pl.ds(ups, outs))
    for copy in leaving:
        copy.wait()


def gradient_wide(src, left, right, branch, mixed, both_came, keys):
    tokens, rows = left[0].shape[0], src.shape[0]
    ups, outs = right[0].shape[1] // 2, mixed.shape[1] // 2
    copied = (*left, *right, *branch, mixed, both_came)
    shape = (rows // 2, ups + outs)
    held = [pltpu.VMEM(array.shape, array.dtype) for array in copied[:-1]]
    held[0] = pltpu.VMEM((tokens, branch[0].shape[1]), jnp.bfloat16)
    held.append(pltpu.VMEM((tokens, LANES), jnp.bfloat16))
    arrivals = 2 + 2 * (2 * ups // (2 * CHUNK)) + 4
    return pl.pallas_call(
        wide_kernel,
        in_specs=[pl.BlockSpec(memory_space=pltpu.VMEM)] * 2
        + [pl.BlockSpec(memory_space=pl.ANY)] * len(copied),
        out_specs=[pl.BlockSpec(memory_space=pl.ANY)] * 4,
        out_shape=[jax.ShapeDtypeStruct(shape, jnp.bfloat16)] * 4,
        scratch_shapes=held
        + [pltpu.VMEM((rows, 2 * tokens), jnp.bfloat16)] * 2
        + [pltpu.VMEM(shape, jnp.bfloat16)] * 4
        + [pltpu.SemaphoreType.DMA((arrivals,)), pltpu.SemaphoreType.DMA((8,))],
        compiler_params=pltpu.CompilerParams(vmem_limit_bytes=GRADIENT),
        cost_estimate=BRIEF,
    )(src, keys, *copied)


def inputs_kernel(
    src, left, both_came, small, small_came, parts, keys, *refs,
):
    turned = refs[-1]
    half = IN_COLUMNS // 2
    tokens, width = left.shape
    left_came = both_came.at[:, width : 2 * width]
    parts_came = both_came.at[:, 2 * width :]
    put = put_into(refs, half)

    def times(one, two):
        return product(turned[:, :tokens], one) + product(turned[:, tokens:], two)

    turn(src[...], (left, left_came), turned)
    for number, at, size in halves_of(MIX, half):
        one = d_experts(small, parts, keys, at, size)
        two = d_experts(small_came, parts_came, keys, at, size)
        put(number, at, times(one, two))
    put(1, MIX, jnp.zeros((turned.shape[0], Q_AT - MIX), jnp.float32))
    for at in range(0, 2 * HEADS * HEAD, CHUNK):
        columns = slice(QK_AT + at, QK_AT + min(at + CHUNK, 2 * HEADS * HEAD))
        put(1, Q_AT + at, times(small[:, columns], small_came[:, columns]))
    put(1, G_AT, times(small[:, WIDE:QK_AT], small_came[:, WIDE:QK_AT]))


def inputs_back_kernel(
    small, parts, keys, tokens, d_hidden, gain, w_gates, w_key, w_value,
    w_query, places, input_grad, own_in, w_both,
):
    w_value.start()
    size = HEADS * HEAD
    w_both[:size, :] = w_query[...]
    w_both[size:, :] = w_key[...]
    total = product(small[:, WIDE:QK_AT], w_gates[...])
    total += product(small[:, QK_AT:], w_both[...])
    tokens.start()
    d_hidden.start()
    for at, size in pieces_of(MIX):
        total += product(d_experts(small, parts, keys, at, size), w_value.rows(at, size))
    picks = ones_where(places[...] == iota((places.shape[0], tokens.shape[1]), 1))
    for at, weight in ((V_AT, w_value.all()), (Q_AT, w_both), (G_AT, w_gates)):
        own = product_nt(picks, weight[...]).astype(jnp.bfloat16)
        own_in[:, at : at + own.shape[1]] = own
    own_in[:, MIX:Q_AT] = jnp.zeros((places.shape[0], Q_AT - MIX), jnp.bfloat16)
    grad = normalise_back(tokens.all()[...].astype(jnp.float32), gain[...].astype(jnp.float32), total)
    input_grad[...] = (d_hidden.all()[...] + grad).astype(jnp.bfloat16)


def pieced(generate, outs, aligned, *operands):
    if not aligned:
        results = [jnp.zeros(shape, dtype) for shape, dtype in outs]
        for number, row, column, value in generate(*operands):
            value = value.astype(results[number].dtype)
            results[number] = lax.dynamic_update_slice(results[number], value, (row, column))
        return results

    def kernel(*refs):
        given, made = refs[: len(operands)], refs[len(operands) :]
        for number, row, column, value in generate(*given):
            rows, columns = slice(row, row + value.shape[0]), slice(column, column + value.shape[1])
            made[number][rows, columns] = value.astype(made[number].dtype)

    return whole(kernel, outs, *operands, grant=FULL)


def summed(pair, rows, columns=slice(None)):
    return sum(part[rows, columns].astype(jnp.float32) for part in pair)


def forked(kept, came):
    columns, rows = kept.shape[1] // 2, kept.shape[0] // 2
    for number in range(2):
        own = slice(number * columns, (number + 1) * columns)
        for half in range(2):
            part = slice(half * rows, (half + 1) * rows)
            yield 2 * number + half, 0, 0, summed((kept, came), part, own)


def paired_halves(*refs):
    for number in range(2):
        column = 0
        own = refs[number * len(refs) // 2 : (number + 1) * len(refs) // 2]
        for pair in zip(own[::2], own[1::2]):
            rows = pair[0].shape[0] // 2
            for half in range(2):
                part = slice(half * rows, (half + 1) * rows)
                yield 2 * number + half, 0, column, summed(pair, part)
            column += pair[0].shape[1]


def laid_out(layout, *refs):
    for number, start, size, column in layout:
        pair = refs[2 * number : 2 * number + 2]
        rows = pair[0].shape[0] // 2
        for half in range(2):
            part = slice(half * rows, (half + 1) * rows)
            yield half, 0, column, summed(pair, part, slice(start, start + size))


def as_row(column):
    size = column.shape[0]
    return jnp.sum(jnp.where(iota((size, size), 0) == iota((size, size), 1), column, 0.0), 0, keepdims=True)


def as_row(column):
    size = column.shape[0]
    return jnp.sum(jnp.where(iota((size, size), 0) == iota((size, size), 1), column, 0.0), 0, keepdims=True)


def last_halves(width, wide_size, *refs):
    rows = refs[0].shape[0] // 2
    for half in range(2):
        part = slice(half * rows, (half + 1) * rows)
        yield half, 0, 0, summed(refs[:2], part, slice(0, wide_size))
        if len(refs) == 2:
            blocks = (refs[0].shape[1] - wide_size) // width // 2
            for block in range(blocks):
                at = wide_size + (half * blocks + block) * width
                for low in range(2):
                    value = summed(refs, slice(low * rows, (low + 1) * rows), slice(at, at + width))
                    yield half, 0, wide_size + (2 * block + low) * width, value
            continue
        for number in range(2):
            pair = refs[2 + 2 * number : 4 + 2 * number]
            tall = pair[0].shape[0] // 2
            for block in range(tall // rows):
                at = half * tall + block * rows
                yield half, 0, wide_size + block * width + number * width // 2, summed(
                    pair, slice(at, at + rows)
                )


def most_done(weight, gain, down, down_came, wide, wide_came):
    yield 0, 0, 0, summed((down, down_came), slice(None))
    along = 0.0
    for at in range(0, HIDDEN, 2 * CHUNK):
        columns = slice(at, at + 2 * CHUNK)
        piece = summed((wide, wide_came), slice(None), columns)
        yield 1, 0, at, piece
        along += jnp.sum(piece * weight[:, columns].astype(jnp.float32), axis=1, keepdims=True)
    yield 2, 0, 0, as_row(along / gain[:, :])
    yield 3, 0, 0, summed((wide, wide_came), slice(None), slice(HIDDEN, HIDDEN + MIX))


def in_done(weight, gain, *refs):
    total = summed(refs, slice(None))
    for number, (at, size) in enumerate(((Q_AT, HEADS * HEAD), (K_AT, HEADS * HEAD), (V_AT, MIX))):
        yield number, 0, 0, total[:, at : at + size]
    gates = total[:, G_AT:].T
    yield 3, 0, 0, gates[:GATES]
    yield 4, 0, 0, gates[2 * GATES : 3 * GATES]
    along = jnp.sum(total * weight[:, :].astype(jnp.float32), axis=1, keepdims=True)
    yield 5, 0, 0, as_row(along / gain[:, :])


class Late:
    def __init__(self, source, target, sems):
        self.source, self.target, self.sems = source, target, sems
        self.shape, self.copies = target.shape, None

    def start(self):
        if len(self.shape) == 3:
            self.copies = [pltpu.make_async_copy(self.source, self.target, self.sems.at[0])]
        else:
            self.copies = [
                pltpu.make_async_copy(
                    self.source.at[pl.ds(at, size)], self.target.at[pl.ds(at, size)], self.sems.at[number]
                )
                for number, (at, size) in enumerate(pieces_of(self.shape[0]))
            ]
        for copy in self.copies:
            copy.start()

    def rows(self, at, size):
        number = at // CHUNK
        if self.copies[number] is not None:
            self.copies[number].wait()
            self.copies[number] = None
        return self.target[at : at + size]

    def all(self):
        for number, copy in enumerate(self.copies):
            if copy is not None:
                copy.wait()
                self.copies[number] = None
        return self.target


def whole(kernel, outs, *operands, scratch=(), grant=VMEM, late=()):
    outs = [jax.ShapeDtypeStruct(shape, dtype) for shape, dtype in outs]
    given, made, kept = len(operands), len(outs), len(scratch)
    buffers = [pltpu.VMEM(operands[number].shape, operands[number].dtype) for number in late]
    sems = [pltpu.SemaphoreType.DMA((len(pieces_of(operands[number].shape[-2])),)) for number in late]

    def run(*refs):
        refs = list(refs)
        extra = refs[given + made + kept :]
        for place, number in enumerate(late):
            refs[number] = Late(refs[number], extra[place], extra[len(late) + place])
        kernel(*refs[: given + made + kept])

    specs = [
        pl.BlockSpec(memory_space=pl.ANY if number in late else pltpu.VMEM) for number in range(given)
    ]
    return pl.pallas_call(
        run,
        out_shape=outs,
        in_specs=specs,
        out_specs=[pl.BlockSpec(memory_space=pltpu.VMEM)] * made,
        scratch_shapes=list(scratch) + buffers + sems,
        compiler_params=pltpu.CompilerParams(vmem_limit_bytes=grant),
        cost_estimate=BRIEF,
    )(*operands)


def body(
    tokens,
    segments,
    value_experts,
    out_experts,
    norm_gain,
    w_query,
    w_key,
    w_value,
    w_vgate,
    w_ogate,
    w_out,
    ffn_gain,
    w_up,
    w_down,
    cotangent,
):
    grid = Grid()
    first, second = grid.plane_a, grid.plane_b
    row_order = grid.order([first, second, *grid.rest])
    unit_orders = jnp.stack(
        [
            grid.order([grid.rest[0], first, second, *grid.rest[1:]]),
            grid.order([grid.rest[0], second, first, *grid.rest[1:]]),
        ]
    )
    micro, _, block, width = tokens.shape
    rows = micro * block
    hidden_units = w_up.shape[1]
    place = lax.axis_index("seq")
    own_segs = lax.dynamic_slice_in_dim(segments, place * block, block, 2)[:, 0]
    prior_start = jnp.maximum(place - 1, 0) * block
    prior_segs = jnp.where(
        place > 0, lax.dynamic_slice_in_dim(segments, prior_start, block, 2)[:, 0], -1
    )
    gain_one, gain_two = norm_gain[None], ffn_gain[None]
    column = np.arange(-(-MIX // LANES) * LANES)
    head_column = np.arange(WIDE)
    keys = np.full((4, column.size), -1, np.int32)
    keys[0, :MIX] = (column // (EXPERTS * HEAD) * LANES + column % HEAD)[:MIX]
    keys[1, :MIX] = (column // HEAD)[:MIX]
    keys[2, : HEADS * HEAD] = (head_column // HEAD * LANES + head_column % HEAD)[: HEADS * HEAD]
    keys[3, HEADS * HEAD : 2 * HEADS * HEAD] = keys[2, : HEADS * HEAD]
    keys = jnp.asarray(keys)
    lane = np.arange(4 * GATES)
    slots = np.zeros((2 * 16 + 8, LANES), np.float32)
    source = 2 * (lane % GATES // EXPERTS) + 2 * HEADS * (lane // (2 * GATES))
    slots[source, lane] = 1
    slots[16 + source + 1, lane] = 1
    slots[32] = -1
    slots[32, : 4 * GATES] = lane % EXPERTS
    slots = jnp.asarray(slots, jnp.bfloat16)
    value_picks, out_picks = (
        jnp.transpose(picks[:, 0], (0, 2, 3, 1))
        for picks in (value_experts, out_experts)
    )
    w_query, w_key, w_value = w_query.T, w_key.T, w_value.T
    share = width // grid.count

    def own_rows(array):
        return lax.dynamic_slice_in_dim(array, grid.me * share, share, 0)

    seg_cols = own_segs.reshape(rows, 1)
    seg_rows = jnp.stack([prior_segs, own_segs], 1)

    field = tokens.reshape(rows, width)
    d_down = cotangent.reshape(rows, width)
    low, full = jnp.bfloat16, jnp.float32
    normed, key = whole(
        key_kernel, [((rows, width), low), ((rows, WIDE), low)], field, gain_one, keys, w_key
    )
    memory_key = passed_along(key, "seq", 1)
    gates, parts, experts, value, w_gates = whole(
        value_kernel,
        [
            ((rows, LANES), full),
            ((rows, LANES), low),
            ((rows, MIX), low),
            ((rows, WIDE), low),
            ((LANES, width), low),
        ],
        after(normed, key), keys, slots, value_picks, out_picks, w_vgate.T, w_ogate.T, w_value,
        late=(7,),
        scratch=[pltpu.VMEM((rows, LANES), full)] * 2,
    )
    memory_value = passed_along(value, "seq", 1)
    own_memory = key, value, memory_key, memory_value

    def paired(value):
        return value, grid.swap(value, grid.core)

    step = 1024
    fixed = pl.BlockSpec((rows, width), lambda j: (0, 0))
    across = pl.BlockSpec((rows, step), lambda j: (0, j))
    up_block = pl.BlockSpec((width, step), lambda j: (0, j))
    down_block = pl.BlockSpec((step, width), lambda j: (j, 0))
    row_block = pl.BlockSpec((1, width), lambda j: (0, 0))

    anywhere = pl.BlockSpec(memory_space=pl.ANY)

    def stepped(kernel, in_specs, out_specs, outs, operands, products, scratch=0, more=()):
        return pl.pallas_call(
            kernel,
            grid=(hidden_units // step,),
            in_specs=in_specs,
            out_specs=out_specs,
            out_shape=[jax.ShapeDtypeStruct(shape, dtype) for shape, dtype in outs],
            scratch_shapes=[pltpu.VMEM((rows, width), full)] * scratch + list(more),
            compiler_params=pltpu.CompilerParams(vmem_limit_bytes=VMEM),
            cost_estimate=BRIEF,
        )(*operands)

    query, both = whole(
        query_kernel,
        [((rows, WIDE), low), ((rows, 2 * width + LANES), low)],
        after(normed, value, memory_key, seg_cols, seg_rows), keys, w_query, d_down, parts,
    )
    both_came = grid.swap(after(both, memory_value), grid.core)
    down_pair = d_down, both_came
    mixed_columns = -(-MIX // 256) * 256
    attended, totals, mixed, hidden, second_both = whole(
        functools.partial(attention_kernel, block),
        [
            ((rows, WIDE), low),
            ((rows, LANES), full),
            ((rows, mixed_columns), low),
            ((rows, width), full),
            ((rows, width + WIDE), low),
        ],
        query, *own_memory, parts, field, gain_two,
        keys, seg_cols, seg_rows, w_out, late=(11,),
    )
    second_pair = second_both, grid.swap(second_both, grid.core)
    units = hidden_units // grid.count
    side = (grid.me // grid.core) % 2
    upper, d_pre, theirs = pl.pallas_call(
        functools.partial(units_up_kernel, grid.core * units),
        grid_spec=pltpu.PrefetchScalarGridSpec(
            num_scalar_prefetch=1,
            grid=(hidden_units // step,),
            in_specs=[
                pl.BlockSpec((rows, width), lambda j, _: (0, 0)),
                pl.BlockSpec((width, step), lambda j, _: (0, j)),
                pl.BlockSpec((rows, width), lambda j, _: (0, 0)),
                pl.BlockSpec((step, width), lambda j, _: (j, 0)),
            ],
            out_specs=[
                pl.BlockSpec((rows, step), lambda j, _: (0, j)),
                pl.BlockSpec((rows, step), lambda j, _: (0, j)),
                pl.BlockSpec((rows, step // 2), lambda j, _: (0, j)),
            ],
        ),
        out_shape=[
            jax.ShapeDtypeStruct((rows, hidden_units), low),
            jax.ShapeDtypeStruct((rows, hidden_units), low),
            jax.ShapeDtypeStruct((rows, hidden_units // 2), low),
        ],
        compiler_params=pltpu.CompilerParams(vmem_limit_bytes=VMEM),
        cost_estimate=BRIEF,
    )(side.reshape(1), second_both, w_up, after(d_down, both_came), w_down)

    source = (row_order[:, None] * share + jnp.arange(share, dtype=jnp.int32)).reshape(-1, 1)
    within = unit_orders // (2 * grid.core) * grid.core + unit_orders % grid.core
    if units == 128:
        unit_blocks = jnp.stack([unit_orders, within])
        came = grid.swap(theirs, grid.core)
        upper_pair = upper, came
    else:
        place = jnp.arange(units, dtype=jnp.int32)
        half_shards = jnp.arange(grid.count // 2, dtype=jnp.int32)
        half_shards = half_shards // grid.core * (2 * grid.core) + half_shards % grid.core
        half_shards = half_shards + (1 - side) * grid.core
        theirs = upper[:, (half_shards[:, None] * units + place).reshape(-1)]
        came = grid.swap(theirs, grid.core)
        lists = [(o[:, :, None] * units + place).reshape(-1) for o in (unit_orders, within)]
        upper_pair = upper[:, lists[0]], came[:, lists[1]]
        blocks = jnp.arange(hidden_units // 128, dtype=jnp.int32).reshape(2, -1)
        unit_blocks = jnp.stack([blocks, blocks])
    pre_pair = paired(d_pre)

    def plane(parts, one, two):
        return parts[1], grid.swap(parts[0], one), parts[3], grid.swap(parts[2], two)

    aligned = share % 16 == 0

    def stage(generate, rows, widths, gate, *operands):
        outs = [((rows, size), low) for size in widths]
        return pieced(generate, outs, aligned, after(operands[0], *gate), *operands[1:])

    def down_rest(pair, masks, gate, used):
        sent = None
        for mask in masks:
            layout, column = [], 0
            for number in range(len(pair) // 2):
                layout.append((number, 0, used, column))
                column += used
            sent, own = stage(
                functools.partial(laid_out, layout), pair[0].shape[0] // 2, [column] * 2, gate, *pair
            )
            pair, used = (own, grid.swap(sent, mask)), column
            gate = (sent,)
        return pair, sent

    their_order = grid.order([first, second, *grid.rest], grid.core)
    their_source = (their_order[:, None] * share + jnp.arange(share, dtype=jnp.int32)).reshape(-1, 1)
    d_hidden, d_branch, branch_theirs = stepped(
        units_back_kernel,
        [across, up_block, anywhere, anywhere, row_block, pl.BlockSpec(source.shape, lambda j: (0, 0))],
        [fixed, fixed, pl.BlockSpec((rows, width // 2), lambda j: (0, 0))],
        [((rows, width), full), ((rows, width), low), ((rows, width // 2), low)],
        (d_pre, w_up, hidden, d_down, gain_two, their_source),
        1,
        1,
        [pltpu.VMEM((rows, width), full), pltpu.VMEM((rows, width), low), pltpu.SemaphoreType.DMA((2,))],
    )
    wide_parts = gradient_wide(
        source, second_pair, pre_pair, (d_branch, grid.swap(branch_theirs, grid.core)), mixed,
        both_came, keys,
    )
    wide_zero = plane(wide_parts, first, second)
    down_sent, down_kept = gradient_units(
        unit_blocks, (after(upper_pair[0], *wide_parts), upper_pair[1]), down_pair
    )
    down_came = grid.swap(down_sent, grid.rest[0])
    (small,) = whole(
        functools.partial(attention_back_kernel, block),
        [((rows, QK_AT + 2 * HEADS * HEAD), low)],
        after(d_branch, down_sent), w_out, gates, parts, attended, query, *own_memory, totals,
        experts, keys, seg_cols, seg_rows, late=(1, 5, 6, 7, 8, 9, 10, 11),
        scratch=[pltpu.VMEM((rows, WIDE), low)] * 3,
    )
    small_pair = paired(small)

    columns = hidden_units // 2, mixed.shape[1] // 2
    wide_two = stage(
        paired_halves, wide_parts[0].shape[0] // 2, [sum(columns)] * 4, (small,), *wide_zero
    )
    wide_one = plane(wide_two, second, first)
    half = (share * grid.count // 4, IN_COLUMNS // 2)
    in_parts = whole(
        inputs_kernel,
        [(half, low)] * 4,
        source, after(normed, *wide_two), both_came, *small_pair, parts, keys,
        scratch=[pltpu.VMEM((2 * half[0], 2 * rows), low)],
    )
    in_one = plane(in_parts, first, second)
    layout = [
        (0, 0, columns[0], 0),
        (1, 0, columns[0], columns[0]),
        (0, columns[0], columns[1], 2 * columns[0]),
        (1, columns[0], columns[1], 2 * columns[0] + columns[1]),
    ]
    wide_sent, wide_own = stage(
        functools.partial(laid_out, layout), wide_one[0].shape[0] // 2, [2 * sum(columns)] * 2,
        in_parts, *wide_one,
    )
    wide_pair = wide_own, grid.swap(wide_sent, grid.rest[0])
    down_two = stage(
        forked, down_kept.shape[0] // 2, [width // 2] * 4, (wide_sent,), down_kept, down_came
    )
    down_one = plane(down_two, first, second)
    (result,) = stepped(
        result_kernel,
        [across, down_block, fixed],
        [fixed],
        [((rows, width), low)],
        (upper, w_down, after(hidden, *down_two)),
        1,
        1,
    )
    in_two = stage(paired_halves, half[0] // 2, [half[1]] * 4, (result,), *in_one)
    in_pairs = plane(in_two, second, first)
    wide_pair, wide_sent = down_rest(wide_pair, grid.rest[1:], in_two, 2 * sum(columns))
    down_three = stage(
        paired_halves, down_one[0].shape[0] // 2, [width // 2] * 4, (wide_sent,), *down_one
    )
    down_pairs = plane(down_three, second, first)
    down_pair, down_sent = down_rest(down_pairs, grid.rest[1:], down_three, width // 2)
    in_pair, in_sent = down_rest(in_pairs, grid.rest[:1], (down_sent,), in_pairs[0].shape[1])
    places = (grid.me * share + jnp.arange(share, dtype=jnp.int32))[:, None]
    input_grad, own_in = whole(
        inputs_back_kernel,
        [((rows, width), low), ((share, IN_COLUMNS), low)],
        small, parts, keys, field, after(d_hidden, in_sent), gain_one,
        w_gates, w_key, w_value, w_query, places,
        late=(3, 4, 8),
        scratch=[pltpu.VMEM((2 * HEADS * HEAD, width), low)],
    )
    in_pair, in_sent = down_rest(in_pair, grid.rest[1:], (input_grad,), in_pair[0].shape[1])
    own_up = own_rows(w_up)
    own_gain_one = own_rows(norm_gain.astype(jnp.float32))[:, None]
    own_gain_two = own_rows(ffn_gain.astype(jnp.float32))[:, None]
    grad_down, grad_up, grad_gain_two, grad_out_w = pieced(
        most_done,
        [
            ((units, width), full),
            ((share, hidden_units), full),
            ((1, share), full),
            ((share, MIX), full),
        ],
        aligned, after(own_up, in_sent), own_gain_two, *down_pair, *wide_pair,
    )
    shapes = [(share, size) for size in (HEADS * HEAD, HEADS * HEAD, MIX)]
    shapes += [(GATES, share), (GATES, share), (1, share)]
    *grads, grad_vgate, grad_ogate, grad_gain_one = pieced(
        in_done,
        [(shape, full) for shape in shapes],
        aligned, after(own_in, grad_down), own_gain_one, *in_pair,
    )
    return (
        result.reshape(tokens.shape),
        input_grad.reshape(tokens.shape),
        grad_gain_one[0],
        *grads,
        grad_vgate.T,
        grad_ogate.T,
        grad_out_w.T,
        grad_gain_two[0],
        grad_up,
        grad_down,
    )


def solution(mesh):
    both = ("seq", "batch")
    stream = P(None, "batch", "seq", None)
    picks = P(None, "batch", "seq", None, None)
    return jax.shard_map(
        body,
        mesh=mesh,
        in_specs=(stream, P(None, "batch", None), picks, picks) + (P(),) * 10 + (stream,),
        out_specs=(
            stream,
            stream,
            P(both),
            P(both, None),
            P(both, None),
            P(both, None),
            P(both, None),
            P(both, None),
            P(None, both),
            P(both),
            P(both, None),
            P(both, None),
        ),
        check_vma=False,
    )
```
